128 devices in a mesh: side: 2 (over core), grp: 64 (over y, z, x).
Axes of the slice: x: 4, y: 4, z: 4, core: 2. Of those that a mesh axis runs over, the one named last changes fastest.
Arguments:
- query_heads: bfloat16 [1024, 8192], P('grp'), may hold values from -160 to 160
- key_cache: bfloat16 [1024, 128, 512], P('grp'), may hold values from -4 to 4
- value_cache: bfloat16 [1024, 128, 512], P('grp'), may hold values from -6 to 6
- cache_lengths: int32 [1024], P('grp'), may hold values from 2 to 128, as said below
- out_weight: bfloat16 [8192, 4096], P(None, 'grp'), may hold values from -0.0625 to 0.0625
- residual: bfloat16 [1024, 4096], P('grp'), may hold values from -4 to 4
- norm_gain: float32 [4096], replicated, may hold values from 0.5 to 1.5
- expert_ids: int32 [1024, 8], P('grp'), may hold values from 0 to 63, all different within a row; in each aligned block of 16 rows (0 to 15, 16 to 31, ...) at most 4 rows name the same one
- route_weights: float32 [1024, 8], P('grp'), may hold values from 0.05 to 0.25
- gate_up: bfloat16 [64, 4096, 1536], P('grp'), may hold values from -0.09375 to 0.09375
- down_weight: bfloat16 [64, 768, 4096], P('grp'), may hold values from -0.21875 to 0.21875
Outputs:
- layer_out: bfloat16 [1024, 4096], P('grp', 'side')
The draws below stay inside these ranges and needn't reach their ends.
Inputs may be any that keep to these rules, and one draw needn't show every extreme that they name: `cache_lengths`: at least one session has 128 live positions. `expert_ids`: each row names 8 different experts; among the 16 sessions of one index of grp (aligned blocks of rows) no expert is named by more than 4 rows, a bound that some block reaches.
All inputs are finite; a program needn't handle non-finite values.
Results may differ from the reference program's by a relative error of at most 0.0055.
Values may be sent and summed in bfloat16 or wider, within the bound.
A program may use at most 128 MiB of HBM per device.

```python
import math
import jax
import jax.numpy as jnp
import numpy as np
from jax import lax

D = 4096
HQ = 64
KVH = 4
HD = 128
HID = 768
TOPK = 8
S_DEV = 16
CTX = 128
SESSIONS = 1024
EXPERTS = 64
CAP = 4
N_GRP = 64


def draw_query_heads(key, part):
    fresh_key = jax.random.fold_in(key, 3)
    fresh = jnp.clip(jax.random.normal(fresh_key, (SESSIONS, HQ * HD), jnp.float32), -5.0, 5.0)
    return fresh.astype(jnp.bfloat16)


def draw_key_cache(key, part):
    fresh_key = jax.random.fold_in(key, 5)
    fresh = jnp.clip(jax.random.normal(fresh_key, (SESSIONS, CTX, KVH * HD), jnp.float32), -4.0, 4.0)
    return fresh.astype(jnp.bfloat16)


def draw_cache_lengths(key, part):
    spread = jax.random.randint(jax.random.fold_in(key, 1), (SESSIONS,), 0, CTX - 1)
    factor = jax.random.randint(jax.random.fold_in(key, 2), (SESSIONS // S_DEV,), 1, 5)
    per_session = jnp.repeat(factor, S_DEV)
    lengths = jnp.minimum(2 + spread * per_session // 4, CTX)
    return lengths.at[0].set(CTX).astype(jnp.int32)


def block_levels(own_key, shape, split, low, largest):
    factor_of = 1.0
    for dim, blocks in split:
        steps = jax.random.uniform(jax.random.fold_in(jax.random.fold_in(own_key, 6), dim), (blocks,), jnp.float32, low / len(split), largest / len(split))
        factor_of = factor_of * jnp.repeat(jnp.exp(steps), shape[dim] // blocks).reshape((-1,) + (1,) * (len(shape) - 1 - dim))
    return factor_of


def assign_block(own_key, own, number, rows, number_of, top, most, slope):
    order = jax.random.permutation(own_key, number_of)
    packed, usual = load_shares(number_of, rows * top, most, slope, True), load_shares(number_of, rows * top, most, slope, False)
    places = jnp.arange(number_of)

    def named(tallies, offset_by):
        used = int((tallies > 0).sum())
        fixed = max(1, used // 4)
        shifted = fixed + (places - fixed + offset_by * (used - fixed)) % max(1, number_of - fixed)
        return jnp.zeros((number_of,), jnp.int32).at[order[jnp.where(places < fixed, places, shifted)]].set(jnp.asarray(tallies, jnp.int32))

    tallies = jnp.where(number % 4 == 0, named(packed, number // 4), named(usual, number - number // 4 - 1))
    mixed = jax.random.permutation(jax.random.fold_in(own, 3), number_of)
    source_of, receiver = mixed[0:number_of // 2 * 2:2], mixed[1:number_of // 2 * 2:2]
    room = jnp.minimum(tallies[source_of] - 1, most - tallies[receiver]) // 2
    room = jnp.where((source_of == order[0]) | (receiver == order[0]) | (tallies[receiver] == 0), 0, jnp.maximum(room, 0))
    shifted = jax.random.randint(jax.random.fold_in(own, 4), (number_of // 2,), 0, 1 << 20) % (room + 1)
    tallies = tallies.at[source_of].add(-shifted).at[receiver].add(shifted)
    members = jnp.searchsorted(jnp.cumsum(tallies), jnp.arange(rows * top), side="right").astype(jnp.int32)
    listing = members.reshape(top, rows).T
    listing = listing[jax.random.permutation(jax.random.fold_in(own, 1), rows)]
    offset_by = jax.random.randint(jax.random.fold_in(own, 2), (rows, 1), 0, top)
    return jnp.take_along_axis(listing, (jnp.arange(top)[None, :] + offset_by) % top, axis=1)


def load_shares(amount, total, limit, lean, full):
    weights = [(1 << 20) // math.isqrt(rank ** lean) + 1 for rank in range(1, amount + 1)]
    largest = limit if full else min(limit, max(-(-total // amount), total * weights[0] // sum(weights)))
    least = 1 if total - largest >= amount - 1 else 0
    holding, rest = [largest] + [least] * (amount - 1), total - largest - least * (amount - 1)
    while rest > 0:
        free = [i for i in range(1, amount) if holding[i] < largest] or [i for i in range(1, amount) if holding[i] < limit]
        mass, budget = sum([weights[i] for i in free]), rest
        for i in free:
            more = min(limit - holding[i], max(1, budget * weights[i] // mass), rest)
            holding[i] = holding[i] + more
            rest = rest - more
    return np.array(holding)


def bell_draw(rng, extent, width, bound, pieces=(), held_as=jnp.bfloat16):
    gain = block_levels(rng, extent, pieces, -0.22, 0.18) if pieces else 1.0
    drawn = jax.random.normal(rng, extent, jnp.float32) * width * gain
    return jnp.minimum(jnp.maximum(drawn, -bound), bound).astype(held_as)


def setup_inputs(seed: int = 0) -> dict:
    key_of = jax.random.split(jax.random.key(seed), 12)
    query_heads = draw_query_heads(jax.random.fold_in(key_of[11], 71), 0)
    key_cache = draw_key_cache(jax.random.fold_in(key_of[11], 71), 0)
    value_cache = bell_draw(key_of[2], (SESSIONS, CTX, KVH * HD), 1.0, 6.0, ((0, 64),))
    cache_lengths = draw_cache_lengths(jax.random.fold_in(key_of[11], 71), 0)
    out_weight = bell_draw(key_of[4], (HQ * HD, D), (HQ * HD) ** -0.5, 0.0625, ((1, 64),))
    residual = bell_draw(key_of[5], (SESSIONS, D), 0.5, 4.0, ((0, 64),))
    norm_gain = jnp.clip(1.0 + 0.1 * jax.random.normal(key_of[6], (D,), jnp.float32), 0.5, 1.5)
    expert_ids_keys = jax.random.split(jax.random.fold_in(key_of[7], 1), SESSIONS // S_DEV)
    expert_ids_turns = jax.random.permutation(jax.random.fold_in(key_of[7], 3), SESSIONS // S_DEV)
    expert_ids = jax.vmap(lambda own, number: assign_block(jax.random.fold_in(key_of[7], 2), own, number, S_DEV, EXPERTS, TOPK, CAP, 2))(expert_ids_keys, expert_ids_turns).reshape((SESSIONS, TOPK))
    route_weights = jnp.clip(0.05 + 0.2 * jax.random.uniform(key_of[8], (SESSIONS, TOPK), jnp.float32) ** block_levels(key_of[8], (SESSIONS, TOPK), ((0, 64),), -0.2, 0.2), 0.05, 0.25)
    gate_up = bell_draw(key_of[9], (EXPERTS, D, 2 * HID), D ** -0.5, 0.09375, ((0, 64),))
    down_weight = bell_draw(key_of[10], (EXPERTS, HID, D), HID ** -0.5, 0.21875, ((0, 64),))
    return {"query_heads": query_heads, "key_cache": key_cache, "value_cache": value_cache, "cache_lengths": cache_lengths, "out_weight": out_weight, "residual": residual, "norm_gain": norm_gain, "expert_ids": expert_ids, "route_weights": route_weights, "gate_up": gate_up, "down_weight": down_weight}


def slots_of(expert_block):
    flat_ids = expert_block.reshape(-1).astype(jnp.int32)
    onehot = (flat_ids[:, None] == jnp.arange(EXPERTS, dtype=jnp.int32)[None, :]).astype(jnp.int32)
    running = jnp.cumsum(onehot, axis=0).astype(jnp.int32)
    return (lax.optimization_barrier(jnp.sum(onehot * running, axis=1)) - 1).astype(jnp.int32)

def attend_all(query_heads, key_cache, value_cache, cache_lengths):
    session_count = query_heads.shape[0]
    group_size = HQ // KVH
    queries = query_heads.astype(jnp.float32).reshape(session_count, KVH, group_size, HD)
    key_heads = key_cache.astype(jnp.float32).reshape(session_count, CTX, KVH, HD)
    value_heads = value_cache.astype(jnp.float32).reshape(session_count, CTX, KVH, HD)
    scores = jnp.einsum('skgd,stkd->skgt', queries, key_heads, precision=lax.Precision.HIGHEST) * HD ** (-0.5)
    visible = jnp.arange(CTX, dtype=jnp.int32)[None, :] < cache_lengths.astype(jnp.int32)[:, None]
    scores = jnp.where(visible[:, None, None, :], scores, -1e+30)
    row_max = lax.optimization_barrier(jnp.max(scores, axis=-1, keepdims=True))
    lifted = jnp.exp(scores - row_max)
    softmax_weights = (lifted / lax.optimization_barrier(jnp.sum(lifted, axis=-1, keepdims=True))).astype(jnp.bfloat16)
    attended = jnp.einsum('skgt,stkd->skgd', softmax_weights.astype(jnp.float32), value_heads, precision=lax.Precision.HIGHEST)
    return attended.astype(jnp.bfloat16).reshape(session_count, HQ * HD)

def expert_rows(token_rows, expert_gate_up, expert_down):
    both_halves = jnp.dot(token_rows, expert_gate_up, preferred_element_type=jnp.float32)
    activated = (jax.nn.silu(both_halves[:, :HID]) * both_halves[:, HID:]).astype(jnp.bfloat16)
    return jnp.dot(activated, expert_down, preferred_element_type=jnp.float32).astype(jnp.bfloat16)

def reference(query_heads, key_cache, value_cache, cache_lengths, out_weight, residual, norm_gain, expert_ids, route_weights, gate_up, down_weight):
    attn_out = attend_all(query_heads, key_cache, value_cache, cache_lengths)
    attn_proj = jnp.dot(attn_out, out_weight, preferred_element_type=jnp.float32)
    hidden = residual.astype(jnp.float32) + attn_proj
    scaling = lax.rsqrt(lax.optimization_barrier(jnp.mean(hidden * hidden, axis=-1, keepdims=True)) + 1e-06)
    normed = (hidden * scaling * norm_gain).astype(jnp.bfloat16)
    slot_index = jax.vmap(slots_of)(expert_ids.reshape(N_GRP, S_DEV, TOPK)).reshape(-1).astype(jnp.int32)
    source = jnp.repeat(jnp.arange(N_GRP, dtype=jnp.int32), S_DEV * TOPK)
    expert_flat = expert_ids.reshape(-1).astype(jnp.int32)
    row_index = (source * CAP + slot_index).astype(jnp.int32)
    session = jnp.repeat(jnp.arange(SESSIONS, dtype=jnp.int32), TOPK)
    bucket = jnp.zeros((EXPERTS, N_GRP * CAP, D), jnp.bfloat16).at[expert_flat, row_index].set(normed[session])
    outputs = lax.map(lambda operands: expert_rows(operands[0], operands[1], operands[2]), (bucket, gate_up, down_weight))
    picked = outputs[expert_flat, row_index].astype(jnp.float32).reshape(SESSIONS, TOPK, D)
    mixture = lax.optimization_barrier(jnp.sum(picked * route_weights.astype(jnp.float32)[:, :, None], axis=1))
    return (hidden + mixture).astype(jnp.bfloat16)
```

```python
import functools

import jax
import jax.numpy as jnp
from jax import lax
from jax.experimental import pallas as pl
from jax.experimental.pallas import tpu as pltpu
from jax.sharding import PartitionSpec as P

HQ = 64
KVH = 4
HD = 128
HID = 768
TOPK = 8
CTX = 128
D = 4096
S = 16
MESH = pl.DeviceIdType.MESH
BF = jnp.bfloat16
F32 = jnp.float32
NT = (((1,), (1,)), ((), ()))


def place():
    side = lax.axis_index("side")
    g = lax.axis_index("grp")
    sa = 16 - 12 * side
    sb = 4 + 12 * side
    ca = lax.rem(g // sa, 4)
    cb = lax.rem(g // sb, 4)
    cx = lax.rem(g, 4)
    return side, g, sa, sb, ca, cb, cx


def moved(g, c, stride, by):
    return g + (lax.rem(c + by + 4, 4) - c) * stride


class Ring:
    def __init__(self, side, plus, minus, sends, recvs, own, slot, half):
        self.side, self.plus, self.minus = side, plus, minus
        self.sends, self.recvs, self.own, self.slot, self.half = sends, recvs, own, slot, half

    def copy(self, src, dst, i, to):
        return pltpu.make_async_remote_copy(
            src_ref=src, dst_ref=dst, send_sem=self.sends.at[i], recv_sem=self.recvs.at[i],
            device_id=(self.side, to), device_id_type=MESH)

    def start(self):
        self.c0 = self.copy(self.own, self.slot(0, 1), 0, self.plus)
        self.c1 = self.copy(self.own, self.slot(0, 3), 1, self.minus)
        self.c0.start()
        self.c1.start()

    def forward(self):
        self.c0.wait_recv()
        self.c2 = self.copy(self.half(self.slot(1, 1), 0), self.half(self.slot(1, 2), 0), 2, self.plus)
        self.c2.start()
        self.c1.wait_recv()
        self.c3 = self.copy(self.half(self.slot(3, 3), 1), self.half(self.slot(3, 2), 1), 3, self.minus)
        self.c3.start()

    def finish(self):
        self.c2.wait_recv()
        self.c3.wait_recv()

    def drain(self):
        for c in (self.c0, self.c1, self.c2, self.c3):
            c.wait_send()


def attend(q_buf, k_buf, v_buf, lens_ref, kv, out):
    lane = lax.broadcasted_iota(jnp.int32, (S, CTX), 1)
    row = lax.broadcasted_iota(jnp.int32, (S, CTX), 0)
    live = jnp.zeros((S, CTX), jnp.int32)
    for s in range(S):
        live = jnp.where(row == s, lens_ref[s], live)
    group = HQ // KVH
    live = jnp.concatenate([live] * group, axis=0)
    lane = jnp.concatenate([lane] * group, axis=0)
    row = jnp.concatenate([row] * group, axis=0)
    queries = jnp.concatenate(
        [q_buf[:, (kv * group + j) * HD:(kv * group + j + 1) * HD] for j in range(group)], axis=0)
    scores = jnp.zeros((S * group, CTX), F32)
    for s in range(S):
        part = lax.dot_general(queries, k_buf[s, :, kv * HD:(kv + 1) * HD], NT, preferred_element_type=F32)
        scores = jnp.where(row == s, part, scores)
    scores = jnp.where(lane < live, scores * HD ** (-0.5), -1e30)
    lifted = jnp.exp(scores - jnp.max(scores, axis=1, keepdims=True))
    weights = (lifted / jnp.sum(lifted, axis=1, keepdims=True))
    spread = jnp.concatenate([jnp.where(row == s, weights, 0.0).astype(BF) for s in range(S)], axis=1)
    values = v_buf[:, :, kv * HD:(kv + 1) * HD].reshape(S * CTX, HD)
    result = jnp.dot(spread, values, preferred_element_type=F32).astype(BF)
    for j in range(group):
        out[:, j * HD:(j + 1) * HD] = result[j * S:(j + 1) * S, :]


def kernel_a(q_ref, k_ref, v_ref, lens_ref, wt_ref, res_ref, gain_ref, hid_ref, nrm_ref,
             q_buf, k_buf, v_buf, w_buf, g0, g1, o_st, r_buf,
             loc, ws, wr, s0p, r0p, s0q, r0q, s1p, r1p, s1q, r1q, os, orv):
    side, g, sa, sb, ca, cb, cx = place()
    other = 1 - side
    ap, am = moved(g, ca, sa, 1), moved(g, ca, sa, -1)
    bp, bm = moved(g, cb, sb, 1), moved(g, cb, sb, -1)
    xp, xm = moved(g, cx, 1, 1), moved(g, cx, 1, -1)
    cy, cz = g // 16, lax.rem(g // 4, 4)

    barrier = pltpu.get_barrier_semaphore()

    def hello(to_side, to):
        pl.semaphore_signal(barrier, inc=1, device_id=(to_side, to), device_id_type=MESH)

    hello(side, ap)
    hello(side, am)
    for i in range(4):
        for j in range(4):
            if i or j:
                hello(side, moved(moved(g, cb, sb, i), cx, 1, j))
            hello(other, moved(moved(g, ca, sa, i), cx, 1, j))

    c_q = pltpu.make_async_copy(q_ref.at[:, pl.ds(pl.multiple_of(side * 4096, 128), 4096)], q_buf, loc.at[0])
    c_k = pltpu.make_async_copy(k_ref.at[:, :, pl.ds(pl.multiple_of(side * 256, 128), 256)], k_buf, loc.at[1])
    c_v = pltpu.make_async_copy(v_ref.at[:, :, pl.ds(pl.multiple_of(side * 256, 128), 256)], v_buf, loc.at[2])
    w_own = wt_ref.at[:, pl.ds(pl.multiple_of(side * 4096, 128), 4096)]
    c_w = pltpu.make_async_copy(w_own, w_buf.at[ca], loc.at[3])
    c_q.start()
    c_k.start()
    c_v.start()
    c_w.start()
    pl.semaphore_wait(barrier, 33)

    def w_slot(source, at):
        return w_buf.at[lax.rem(ca - source + 4, 4)]

    ring_w = Ring(side, ap, am, ws, wr, w_own, w_slot, lambda ref, h: ref.at[h * 32:(h + 1) * 32])
    ring_w.start()
    c_q.wait()
    c_k.wait()
    c_v.wait()

    def first(route, plus, minus, sends, recvs):
        return Ring(side, plus, minus, sends, recvs, route.at[0, 0],
                    lambda source, at: route.at[0, at], lambda ref, h: ref.at[:, h * 1024:(h + 1) * 1024])

    def second(route, plus, minus, sends, recvs):
        return Ring(side, plus, minus, sends, recvs, route.at[0],
                    lambda source, at: route.at[at], lambda ref, h: ref.at[h * 2:(h + 1) * 2])

    ra, rb = first(g0, bp, bm, s0p, r0p), first(g1, xp, xm, s1p, r1p)
    rc, rd = second(g0, xp, xm, s0q, r0q), second(g1, bp, bm, s1q, r1q)
    attend(q_buf, k_buf, v_buf, lens_ref, 0, g0.at[0, 0])
    ra.start()
    attend(q_buf, k_buf, v_buf, lens_ref, 1, g1.at[0, 0])
    rb.start()
    ra.forward()
    rb.forward()
    ra.finish()
    rc.start()
    rb.finish()
    rd.start()
    ring_w.forward()
    rc.forward()
    rd.forward()
    c_w.wait()
    ring_w.finish()
    rc.finish()
    p0 = lax.dot_general(g0[...].reshape(256, 2048), w_buf[:, :, 0:2048].reshape(256, 2048), NT,
                         preferred_element_type=F32)
    rd.finish()
    p1 = lax.dot_general(g1[...].reshape(256, 2048), w_buf[:, :, 2048:4096].reshape(256, 2048), NT,
                         preferred_element_type=F32)
    mine = cb * 4 + cx
    sent = []
    for bi in range(4):
        for xi in range(4):
            n = bi * 4 + xi
            u, w = (xi * 4 + bi) * S, (bi * 4 + xi) * S
            block = (p0[u:u + S, :] + p1[w:w + S, :]).astype(BF)
            o_st[n] = block
            if n == 0:
                r_buf[side, mine] = block
    for bi in range(4):
        for xi in range(4):
            n = bi * 4 + xi
            to = moved(moved(g, cb, sb, -bi), cx, 1, -xi)
            for e in range(2):
                if n == 0 and e == 0:
                    continue
                copy = pltpu.make_async_remote_copy(
                    src_ref=o_st.at[n], dst_ref=r_buf.at[side, mine],
                    send_sem=os.at[n, e], recv_sem=orv.at[side, mine],
                    device_id=(side if e == 0 else other, to), device_id_type=MESH)
                copy.start()
                sent.append(copy)
    for i in range(4):
        for j in range(4):
            if i or j:
                n = lax.rem(cb + i, 4) * 4 + lax.rem(cx + j, 4)
                pltpu.make_async_remote_copy(
                    src_ref=o_st.at[0], dst_ref=r_buf.at[side, n], send_sem=os.at[0, 0], recv_sem=orv.at[side, n],
                    device_id=(side, bp), device_id_type=MESH).wait_recv()
            n = lax.rem(ca + i, 4) * 4 + lax.rem(cx + j, 4)
            pltpu.make_async_remote_copy(
                src_ref=o_st.at[0], dst_ref=r_buf.at[other, n], send_sem=os.at[0, 0], recv_sem=orv.at[other, n],
                device_id=(side, bp), device_id_type=MESH).wait_recv()
    squares = jnp.zeros((S, 128), F32)
    for y in range(4):
        for z in range(4):
            for m in range(2):
                pieces = []
                for x in (2 * m, 2 * m + 1):
                    pieces.append(r_buf[0, z * 4 + x, :, y * 64:(y + 1) * 64].astype(F32)
                                  + r_buf[1, y * 4 + x, :, z * 64:(z + 1) * 64].astype(F32))
                at = (y * 8 + z * 2 + m) * 128
                tile = res_ref[:, at:at + 128].astype(F32) + jnp.concatenate(pieces, axis=1)
                hid_ref[:, at:at + 128] = tile
                squares = squares + tile * tile
    scaling = lax.rsqrt(jnp.sum(squares, axis=1, keepdims=True) * (1.0 / D) + 1e-06)
    for at in range(0, D, 512):
        nrm_ref[:, at:at + 512] = (hid_ref[:, at:at + 512] * scaling * gain_ref[:, at:at + 512]).astype(BF)
    for ring in (ring_w, ra, rb, rc, rd):
        ring.drain()
    for copy in sent:
        copy.wait_send()


def attention_half(q, k, v, lens, wt, res, gain):
    vm = pl.BlockSpec(memory_space=pltpu.VMEM)
    hb = pl.BlockSpec(memory_space=pl.ANY)
    sm = pl.BlockSpec(memory_space=pltpu.SMEM)
    dma = pltpu.SemaphoreType.DMA
    return pl.pallas_call(
        kernel_a,
        out_shape=(jax.ShapeDtypeStruct((S, D), F32), jax.ShapeDtypeStruct((S, D), BF)),
        in_specs=[hb, hb, hb, sm, hb, vm, vm],
        out_specs=(vm, vm),
        scratch_shapes=[
            pltpu.VMEM((S, 4096), BF), pltpu.VMEM((S, CTX, 256), BF), pltpu.VMEM((S, CTX, 256), BF),
            pltpu.VMEM((4, 64, 4096), BF), pltpu.VMEM((4, 4, S, 2048), BF), pltpu.VMEM((4, 4, S, 2048), BF),
            pltpu.VMEM((16, S, 256), BF), pltpu.VMEM((2, 16, S, 256), BF),
            dma((4,)), dma((4,)), dma((4,)), dma((4,)), dma((4,)), dma((4,)), dma((4,)),
            dma((4,)), dma((4,)), dma((4,)), dma((4,)), dma((16, 2)), dma((2, 16)),
        ],
        compiler_params=pltpu.CompilerParams(collective_id=0, has_side_effects=True, vmem_limit_bytes=40 << 20),
        name="attention_half",
    )(q, k, v, lens, wt, res, gain)


def from_behind(value, axis, steps):
    count = lax.axis_size(axis)
    leading, last = (max(0, -steps), min(count, count - steps))
    return lax.ppermute(value, axis, [(source, source + steps) for source in range(leading, last)])


def partner(block, axis, apart):
    count = lax.axis_size(axis)
    route = []
    for low in range(count):
        high = low | 1 << apart
        if high != low and high < count:
            route += [(low, high), (high, low)]
    return lax.ppermute(block, axis, route)


def slots_of(expert_block, groups):
    flat_ids = expert_block.reshape(-1)
    onehot = (flat_ids[:, None] == jnp.arange(groups, dtype=jnp.int32)[None, :]).astype(jnp.int32)
    running = jnp.cumsum(onehot, axis=0)
    return jnp.sum(onehot * running, axis=1) - 1


def expert_rows(token_rows, expert_gate_up, expert_down):
    both_halves = jnp.dot(token_rows, expert_gate_up, preferred_element_type=jnp.float32)
    activated = (jax.nn.silu(both_halves[:, :HID]) * both_halves[:, HID:]).astype(jnp.bfloat16)
    return jnp.dot(activated, expert_down, preferred_element_type=jnp.float32).astype(jnp.bfloat16)


def body(
    query_heads,
    key_cache,
    value_cache,
    cache_lengths,
    out_weight,
    residual,
    norm_gain,
    expert_ids,
    route_weights,
    gate_up,
    down_weight,
):
    side_index = lax.axis_index("side")
    on_attention = side_index == 0
    groups = lax.axis_size("grp")
    session_count = query_heads.shape[0]
    model_width = residual.shape[1]
    capacity = max(2, 2 * session_count * TOPK // groups)
    total_slots = groups * capacity
    hidden, normed = attention_half(
        query_heads, key_cache, value_cache, cache_lengths, out_weight.T, residual, norm_gain.reshape(1, -1)
    )
    slot_index = slots_of(expert_ids, groups)
    position = expert_ids.reshape(-1) * capacity + slot_index
    placing = jnp.arange(total_slots, dtype=jnp.int32)[:, None] == position[None, :]
    dispatch = jnp.sum(
        placing.reshape(total_slots, session_count, TOPK).astype(jnp.bfloat16), axis=2
    )
    outgoing_rows = jnp.dot(dispatch, normed, preferred_element_type=jnp.float32).astype(
        jnp.bfloat16
    )
    outgoing_rows = outgoing_rows.reshape(groups, capacity, model_width)
    expert_gate_up = gate_up[0]
    expert_down = down_weight[0]

    def compute(token_slots):
        flat_rows = token_slots.reshape(-1, model_width)
        return expert_rows(flat_rows, expert_gate_up, expert_down).reshape(token_slots.shape)

    crossed = from_behind(outgoing_rows, "side", 1)
    results = lax.cond(
        on_attention,
        lambda operands: jnp.zeros_like(operands),
        compute,
        lax.all_to_all(crossed, "grp", split_axis=0, concat_axis=0, tiled=True),
    )
    returned = lax.all_to_all(results, "grp", split_axis=0, concat_axis=0, tiled=True)
    weighting = (position[:, None] == jnp.arange(total_slots, dtype=jnp.int32)[None, :]).astype(
        jnp.float32
    )
    weighting = weighting * route_weights.reshape(-1)[:, None]
    weighting = jnp.sum(weighting.reshape(session_count, TOPK, total_slots), axis=1)
    mixture = jnp.dot(
        weighting,
        returned.reshape(total_slots, model_width).astype(jnp.float32),
        precision=lax.Precision.HIGHEST,
    )
    half_width = model_width // 2
    outgoing = jnp.where(on_attention, hidden[:, half_width:], mixture[:, :half_width])
    incoming = partner(outgoing, "side", 0)
    combined = jnp.where(
        on_attention, hidden[:, :half_width] + incoming, incoming + mixture[:, half_width:]
    )
    return combined.astype(jnp.bfloat16)


def solution(mesh):
    return jax.shard_map(
        body,
        mesh=mesh,
        in_specs=(
            P("grp", None),
            P("grp", None, None),
            P("grp", None, None),
            P("grp"),
            P(None, "grp"),
            P("grp", None),
            P(),
            P("grp", None),
            P("grp", None),
            P("grp", None, None),
            P("grp", None, None),
        ),
        out_specs=P("grp", "side"),
        check_vma=False,
    )
```

```python
import jax
import jax.numpy as jnp
from jax import lax
from jax.experimental import pallas as pl
from jax.experimental.pallas import tpu as pltpu
from jax.sharding import PartitionSpec as P

HQ = 64
KVH = 4
HD = 128
HID = 768
TOPK = 8
CTX = 128
D = 4096
S = 16
MESH = pl.DeviceIdType.MESH
BF = jnp.bfloat16
F32 = jnp.float32
NT = (((1,), (1,)), ((), ()))


def place():
    side = lax.axis_index("side")
    g = lax.axis_index("grp")
    sa = 16 - 12 * side
    sb = 4 + 12 * side
    ca = lax.rem(g // sa, 4)
    cb = lax.rem(g // sb, 4)
    cx = lax.rem(g, 4)
    return side, g, sa, sb, ca, cb, cx


def moved(g, c, stride, by):
    return g + (lax.rem(c + by + 4, 4) - c) * stride


def attend(q_buf, k_buf, v_buf, lens_ref, kv, out):
    lane = lax.broadcasted_iota(jnp.int32, (S, CTX), 1)
    row = lax.broadcasted_iota(jnp.int32, (S, CTX), 0)
    live = jnp.zeros((S, CTX), jnp.int32)
    for s in range(S):
        live = jnp.where(row == s, lens_ref[s], live)
    group = HQ // KVH
    live = jnp.concatenate([live] * group, axis=0)
    lane = jnp.concatenate([lane] * group, axis=0)
    row = jnp.concatenate([row] * group, axis=0)
    queries = jnp.concatenate(
        [q_buf[:, (kv * group + j) * HD:(kv * group + j + 1) * HD] for j in range(group)], axis=0)
    scores = jnp.zeros((S * group, CTX), F32)
    for s in range(S):
        part = lax.dot_general(queries, k_buf[s, :, kv * HD:(kv + 1) * HD], NT, preferred_element_type=F32)
        scores = jnp.where(row == s, part, scores)
    scores = jnp.where(lane < live, scores * HD ** (-0.5), -1e30)
    lifted = jnp.exp(scores - jnp.max(scores, axis=1, keepdims=True))
    weights = (lifted / jnp.sum(lifted, axis=1, keepdims=True))
    spread = jnp.concatenate([jnp.where(row == s, weights, 0.0).astype(BF) for s in range(S)], axis=1)
    values = v_buf[:, :, kv * HD:(kv + 1) * HD].reshape(S * CTX, HD)
    result = jnp.dot(spread, values, preferred_element_type=F32).astype(BF)
    for j in range(group):
        out[:, j * HD:(j + 1) * HD] = result[j * S:(j + 1) * S, :]


class Links:
    def __init__(self, sends, recvs):
        self.sends, self.recvs, self.used, self.open = sends, recvs, 0, []

    def make(self, src, dst, to_side, to):
        i = self.used
        self.used += 1
        copy = pltpu.make_async_remote_copy(
            src_ref=src, dst_ref=dst, send_sem=self.sends.at[i], recv_sem=self.recvs.at[i],
            device_id=(to_side, to), device_id_type=MESH)
        self.open.append(copy)
        return copy

    def push(self, src, dst, to_side, to):
        copy = self.make(src, dst, to_side, to)
        copy.start()
        return copy

    def drain(self):
        for copy in self.open:
            copy.wait_send()


class Gather:
    def __init__(self, links, side, plus, minus, own, slot, half):
        self.links, self.side, self.plus, self.minus = links, side, plus, minus
        self.own, self.slot, self.half = own, slot, half

    def start(self):
        self.c0 = self.links.push(self.own, self.slot(0, 1), self.side, self.plus)
        self.c1 = self.links.push(self.own, self.slot(0, 3), self.side, self.minus)

    def forward(self):
        half, slot = self.half, self.slot
        self.c0.wait_recv()
        self.c2 = self.links.push(half(slot(1, 1), 0), half(slot(1, 2), 0), self.side, self.plus)
        self.c1.wait_recv()
        self.c3 = self.links.push(half(slot(3, 3), 1), half(slot(3, 2), 1), self.side, self.minus)

    def finish(self):
        self.c2.wait_recv()
        self.c3.wait_recv()


class Scatter:
    def __init__(self, links, side, plus, minus, block, stage, into, half):
        self.links, self.side, self.plus, self.minus = links, side, plus, minus
        self.block, self.stage, self.into, self.half = block, stage, into, half

    def start(self):
        stage, into, half = self.stage, self.into, self.half
        for h in range(2):
            half(stage.at[0], h)[...] = self.block(2, h).astype(BF)
        self.c0 = self.links.push(half(stage.at[0], 0), half(into.at[0], 0), self.side, self.plus)
        self.c1 = self.links.push(half(stage.at[0], 1), half(into.at[0], 1), self.side, self.minus)
        half(stage.at[1], 1)[...] = self.block(3, 1).astype(BF)
        half(stage.at[2], 0)[...] = self.block(1, 0).astype(BF)

    def forward(self):
        stage, into, half = self.stage, self.into, self.half
        self.c0.wait_recv()
        half(stage.at[1], 0)[...] = (self.block(3, 0) + half(into.at[0], 0)[...].astype(F32)).astype(BF)
        self.c2 = self.links.push(stage.at[1], into.at[1], self.side, self.plus)
        self.c1.wait_recv()
        half(stage.at[2], 1)[...] = (self.block(1, 1) + half(into.at[0], 1)[...].astype(F32)).astype(BF)
        self.c3 = self.links.push(stage.at[2], into.at[2], self.side, self.minus)

    def finish(self):
        self.c2.wait_recv()
        self.c3.wait_recv()

    def result(self, h):
        return (self.block(0, h) + self.half(self.into.at[1], h)[...].astype(F32)
                + self.half(self.into.at[2], h)[...].astype(F32))


def routing(info, order, experts):
    lane = lax.broadcasted_iota(jnp.int32, (16, 128), 1)
    tiles = []
    for t in range(2):
        tile = jnp.zeros((16, 128), F32)
        for i in range(8):
            b, x = order(t * 8 + i)
            block = info[x, b]
            moved_block = pltpu.roll(block, 16 * i, 1) if i else block
            tile = jnp.where(lane // 16 == i, moved_block, tile)
        tiles.append(tile)
    table = jnp.concatenate(tiles, axis=1)
    ids, route = table[0:8, :], table[8:16, :]
    first = lax.broadcasted_iota(jnp.int32, (256, 256), 0)
    later = lax.broadcasted_iota(jnp.int32, (256, 256), 1)
    before = jnp.where((first // 16 == later // 16) & (first < later), 1.0, 0.0).astype(BF)
    token = lax.broadcasted_iota(jnp.int32, (8, 256), 1) // 16
    named, weight = [], []
    for e in experts:
        hit = ids == e.astype(F32)
        named.append(jnp.sum(jnp.where(hit, 1.0, 0.0), axis=0, keepdims=True))
        weight.append(jnp.sum(jnp.where(hit, route, 0.0), axis=0, keepdims=True))
    named8 = jnp.concatenate(named + [jnp.zeros((4, 256), F32)], axis=0)
    rank = jnp.dot(named8.astype(BF), before, preferred_element_type=F32)
    b, x = order(token)
    spot = jnp.where(named8 > 0.5, (b * 4 + x).astype(F32) * 4.0 + rank, -1.0)
    rows = lax.broadcasted_iota(jnp.int32, (64, 256), 0).astype(F32)
    picks, weighted = [], []
    for i in range(4):
        hit = rows == spot[i:i + 1, :]
        picks.append(jnp.where(hit, 1.0, 0.0))
        weighted.append(jnp.where(hit, weight[i], 0.0))
    return jnp.concatenate(picks, axis=0).astype(BF), jnp.concatenate(weighted, axis=0)


def order0(n):
    return n % 4, n // 4


def order1(n):
    return n // 4, n % 4


def kernel(q_ref, k_ref, v_ref, lens_ref, wt_ref, res_ref, gain_ref, ids_ref, route_ref, up_ref, down_ref, out_ref,
           q_buf, k_buf, v_buf, w_buf, g0, g1, o_st, r_buf, hid, info, n0, n1, x_st, x_own, x_far, x_via,
           wg, wu, wd, a_own, a_far, y_st, z_buf, z_via, m0, m1, st0, in0, st1, in1, st2, in2, st3, in3, f0, f1,
           loc, sends, recvs, os, orv):
    side, g, sa, sb, ca, cb, cx = place()
    other = 1 - side
    ap, am = moved(g, ca, sa, 1), moved(g, ca, sa, -1)
    bp, bm = moved(g, cb, sb, 1), moved(g, cb, sb, -1)
    xp, xm = moved(g, cx, 1, 1), moved(g, cx, 1, -1)
    links = Links(sends, recvs)
    barrier = pltpu.get_barrier_semaphore()

    def hello(to_side, to):
        pl.semaphore_signal(barrier, inc=1, device_id=(to_side, to), device_id_type=MESH)

    hello(side, ap)
    hello(side, am)
    for i in range(4):
        for j in range(4):
            if i or j:
                hello(side, moved(moved(g, cb, sb, i), cx, 1, j))
            hello(other, moved(moved(g, ca, sa, i), cx, 1, j))

    def fetch(src, dst, i):
        copy = pltpu.make_async_copy(src, dst, loc.at[i])
        copy.start()
        return copy

    def at_side(base, size):
        return pl.ds(pl.multiple_of(base * size, 128), size)

    c_q = fetch(q_ref.at[:, at_side(side, 4096)], q_buf, 0)
    c_k = fetch(k_ref.at[:, :, at_side(side, 256)], k_buf, 1)
    c_v = fetch(v_ref.at[:, :, at_side(side, 256)], v_buf, 2)
    w_own = wt_ref.at[:, at_side(side, 4096)]
    c_w = fetch(w_own, w_buf.at[ca], 3)
    c_ffn = []
    for h in range(2):
        depth = at_side(side if h == 0 else other, 2048)
        c_ffn.append(fetch(up_ref.at[depth, at_side(side, 384)], wg.at[h], 4 + h))
        c_ffn.append(fetch(up_ref.at[depth, at_side(side + 2, 384)], wu.at[h], 6 + h))
        c_ffn.append(fetch(down_ref.at[at_side(side if h == 0 else other, 384), at_side(side, 2048)], wd.at[h], 8 + h))
    info[0, 0] = jnp.zeros((16, 128), F32)
    info[0, 0, 0:8, 0:16] = ids_ref[...].astype(F32)
    info[0, 0, 8:16, 0:16] = route_ref[...]
    pl.semaphore_wait(barrier, 33)

    def gather(plus, minus, own, slot, half):
        return Gather(links, side, plus, minus, own, slot, half)

    def first(buf, plus, minus, half):
        return gather(plus, minus, buf.at[0, 0], lambda source, at: buf.at[0, at], half)

    def second(buf, plus, minus):
        return gather(plus, minus, buf.at[0], lambda source, at: buf.at[at], lambda ref, h: ref.at[h * 2:(h + 1) * 2])

    def cut(size):
        return lambda ref, h: ref.at[:, h * size:(h + 1) * size]

    ring_w = gather(ap, am, w_own, lambda source, at: w_buf.at[lax.rem(ca - source + 4, 4)],
                    lambda ref, h: ref.at[h * 32:(h + 1) * 32])
    ring_w.start()
    tell = first(info, bp, bm, lambda ref, h: ref.at[h * 8:(h + 1) * 8])
    tell_on = second(info, xp, xm)
    tell.start()
    c_q.wait()
    c_k.wait()
    c_v.wait()
    ra, rb = first(g0, bp, bm, cut(1024)), first(g1, xp, xm, cut(1024))
    rc, rd = second(g0, xp, xm), second(g1, bp, bm)
    attend(q_buf, k_buf, v_buf, lens_ref, 0, g0.at[0, 0])
    ra.start()
    tell.forward()
    attend(q_buf, k_buf, v_buf, lens_ref, 1, g1.at[0, 0])
    rb.start()
    tell.finish()
    tell_on.start()
    ra.forward()
    rb.forward()
    ra.finish()
    rc.start()
    rb.finish()
    rd.start()
    tell_on.forward()
    ring_w.forward()
    rc.forward()
    rd.forward()
    tell_on.finish()
    experts = [moved(g, ca, sa, i) for i in range(4)]
    pick0, weigh0 = routing(info, order0, experts)
    pick1, weigh1 = routing(info, order1, experts)
    c_w.wait()
    ring_w.finish()
    rc.finish()
    p0 = lax.dot_general(g0[...].reshape(256, 2048), w_buf[:, :, 0:2048].reshape(256, 2048), NT,
                         preferred_element_type=F32)
    rd.finish()
    p1 = lax.dot_general(g1[...].reshape(256, 2048), w_buf[:, :, 2048:4096].reshape(256, 2048), NT,
                         preferred_element_type=F32)
    mine = cb * 4 + cx
    for n in range(16):
        bi, xi = n // 4, n % 4
        u = (xi * 4 + bi) * S
        block = (p0[u:u + S, :] + p1[n * S:(n + 1) * S, :]).astype(BF)
        o_st[n] = block
        if n == 0:
            r_buf[side, mine] = block
    sent = []
    for n in range(16):
        to = moved(moved(g, cb, sb, -(n // 4)), cx, 1, -(n % 4))
        for e in range(2):
            if n == 0 and e == 0:
                continue
            copy = pltpu.make_async_remote_copy(
                src_ref=o_st.at[n], dst_ref=r_buf.at[side, mine], send_sem=os.at[n, e], recv_sem=orv.at[side, mine],
                device_id=(side if e == 0 else other, to), device_id_type=MESH)
            copy.start()
            sent.append(copy)

    def arrived(source_side, n):
        pltpu.make_async_remote_copy(
            src_ref=o_st.at[0], dst_ref=r_buf.at[source_side, n], send_sem=os.at[0, 0], recv_sem=orv.at[source_side, n],
            device_id=(side, bp), device_id_type=MESH).wait_recv()

    for i in range(4):
        for j in range(4):
            if i or j:
                arrived(side, lax.rem(cb + i, 4) * 4 + lax.rem(cx + j, 4))
            arrived(other, lax.rem(ca + i, 4) * 4 + lax.rem(cx + j, 4))
    squares = jnp.zeros((S, 128), F32)
    for y in range(4):
        for z in range(4):
            for m in range(2):
                pieces = []
                for x in (2 * m, 2 * m + 1):
                    pieces.append(r_buf[0, z * 4 + x, :, y * 64:(y + 1) * 64].astype(F32)
                                  + r_buf[1, y * 4 + x, :, z * 64:(z + 1) * 64].astype(F32))
                at = (y * 8 + z * 2 + m) * 128
                tile = res_ref[:, at:at + 128].astype(F32) + jnp.concatenate(pieces, axis=1)
                hid[:, at:at + 128] = tile
                squares = squares + tile * tile
    scaling = lax.rsqrt(jnp.sum(squares, axis=1, keepdims=True) * (1.0 / D) + 1e-06)

    def columns(r):
        return pl.ds(pl.multiple_of(side * 2048 + r * 1024, 128), 1024)

    na, nb = first(n0, bp, bm, cut(512)), first(n1, xp, xm, cut(512))
    nc, nd = second(n0, xp, xm), second(n1, bp, bm)
    n0[0, 0] = (hid[:, columns(0)] * scaling * gain_ref[:, columns(0)]).astype(BF)
    na.start()
    n1[0, 0] = (hid[:, columns(1)] * scaling * gain_ref[:, columns(1)]).astype(BF)
    nb.start()
    na.forward()
    nb.forward()
    na.finish()
    nc.start()
    nb.finish()
    nd.start()
    nc.forward()
    nd.forward()

    def part(r):
        return slice(r * 1024, (r + 1) * 1024)

    nc.finish()
    rows = jnp.dot(pick0, n0[...].reshape(256, 1024), preferred_element_type=F32).astype(BF).reshape(4, 4, S, 1024)
    x_own[0, :, :, part(0)] = rows[0]
    x_st[:, :, :, part(0)] = rows[1:]
    via0 = links.push(x_st.at[1, :, :, part(0)], x_via.at[0], side, ap)
    to0 = [links.push(x_st.at[0, :, :, part(0)], x_own.at[1, :, :, part(0)], side, ap),
           links.push(x_st.at[2, :, :, part(0)], x_own.at[3, :, :, part(0)], side, am)]
    nd.finish()
    rows = jnp.dot(pick1, n1[...].reshape(256, 1024), preferred_element_type=F32).astype(BF).reshape(4, 4, S, 1024)
    x_own[0, :, :, part(1)] = rows[0]
    x_st[:, :, :, part(1)] = rows[1:]
    via1 = links.push(x_st.at[1, :, :, part(1)], x_via.at[1], side, am)
    to1 = [links.push(x_st.at[0, :, :, part(1)], x_own.at[1, :, :, part(1)], side, ap),
           links.push(x_st.at[2, :, :, part(1)], x_own.at[3, :, :, part(1)], side, am)]
    swaps = [links.push(x_own.at[0], x_far.at[:, 0], other, g)]
    via0.wait_recv()
    on0 = links.push(x_via.at[0], x_own.at[2, :, :, part(0)], side, ap)
    via1.wait_recv()
    on1 = links.push(x_via.at[1], x_own.at[2, :, :, part(1)], side, am)
    to0[0].wait_recv()
    to1[0].wait_recv()
    swaps.append(links.push(x_own.at[1], x_far.at[:, 1], other, g))
    to0[1].wait_recv()
    to1[1].wait_recv()
    swaps.append(links.push(x_own.at[3], x_far.at[:, 3], other, g))
    on0.wait_recv()
    on1.wait_recv()
    swaps.append(links.push(x_own.at[2], x_far.at[:, 2], other, g))
    for copy in c_ffn:
        copy.wait()
    near = x_own[...].reshape(256, 2048)
    gate = jnp.dot(near, wg[0], preferred_element_type=F32)
    up = jnp.dot(near, wu[0], preferred_element_type=F32)
    for copy in swaps:
        copy.wait_recv()
    far = x_far[...].reshape(256, 2048)
    gate = gate + jnp.dot(far, wg[1], preferred_element_type=F32)
    up = up + jnp.dot(far, wu[1], preferred_element_type=F32)
    a_own[...] = (gate / (1.0 + jnp.exp(-gate)) * up).astype(BF).reshape(4, 4, S, 384)
    swaps = [links.push(a_own.at[i], a_far.at[:, i], other, g) for i in range(4)]
    results = jnp.dot(a_own[...].reshape(256, 384), wd[0], preferred_element_type=F32)
    for copy in swaps:
        copy.wait_recv()
    results = results + jnp.dot(a_far[...].reshape(256, 384), wd[1], preferred_element_type=F32)
    results = results.astype(BF).reshape(4, 64, 2048)
    z_buf[0] = results[0]
    y_st[...] = results[1:]
    via0 = links.push(y_st.at[1, :, part(0)], z_via.at[0], side, ap)
    via1 = links.push(y_st.at[1, :, part(1)], z_via.at[1], side, am)
    back = [links.push(y_st.at[0], z_buf.at[1], side, am), links.push(y_st.at[2], z_buf.at[3], side, ap)]
    via0.wait_recv()
    on0 = links.push(z_via.at[0], z_buf.at[2, :, part(0)], side, ap)
    via1.wait_recv()
    on1 = links.push(z_via.at[1], z_buf.at[2, :, part(1)], side, am)
    for copy in back + [on0, on1]:
        copy.wait_recv()

    def mix(weigh, r):
        high = weigh.astype(BF)
        low = (weigh - high.astype(F32)).astype(BF)
        both = jnp.concatenate([high, low], axis=1)
        both = lax.dot_general(both, z_buf[:, :, part(r)].reshape(256, 1024), (((0,), (0,)), ((), ())),
                               preferred_element_type=F32)
        return (both[0:256, :] + both[256:512, :]).reshape(4, 4, S, 1024)

    m0[...] = mix(weigh0, 0)
    m1[...] = mix(weigh1, 1)

    def scatter_first(m, plus, minus, stage, into):
        return Scatter(links, side, plus, minus, lambda i, h: m[i, h * 2:(h + 1) * 2], stage, into,
                       lambda ref, h: ref.at[h * 2:(h + 1) * 2])

    def scatter_last(f, plus, minus, stage, into):
        return Scatter(links, side, plus, minus, lambda i, h: f[i, :, h * 512:(h + 1) * 512], stage, into, cut(512))

    sc, sd = scatter_first(m0, xp, xm, st0, in0), scatter_first(m1, bp, bm, st1, in1)
    sa0, sb0 = scatter_last(f0, bp, bm, st2, in2), scatter_last(f1, xp, xm, st3, in3)
    sc.start()
    sd.start()
    sc.forward()
    sd.forward()
    for last, before, f in ((sa0, sc, f0), (sb0, sd, f1)):
        before.finish()
        for h in range(2):
            f[h * 2:(h + 1) * 2] = before.result(h)
        last.start()
    sa0.forward()
    sb0.forward()
    for r, last in ((0, sa0), (1, sb0)):
        last.finish()
        for h in range(2):
            at = pl.ds(pl.multiple_of(side * 2048 + r * 1024 + h * 512, 128), 512)
            out_ref[:, r * 1024 + h * 512:r * 1024 + (h + 1) * 512] = (hid[:, at] + last.result(h)).astype(BF)
    links.drain()
    for copy in sent:
        copy.wait_send()


def body(q, k, v, lens, out_weight, residual, norm_gain, expert_ids, route_weights, gate_up, down_weight):
    vm = pl.BlockSpec(memory_space=pltpu.VMEM)
    hb = pl.BlockSpec(memory_space=pltpu.HBM)
    sm = pl.BlockSpec(memory_space=pltpu.SMEM)
    dma = pltpu.SemaphoreType.DMA

    def vb(*shape):
        return pltpu.VMEM(shape, BF)

    def vf(*shape):
        return pltpu.VMEM(shape, F32)

    return pl.pallas_call(
        kernel,
        out_shape=jax.ShapeDtypeStruct((S, D // 2), BF),
        in_specs=[hb, hb, hb, sm, hb, vm, vm, vm, vm, hb, hb],
        out_specs=vm,
        scratch_shapes=[
            vb(S, 4096), vb(S, CTX, 256), vb(S, CTX, 256), vb(4, 64, 4096), vb(4, 4, S, 2048), vb(4, 4, S, 2048),
            vb(16, S, 256), vb(2, 16, S, 256), vf(S, D), vf(4, 4, 16, 128), vb(4, 4, S, 1024), vb(4, 4, S, 1024),
            vb(3, 4, S, 2048), vb(4, 4, S, 2048), vb(4, 4, S, 2048), vb(2, 4, S, 1024),
            vb(2, 2048, 384), vb(2, 2048, 384), vb(2, 384, 2048), vb(4, 4, S, 384), vb(4, 4, S, 384),
            vb(3, 64, 2048), vb(4, 64, 2048), vb(2, 64, 1024), vf(4, 4, S, 1024), vf(4, 4, S, 1024),
            vb(3, 4, S, 1024), vb(3, 4, S, 1024), vb(3, 4, S, 1024), vb(3, 4, S, 1024),
            vb(3, S, 1024), vb(3, S, 1024), vb(3, S, 1024), vb(3, S, 1024), vf(4, S, 1024), vf(4, S, 1024),
            dma((10,)), dma((96,)), dma((96,)), dma((16, 2)), dma((2, 16)),
        ],
        compiler_params=pltpu.CompilerParams(collective_id=0, has_side_effects=True, vmem_limit_bytes=60 << 20),
        name="decode_layer",
    )(q, k, v, lens, out_weight.T, residual, norm_gain.reshape(1, -1), expert_ids.T, route_weights.T,
      gate_up[0], down_weight[0])


def solution(mesh):
    return jax.shard_map(
        body,
        mesh=mesh,
        in_specs=(
            P("grp", None), P("grp", None, None), P("grp", None, None), P("grp"), P(None, "grp"), P("grp", None), P(),
            P("grp", None), P("grp", None), P("grp", None, None), P("grp", None, None),
        ),
        out_specs=P("grp", "side"),
        check_vma=False,
    )
```

```python
import jax
import jax.numpy as jnp
from jax import lax
from jax.experimental import pallas as pl
from jax.experimental.pallas import tpu as pltpu
from jax.sharding import PartitionSpec as P

HQ = 64
KVH = 4
HD = 128
HID = 768
TOPK = 8
CTX = 128
D = 4096
S = 16
MESH = pl.DeviceIdType.MESH
BF = jnp.bfloat16
F32 = jnp.float32
NT = (((1,), (1,)), ((), ()))


def place():
    side = lax.axis_index("side")
    g = lax.axis_index("grp")
    sa = 16 - 12 * side
    sb = 4 + 12 * side
    ca = lax.rem(g // sa, 4)
    cb = lax.rem(g // sb, 4)
    cx = lax.rem(g, 4)
    return side, g, sa, sb, ca, cb, cx


def moved(g, c, stride, by):
    return g + (lax.rem(c + by + 4, 4) - c) * stride


def attend(q_buf, k_buf, v_buf, lens_ref, kv, out):
    lane = lax.broadcasted_iota(jnp.int32, (S, CTX), 1)
    row = lax.broadcasted_iota(jnp.int32, (S, CTX), 0)
    live = jnp.zeros((S, CTX), jnp.int32)
    for s in range(S):
        live = jnp.where(row == s, lens_ref[s], live)
    group = HQ // KVH
    live = jnp.concatenate([live] * group, axis=0)
    lane = jnp.concatenate([lane] * group, axis=0)
    row = jnp.concatenate([row] * group, axis=0)
    queries = jnp.concatenate(
        [q_buf[:, (kv * group + j) * HD:(kv * group + j + 1) * HD] for j in range(group)], axis=0)
    scores = jnp.zeros((S * group, CTX), F32)
    for s in range(S):
        part = lax.dot_general(queries, k_buf[s, :, kv * HD:(kv + 1) * HD], NT, preferred_element_type=F32)
        scores = jnp.where(row == s, part, scores)
    scores = jnp.where(lane < live, scores * HD ** (-0.5), -1e30)
    lifted = jnp.exp(scores - jnp.max(scores, axis=1, keepdims=True))
    weights = (lifted / jnp.sum(lifted, axis=1, keepdims=True))
    spread = jnp.concatenate([jnp.where(row == s, weights, 0.0).astype(BF) for s in range(S)], axis=1)
    values = v_buf[:, :, kv * HD:(kv + 1) * HD].reshape(S * CTX, HD)
    result = jnp.dot(spread, values, preferred_element_type=F32).astype(BF)
    for j in range(group):
        out[:, j * HD:(j + 1) * HD] = result[j * S:(j + 1) * S, :]


class Links:
    def __init__(self, sends, recvs):
        self.sends, self.recvs, self.used, self.open = sends, recvs, 0, []

    def make(self, src, dst, to_side, to):
        i = self.used
        self.used += 1
        copy = pltpu.make_async_remote_copy(
            src_ref=src, dst_ref=dst, send_sem=self.sends.at[i], recv_sem=self.recvs.at[i],
            device_id=(to_side, to), device_id_type=MESH)
        self.open.append(copy)
        return copy

    def push(self, src, dst, to_side, to):
        copy = self.make(src, dst, to_side, to)
        copy.start()
        return copy

    def drain(self):
        for copy in self.open:
            copy.wait_send()


class Columns:
    def __init__(self, links, side, plus, minus, own, slot):
        self.links, self.side, self.plus, self.minus, self.own, self.slot = links, side, plus, minus, own, slot

    def start(self):
        low, high = slice(0, 32), slice(32, 64)
        push, own, slot = self.links.push, self.own, self.slot(0)
        self.c0 = push(own.at[low], slot.at[low], self.side, self.plus)
        self.c1 = push(own.at[high], slot.at[high], self.side, self.minus)
        self.rest = [push(own.at[high], slot.at[high], self.side, self.plus),
                     push(own.at[low], slot.at[low], self.side, self.minus)]

    def forward(self):
        self.c0.wait_recv()
        at = self.slot(1).at[0:32]
        self.rest.append(self.links.push(at, at, self.side, self.plus))
        self.c1.wait_recv()
        at = self.slot(3).at[32:64]
        self.rest.append(self.links.push(at, at, self.side, self.minus))

    def finish(self):
        for copy in self.rest:
            copy.wait_recv()


class Gather:
    def __init__(self, links, side, p, q, buf, half=None):
        self.links, self.side, self.p, self.q, self.buf, self.half = links, side, p, q, buf, half
        self.got = {}

    def send(self, i, j, to, di, dj, view=None):
        src, dst = self.buf.at[i, j], self.buf.at[(i + di) % 4, (j + dj) % 4]
        if view is not None:
            src, dst = self.half(src, view), self.half(dst, view)
        self.got[(i + di) % 4, (j + dj) % 4, view] = self.links.push(src, dst, self.side, to)

    def wait(self, i, j, view=None):
        self.got.pop((i, j, view)).wait_recv()

    def along_q(self, j):
        self.send(0, j, self.q[0], 1, 0)
        self.send(0, j, self.q[1], 3, 0)

    def start(self):
        self.send(0, 0, self.p[0], 0, 1)
        self.send(0, 0, self.p[1], 0, 3)
        if self.half is None:
            self.send(0, 0, self.p[2], 0, 2)
        self.along_q(0)

    def step1(self):
        self.wait(0, 1)
        if self.half is not None:
            self.send(0, 1, self.p[0], 0, 1, 0)
        self.along_q(1)
        self.wait(0, 3)
        if self.half is not None:
            self.send(0, 3, self.p[1], 0, 3, 1)
        self.along_q(3)
        self.wait(1, 0)
        self.send(1, 0, self.q[0], 1, 0)

    def step2(self):
        if self.half is None:
            self.wait(0, 2)
        else:
            self.wait(0, 2, 0)
            self.wait(0, 2, 1)
        self.along_q(2)
        self.wait(1, 1)
        self.send(1, 1, self.q[0], 1, 0)
        self.wait(3, 3)
        self.send(3, 3, self.q[1], 3, 0)

    def step3(self):
        self.wait(3, 2)
        self.send(3, 2, self.q[1], 3, 0)

    def finish(self):
        for key in list(self.got):
            self.wait(*key)


class Scatter:
    def __init__(self, links, side, p, q, m, far, over, near, last):
        self.links, self.side, self.p, self.q, self.m = links, side, p, q, m
        self.far, self.over, self.near, self.last = far, over, near, last

    def start(self):
        links, m, far, over = self.links, self.m, self.far, self.over
        self.c_far, self.c_over = {}, {}
        for j in (0, 3, 1, 2):
            far[0, j] = m[2, j].astype(BF)
            to = self.q[0] if j < 2 else self.q[1]
            self.c_far[j] = links.push(far.at[0, j], far.at[1, j], self.side, to)
        for j in (2, 1, 3, 0):
            way = 0 if j >= 2 else 1
            over[0, way, j] = m[3 if way == 0 else 1, j].astype(BF)
            self.c_over[way, j] = links.push(over.at[0, way, j], over.at[1, way, j], self.side, self.q[way])

    def forward(self):
        links, m, far, over = self.links, self.m, self.far, self.over
        for j in (0, 3, 1, 2):
            way = 0 if j < 2 else 1
            self.c_far[j].wait_recv()
            over[0, way, j] = (m[3 if way == 0 else 1, j] + far[1, j].astype(F32)).astype(BF)
            self.c_over[way, j] = links.push(over.at[0, way, j], over.at[1, way, j], self.side, self.q[way])

    def turn(self, js):
        links, near, over = self.links, self.near, self.over
        for j in js:
            self.c_over[0, j].wait_recv()
            self.c_over[1, j].wait_recv()
            block = self.m[0, j] + over[1, 0, j].astype(F32) + over[1, 1, j].astype(F32)
            if j == 0:
                self.own = block
            else:
                near[0, j] = block.astype(BF)
                self.last[j] = links.push(near.at[0, j], near.at[1, j], self.side, self.p[(None, 1, 2, 0)[j]])

    def result(self):
        block = self.own
        for j in (1, 3, 2):
            self.last[j].wait_recv()
            block = block + self.near[1, j].astype(F32)
        return block


def routing(info, order, experts):
    lane = lax.broadcasted_iota(jnp.int32, (16, 128), 1)
    tiles = []
    for t in range(2):
        tile = jnp.zeros((16, 128), F32)
        for i in range(8):
            b, x = order(t * 8 + i)
            block = info[x, b]
            moved_block = pltpu.roll(block, 16 * i, 1) if i else block
            tile = jnp.where(lane // 16 == i, moved_block, tile)
        tiles.append(tile)
    table = jnp.concatenate(tiles, axis=1)
    ids, route = table[0:8, :], table[8:16, :]
    first = lax.broadcasted_iota(jnp.int32, (256, 256), 0)
    later = lax.broadcasted_iota(jnp.int32, (256, 256), 1)
    before = jnp.where((first // 16 == later // 16) & (first < later), 1.0, 0.0).astype(BF)
    token = lax.broadcasted_iota(jnp.int32, (8, 256), 1) // 16
    named, weight = [], []
    for e in experts:
        hit = ids == e.astype(F32)
        named.append(jnp.sum(jnp.where(hit, 1.0, 0.0), axis=0, keepdims=True))
        weight.append(jnp.sum(jnp.where(hit, route, 0.0), axis=0, keepdims=True))
    named8 = jnp.concatenate(named + [jnp.zeros((4, 256), F32)], axis=0)
    rank = jnp.dot(named8.astype(BF), before, preferred_element_type=F32)
    b, x = order(token)
    spot = jnp.where(named8 > 0.5, (b * 4 + x).astype(F32) * 4.0 + rank, -1.0)
    rows = lax.broadcasted_iota(jnp.int32, (64, 256), 0).astype(F32)
    picks, weighted = [], []
    for i in range(4):
        hit = rows == spot[i:i + 1, :]
        picks.append(jnp.where(hit, 1.0, 0.0))
        weighted.append(jnp.where(hit, weight[i], 0.0))
    return jnp.concatenate(picks, axis=0).astype(BF), jnp.concatenate(weighted, axis=0)


def order0(n):
    return n % 4, n // 4


def order1(n):
    return n // 4, n % 4


def kernel(q_ref, k_ref, v_ref, lens_ref, wt_ref, res_ref, gain_ref, ids_ref, route_ref, up_ref, down_ref, out_ref,
           q_buf, k_buf, v_buf, w_buf, g0, g1, o_st, r_buf, hid, info, n0, n1, x_st, x_own, x_far, x_via,
           w_gu, wd, h_own, h_far, a_own, a_far, y_st, z_buf, z_via, m0, m1,
           far0, over0, near0, far1, over1, near1, loc, sends, recvs, os, orv):
    side, g, sa, sb, ca, cb, cx = place()
    other = 1 - side
    ap, am = moved(g, ca, sa, 1), moved(g, ca, sa, -1)
    b_way = [moved(g, cb, sb, i) for i in (1, -1, 2)]
    x_way = [moved(g, cx, 1, i) for i in (1, -1, 2)]
    links = Links(sends, recvs)
    barrier = pltpu.get_barrier_semaphore()

    def hello(to_side, to):
        pl.semaphore_signal(barrier, inc=1, device_id=(to_side, to), device_id_type=MESH)

    hello(side, ap)
    hello(side, am)
    for i in range(4):
        for j in range(4):
            if i or j:
                hello(side, moved(moved(g, cb, sb, i), cx, 1, j))
            hello(other, moved(moved(g, ca, sa, i), cx, 1, j))

    def fetch(src, dst, i):
        copy = pltpu.make_async_copy(src, dst, loc.at[i])
        copy.start()
        return copy

    def at_side(base, size):
        return pl.ds(pl.multiple_of(base * size, 128), size)

    c_q = fetch(q_ref.at[:, at_side(side, 4096)], q_buf, 0)
    c_k = fetch(k_ref.at[:, :, at_side(side, 256)], k_buf, 1)
    c_v = fetch(v_ref.at[:, :, at_side(side, 256)], v_buf, 2)
    w_own = wt_ref.at[:, at_side(side, 4096)]
    c_w = fetch(w_own, w_buf.at[ca], 3)
    info[0, 0] = jnp.zeros((16, 128), F32)
    info[0, 0, 0:8, 0:16] = ids_ref[...].astype(F32)
    info[0, 0, 8:16, 0:16] = route_ref[...]
    c_q.wait()
    c_k.wait()
    c_v.wait()
    attend(q_buf, k_buf, v_buf, lens_ref, 0, g0.at[0, 0])
    attend(q_buf, k_buf, v_buf, lens_ref, 1, g1.at[0, 0])
    pl.semaphore_wait(barrier, 33)
    ring_w = Columns(links, side, ap, am, w_own, lambda source: w_buf.at[lax.rem(ca - source + 4, 4)])
    tell = Gather(links, side, b_way, x_way, info)
    cut = lambda ref, h: ref.at[:, h * 1024:(h + 1) * 1024]
    ra = Gather(links, side, b_way, x_way, g0, cut)
    rb = Gather(links, side, x_way, b_way, g1, cut)
    ra.start()
    rb.start()
    tell.start()
    ring_w.start()
    c_ffn = []
    for h in range(2):
        depth = at_side(side if h == 0 else other, 2048)
        c_ffn.append(fetch(up_ref.at[depth, at_side(side, 384)], w_gu.at[h, :, 0:384], 4 + h))
        c_ffn.append(fetch(up_ref.at[depth, at_side(side + 2, 384)], w_gu.at[h, :, 384:768], 6 + h))
        c_ffn.append(fetch(down_ref.at[at_side(side if h == 0 else other, 384), at_side(side, 2048)], wd.at[h], 8 + h))
    ra.step1()
    rb.step1()
    tell.step1()
    ra.step2()
    rb.step2()
    tell.step2()
    ring_w.forward()
    ra.step3()
    rb.step3()
    tell.step3()
    tell.finish()
    experts = [moved(g, ca, sa, i) for i in range(4)]
    pick0, weigh0 = routing(info, order0, experts)
    pick1, weigh1 = routing(info, order1, experts)
    ra.finish()
    rb.finish()
    c_w.wait()
    ring_w.finish()
    p0 = lax.dot_general(g0[...].reshape(256, 2048), w_buf[:, :, 0:2048].reshape(256, 2048), NT,
                         preferred_element_type=F32)
    p1 = lax.dot_general(g1[...].reshape(256, 2048), w_buf[:, :, 2048:4096].reshape(256, 2048), NT,
                         preferred_element_type=F32)
    mine = cb * 4 + cx
    sent = []
    for n in sorted(range(16), key=lambda n: -((0, 1, 2, 1)[n // 4] + (0, 1, 2, 1)[n % 4])):
        bi, xi = n // 4, n % 4
        u = (xi * 4 + bi) * S
        block = (p0[u:u + S, :] + p1[n * S:(n + 1) * S, :]).astype(BF)
        o_st[n] = block
        if n == 0:
            r_buf[side, mine] = block
        to = moved(moved(g, cb, sb, -bi), cx, 1, -xi)
        for e in range(2):
            if n == 0 and e == 0:
                continue
            copy = pltpu.make_async_remote_copy(
                src_ref=o_st.at[n], dst_ref=r_buf.at[side, mine], send_sem=os.at[n, e], recv_sem=orv.at[side, mine],
                device_id=(side if e == 0 else other, to), device_id_type=MESH)
            copy.start()
            sent.append(copy)

    def arrived(source_side, n):
        pltpu.make_async_remote_copy(
            src_ref=o_st.at[0], dst_ref=r_buf.at[source_side, n], send_sem=os.at[0, 0], recv_sem=orv.at[source_side, n],
            device_id=(side, ap), device_id_type=MESH).wait_recv()

    for i in range(4):
        for j in range(4):
            if i or j:
                arrived(side, lax.rem(cb + i, 4) * 4 + lax.rem(cx + j, 4))
            arrived(other, lax.rem(ca + i, 4) * 4 + lax.rem(cx + j, 4))
    squares = jnp.zeros((S, 128), F32)
    for y in range(4):
        for z in range(4):
            for m in range(2):
                pieces = []
                for x in (2 * m, 2 * m + 1):
                    pieces.append(r_buf[0, z * 4 + x, :, y * 64:(y + 1) * 64].astype(F32)
                                  + r_buf[1, y * 4 + x, :, z * 64:(z + 1) * 64].astype(F32))
                at = (y * 8 + z * 2 + m) * 128
                tile = res_ref[:, at:at + 128].astype(F32) + jnp.concatenate(pieces, axis=1)
                hid[:, at:at + 128] = tile
                squares = squares + tile * tile
    scaling = lax.rsqrt(jnp.sum(squares, axis=1, keepdims=True) * (1.0 / D) + 1e-06)

    def columns(r):
        return pl.ds(pl.multiple_of(side * 2048 + r * 1024, 128), 1024)

    na = Gather(links, side, b_way, x_way, n0)
    nb = Gather(links, side, x_way, b_way, n1)
    n0[0, 0] = (hid[:, columns(0)] * scaling * gain_ref[:, columns(0)]).astype(BF)
    na.start()
    n1[0, 0] = (hid[:, columns(1)] * scaling * gain_ref[:, columns(1)]).astype(BF)
    nb.start()
    na.step1()
    nb.step1()
    na.step2()
    nb.step2()
    na.step3()
    nb.step3()

    def part(r):
        return slice(r * 1024, (r + 1) * 1024)

    def via_out(r, c):
        at = slice(2 * c, 2 * c + 2)
        return links.push(x_st.at[1, at, :, part(r)], x_via.at[r, at], side, (ap, am)[r])

    def via_on(r, c):
        at = slice(2 * c, 2 * c + 2)
        return links.push(x_via.at[r, at], x_own.at[2, at, :, part(r)], side, (ap, am)[r])

    vias, direct = [], {1: [], 3: []}
    for r, ring, n_buf, pick in ((0, na, n0, pick0), (1, nb, n1, pick1)):
        ring.finish()
        rows = jnp.dot(pick, n_buf[...].reshape(256, 1024), preferred_element_type=F32).astype(BF)
        rows = rows.reshape(4, 4, S, 1024)
        x_st[:, :, :, part(r)] = rows[1:]
        x_own[0, :, :, part(r)] = rows[0]
        vias += [(r, c, via_out(r, c)) for c in range(2)]
        direct[1].append(links.push(x_st.at[0, :, :, part(r)], x_own.at[1, :, :, part(r)], side, ap))
        direct[3].append(links.push(x_st.at[2, :, :, part(r)], x_own.at[3, :, :, part(r)], side, am))

    def swap(i):
        return links.push(x_own.at[i], x_far.at[i], other, g)

    def front(src, dst, h, i):
        rows = src[i].reshape(64, 2048)
        dst[i] = jnp.dot(rows, w_gu[h], preferred_element_type=F32).reshape(4, S, 768)

    swaps = {0: swap(0)}
    for copy in c_ffn:
        copy.wait()
    front(x_own, h_own, 0, 0)
    ons = []
    for r, c, copy in vias:
        copy.wait_recv()
        ons.append(via_on(r, c))
    for i in (1, 3):
        for copy in direct[i]:
            copy.wait_recv()
        swaps[i] = swap(i)
    front(x_own, h_own, 0, 1)
    front(x_own, h_own, 0, 3)
    for i in (0, 1, 3):
        swaps[i].wait_recv()
        front(x_far, h_far, 1, i)
    for copy in ons:
        copy.wait_recv()
    swaps[2] = swap(2)
    front(x_own, h_own, 0, 2)
    swaps[2].wait_recv()
    front(x_far, h_far, 1, 2)
    swaps = []
    for i in range(4):
        both = h_own[i] + h_far[:, i]
        gate, up = both[:, :, 0:384], both[:, :, 384:768]
        a_own[i] = (gate / (1.0 + jnp.exp(-gate)) * up).astype(BF)
        swaps.append(links.push(a_own.at[i], a_far.at[:, i], other, g))
    near2 = jnp.dot(a_own[2].reshape(64, 384), wd[0], preferred_element_type=F32)
    for copy in swaps:
        copy.wait_recv()
    y_st[1] = (near2 + jnp.dot(a_far[2].reshape(64, 384), wd[1], preferred_element_type=F32)).astype(BF)
    vias = []
    for r in range(2):
        for c in range(2):
            at = slice(32 * c, 32 * c + 32)
            vias.append((r, at, links.push(y_st.at[1, at, part(r)], z_via.at[r, at], side, (ap, am)[r])))
    back = []
    for i in (1, 3, 0):
        rows = (jnp.dot(a_own[i].reshape(64, 384), wd[0], preferred_element_type=F32)
                + jnp.dot(a_far[i].reshape(64, 384), wd[1], preferred_element_type=F32)).astype(BF)
        if i == 0:
            z_buf[0] = rows
        else:
            y_st[i - 1] = rows
            back.append(links.push(y_st.at[i - 1], z_buf.at[i], side, am if i == 1 else ap))
    for r, at, copy in vias:
        copy.wait_recv()
        back.append(links.push(z_via.at[r, at], z_buf.at[2, at, part(r)], side, (ap, am)[r]))
    for copy in back:
        copy.wait_recv()

    def mix(weigh, r):
        high = weigh.astype(BF)
        low = (weigh - high.astype(F32)).astype(BF)
        both = jnp.concatenate([high, low], axis=1)
        both = lax.dot_general(both, z_buf[:, :, part(r)].reshape(256, 1024), (((0,), (0,)), ((), ())),
                               preferred_element_type=F32)
        return (both[0:256, :] + both[256:512, :]).reshape(4, 4, S, 1024)

    sc = Scatter(links, side, b_way, x_way, m0, far0, over0, near0, {})
    sd = Scatter(links, side, x_way, b_way, m1, far1, over1, near1, {})
    m0[...] = mix(weigh0, 0)
    sc.start()
    m1[...] = mix(weigh1, 1)
    sd.start()
    sc.forward()
    sd.forward()
    sc.turn((2, 1, 3, 0))
    sd.turn((2, 1, 3, 0))
    for r, ring in ((0, sc), (1, sd)):
        out_ref[:, part(r)] = hid[:, columns(r)] + ring.result()
    links.drain()
    for copy in sent:
        copy.wait_send()


def body(q, k, v, lens, out_weight, residual, norm_gain, expert_ids, route_weights, gate_up, down_weight):
    vm = pl.BlockSpec(memory_space=pltpu.VMEM)
    hb = pl.BlockSpec(memory_space=pltpu.HBM)
    sm = pl.BlockSpec(memory_space=pltpu.SMEM)
    dma = pltpu.SemaphoreType.DMA

    def vb(*shape):
        return pltpu.VMEM(shape, BF)

    def vf(*shape):
        return pltpu.VMEM(shape, F32)

    return pl.pallas_call(
        kernel,
        out_shape=jax.ShapeDtypeStruct((S, D // 2), F32),
        in_specs=[hb, hb, hb, sm, hb, vm, vm, vm, vm, hb, hb],
        out_specs=vm,
        scratch_shapes=[
            vb(S, 4096), vb(S, CTX, 256), vb(S, CTX, 256), vb(4, 64, 4096), vb(4, 4, S, 2048), vb(4, 4, S, 2048),
            vb(16, S, 256), vb(2, 16, S, 256), vf(S, D), vf(4, 4, 16, 128), vb(4, 4, S, 1024), vb(4, 4, S, 1024),
            vb(3, 4, S, 2048), vb(4, 4, S, 2048), vb(4, 4, S, 2048), vb(2, 4, S, 1024),
            vb(2, 2048, 768), vb(2, 384, 2048), vf(4, 4, S, 768), vf(4, 4, S, 768), vb(4, 4, S, 384), vb(4, 4, S, 384),
            vb(3, 64, 2048), vb(4, 64, 2048), vb(2, 64, 1024), vf(4, 4, S, 1024), vf(4, 4, S, 1024),
            vb(2, 4, S, 1024), vb(2, 2, 4, S, 1024), vb(2, 4, S, 1024),
            vb(2, 4, S, 1024), vb(2, 2, 4, S, 1024), vb(2, 4, S, 1024),
            dma((10,)), dma((160,)), dma((160,)), dma((16, 2)), dma((2, 16)),
        ],
        compiler_params=pltpu.CompilerParams(collective_id=0, has_side_effects=True, vmem_limit_bytes=60 << 20),
        name="decode_layer",
    )(q, k, v, lens, out_weight.T, residual, norm_gain.reshape(1, -1), expert_ids.T, route_weights.T,
      gate_up[0], down_weight[0]).astype(BF)


def solution(mesh):
    return jax.shard_map(
        body,
        mesh=mesh,
        in_specs=(
            P("grp", None), P("grp", None, None), P("grp", None, None), P("grp"), P(None, "grp"), P("grp", None), P(),
            P("grp", None), P("grp", None), P("grp", None, None), P("grp", None, None),
        ),
        out_specs=P("grp", "side"),
        check_vma=False,
    )
```

```python
import jax
import jax.numpy as jnp
from jax import lax
from jax.experimental import pallas as pl
from jax.experimental.pallas import tpu as pltpu
from jax.sharding import PartitionSpec as P

HQ = 64
KVH = 4
HD = 128
HID = 768
TOPK = 8
CTX = 128
D = 4096
S = 16
MESH = pl.DeviceIdType.MESH
BF = jnp.bfloat16
F32 = jnp.float32
NT = (((1,), (1,)), ((), ()))


def place():
    side = lax.axis_index("side")
    g = lax.axis_index("grp")
    sa = 16 - 12 * side
    sb = 4 + 12 * side
    ca = lax.rem(g // sa, 4)
    cb = lax.rem(g // sb, 4)
    cx = lax.rem(g, 4)
    return side, g, sa, sb, ca, cb, cx


def moved(g, c, stride, by):
    return g + (lax.rem(c + by + 4, 4) - c) * stride


def attend(q_buf, k_buf, v_buf, lens_ref, kv):
    lane = lax.broadcasted_iota(jnp.int32, (S, CTX), 1)
    row = lax.broadcasted_iota(jnp.int32, (S, CTX), 0)
    live = jnp.zeros((S, CTX), jnp.int32)
    for s in range(S):
        live = jnp.where(row == s, lens_ref[s], live)
    group = HQ // KVH
    live = jnp.concatenate([live] * group, axis=0)
    lane = jnp.concatenate([lane] * group, axis=0)
    row = jnp.concatenate([row] * group, axis=0)
    queries = jnp.concatenate(
        [q_buf[:, (kv * group + j) * HD:(kv * group + j + 1) * HD] for j in range(group)], axis=0)
    scores = jnp.zeros((S * group, CTX), F32)
    for s in range(S):
        part = lax.dot_general(queries, k_buf[s, :, kv * HD:(kv + 1) * HD], NT, preferred_element_type=F32)
        scores = jnp.where(row == s, part, scores)
    scores = jnp.where(lane < live, scores * HD ** (-0.5), -1e30)
    lifted = jnp.exp(scores - jnp.max(scores, axis=1, keepdims=True))
    weights = (lifted / jnp.sum(lifted, axis=1, keepdims=True))
    spread = jnp.concatenate([jnp.where(row == s, weights, 0.0).astype(BF) for s in range(S)], axis=1)
    values = v_buf[:, :, kv * HD:(kv + 1) * HD].reshape(S * CTX, HD)
    return jnp.dot(spread, values, preferred_element_type=F32).astype(BF)


class Links:
    def __init__(self, sends, recvs):
        self.sends, self.recvs, self.used, self.open = sends, recvs, 0, []

    def make(self, src, dst, to_side, to):
        i = self.used
        self.used += 1
        copy = pltpu.make_async_remote_copy(
            src_ref=src, dst_ref=dst, send_sem=self.sends.at[i], recv_sem=self.recvs.at[i],
            device_id=(to_side, to), device_id_type=MESH)
        self.open.append(copy)
        return copy

    def push(self, src, dst, to_side, to):
        copy = self.make(src, dst, to_side, to)
        copy.start()
        return copy

    def drain(self):
        for copy in self.open:
            copy.wait_send()


class Columns:
    def __init__(self, links, side, plus, minus, own, slot):
        self.links, self.side, self.plus, self.minus, self.own, self.slot = links, side, plus, minus, own, slot

    def start(self):
        low, high = slice(0, 32), slice(32, 64)
        push, own, slot = self.links.push, self.own, self.slot(0)
        self.c0 = push(own.at[low], slot.at[low], self.side, self.plus)
        self.c1 = push(own.at[high], slot.at[high], self.side, self.minus)
        self.rest = [push(own.at[high], slot.at[high], self.side, self.plus),
                     push(own.at[low], slot.at[low], self.side, self.minus)]

    def forward(self):
        self.c0.wait_recv()
        at = self.slot(1).at[0:32]
        self.rest.append(self.links.push(at, at, self.side, self.plus))
        self.c1.wait_recv()
        at = self.slot(3).at[32:64]
        self.rest.append(self.links.push(at, at, self.side, self.minus))

    def finish(self):
        for copy in self.rest:
            copy.wait_recv()


class Gather:
    def __init__(self, links, side, p, q, buf, half=None):
        self.links, self.side, self.p, self.q, self.buf, self.half = links, side, p, q, buf, half
        self.got = {}

    def send(self, i, j, to, di, dj, view=None):
        src, dst = self.buf.at[i, j], self.buf.at[(i + di) % 4, (j + dj) % 4]
        if view is not None:
            src, dst = self.half(src, view), self.half(dst, view)
        self.got[(i + di) % 4, (j + dj) % 4, view] = self.links.push(src, dst, self.side, to)

    def wait(self, i, j, view=None):
        self.got.pop((i, j, view)).wait_recv()

    def along_q(self, j):
        self.send(0, j, self.q[0], 1, 0)
        self.send(0, j, self.q[1], 3, 0)

    def start(self):
        self.send(0, 0, self.p[0], 0, 1)
        self.send(0, 0, self.p[1], 0, 3)
        if self.half is None:
            self.send(0, 0, self.p[2], 0, 2)
        self.along_q(0)

    def step1(self):
        self.wait(0, 1)
        if self.half is not None:
            self.send(0, 1, self.p[0], 0, 1, 0)
        self.along_q(1)
        self.wait(0, 3)
        if self.half is not None:
            self.send(0, 3, self.p[1], 0, 3, 1)
        self.along_q(3)
        self.wait(1, 0)
        self.send(1, 0, self.q[0], 1, 0)

    def step2(self):
        if self.half is None:
            self.wait(0, 2)
        else:
            self.wait(0, 2, 0)
            self.wait(0, 2, 1)
        self.along_q(2)

    def step3(self):
        self.wait(1, 1)
        self.send(1, 1, self.q[0], 1, 0)
        self.wait(3, 3)
        self.send(3, 3, self.q[1], 3, 0)
        self.wait(3, 2)
        self.send(3, 2, self.q[1], 3, 0)

    def finish(self):
        for key in list(self.got):
            self.wait(*key)


class Scatter:
    def __init__(self, links, side, p, q, m, far, over, near):
        self.links, self.side, self.p, self.q, self.m = links, side, p, q, m
        self.far, self.over, self.near = far, over, near
        self.c_far, self.c_over, self.c_near = {}, {}, {}

    def start_far(self):
        for j in (2, 1, 3, 0):
            self.far[0, j] = self.m[2, j].astype(BF)
            self.c_far[j] = self.links.push(self.far.at[0, j], self.far.at[1, j], self.side, self.q[0 if j < 2 else 1])

    def send_over(self, way, j, extra):
        block = self.m[3 if way == 0 else 1, j]
        if extra:
            self.c_far[j].wait_recv()
            block = block + self.far[1, j].astype(F32)
        self.over[0, way, j] = block.astype(BF)
        self.c_over[way, j] = self.links.push(
            self.over.at[0, way, j], self.over.at[1, way, j], self.side, self.q[way])

    def start_over(self):
        for j in (2, 1, 3, 0):
            self.send_over(0 if j >= 2 else 1, j, False)

    def forward(self):
        for j in (2, 1, 3, 0):
            self.send_over(0 if j < 2 else 1, j, True)

    def turn(self):
        for j in (2, 1, 3, 0):
            self.c_over[0, j].wait_recv()
            self.c_over[1, j].wait_recv()
            block = self.m[0, j] + self.over[1, 0, j].astype(F32) + self.over[1, 1, j].astype(F32)
            if j == 0:
                self.own = block
            else:
                self.near[0, j] = block.astype(BF)
                self.c_near[j] = self.links.push(
                    self.near.at[0, j], self.near.at[1, j], self.side, self.p[(None, 1, 2, 0)[j]])

    def result(self):
        block = self.own
        for j in (1, 3, 2):
            self.c_near[j].wait_recv()
            block = block + self.near[1, j].astype(F32)
        return block


def routing(info, experts):
    lane = lax.broadcasted_iota(jnp.int32, (16, 128), 1)
    tiles = []
    for t in range(2):
        tile = jnp.zeros((16, 128), F32)
        for i in range(8):
            b, x = divmod(t * 8 + i, 4)
            block = info[x, b]
            moved_block = pltpu.roll(block, 16 * i, 1) if i else block
            tile = jnp.where(lane // 16 == i, moved_block, tile)
        tiles.append(tile)
    table = jnp.concatenate(tiles, axis=1)
    ids, route = table[0:8, :], table[8:16, :]
    first = lax.broadcasted_iota(jnp.int32, (256, 256), 0)
    later = lax.broadcasted_iota(jnp.int32, (256, 256), 1)
    before = jnp.where((first // 16 == later // 16) & (first < later), 1.0, 0.0).astype(BF)
    token = lax.broadcasted_iota(jnp.int32, (8, 256), 1) // 16
    named, weight = [], []
    for e in experts:
        hit = ids == e.astype(F32)
        named.append(jnp.sum(jnp.where(hit, 1.0, 0.0), axis=0, keepdims=True))
        weight.append(jnp.sum(jnp.where(hit, route, 0.0), axis=0, keepdims=True))
    named8 = jnp.concatenate(named + [jnp.zeros((4, 256), F32)], axis=0)
    rank = jnp.dot(named8.astype(BF), before, preferred_element_type=F32)
    spot = jnp.where(named8 > 0.5, (token % 4).astype(F32) * 4.0 + rank, -1.0)
    rows = lax.broadcasted_iota(jnp.int32, (16, 256), 0).astype(F32)
    picks, weighted = [], []
    for i in range(4):
        hit = rows == spot[i:i + 1, :]
        picks.append(jnp.where(hit, 1.0, 0.0))
        weighted.append(jnp.where(hit, weight[i], 0.0))
    picks, weighted = jnp.concatenate(picks, axis=0), jnp.concatenate(weighted, axis=0)
    pick, weigh = [], []
    for b in range(4):
        at = slice(64 * b, 64 * b + 64)
        pick.append(picks[:, at].astype(BF))
        high = weighted[:, at].astype(BF)
        weigh.append(jnp.concatenate([high, (weighted[:, at] - high.astype(F32)).astype(BF)], axis=1))
    return pick, weigh


SLOT = (0, 1, 3, 2)
HEADS0 = 20


def kernel(q_ref, k_ref, v_ref, lens_ref, wt_ref, res_ref, gain_ref, ids_ref, route_ref, up_ref, down_ref, out_ref,
           q_buf, k_buf, v_buf, w_buf, g0, g1, o_st, r_buf, hid, info, n_buf, x_st, x_own, x_far, x_via,
           w_gu, wd, h_own, h_far, a_own, a_far, d_near, y_st, z_buf, z_via, m_buf, far, over, near,
           res_buf, gain_buf, ids_buf, route_buf, lens_buf, loc, sends, recvs, os, orv):
    side, g, sa, sb, ca, cb, cx = place()
    other = 1 - side
    ap, am = moved(g, ca, sa, 1), moved(g, ca, sa, -1)
    b_way = [moved(g, cb, sb, i) for i in (1, -1, 2)]
    x_way = [moved(g, cx, 1, i) for i in (1, -1, 2)]
    links = Links(sends, recvs)
    barrier = pltpu.get_barrier_semaphore()

    def hello(to_side, to):
        pl.semaphore_signal(barrier, inc=1, device_id=(to_side, to), device_id_type=MESH)

    hello(side, ap)
    hello(side, am)
    for i in range(4):
        for j in range(4):
            if i or j:
                hello(side, moved(moved(g, cb, sb, i), cx, 1, j))
            hello(other, moved(moved(g, ca, sa, i), cx, 1, j))

    def fetch(src, dst, i):
        copy = pltpu.make_async_copy(src, dst, loc.at[i])
        copy.start()
        return copy

    def at_side(base, size):
        return pl.ds(pl.multiple_of(base * size, 128), size)

    c_lens = fetch(lens_ref, lens_buf, 14)
    c_q = fetch(q_ref.at[:, at_side(side, 4096)], q_buf, 0)
    c_k = fetch(k_ref.at[:, :, at_side(side, 256)], k_buf, 1)
    c_v = fetch(v_ref.at[:, :, at_side(side, 256)], v_buf, 2)
    w_own = wt_ref.at[:, at_side(side, 4096)]
    c_w = fetch(w_own, w_buf.at[ca], 3)
    c_ids = fetch(ids_ref, ids_buf, 10)
    c_route = fetch(route_ref, route_buf, 11)
    info[0, 0] = jnp.zeros((16, 128), F32)
    c_lens.wait()
    c_q.wait()
    c_k.wait()
    c_v.wait()
    group = HQ // KVH
    for kv in range(2):
        result = attend(q_buf, k_buf, v_buf, lens_buf, kv)
        for j in range(group):
            n = kv * group + j
            out, n = (g0, n) if n < HEADS0 else (g1, n - HEADS0)
            out[0, 0, :, n * HD:(n + 1) * HD] = result[j * S:(j + 1) * S, :]
    c_ids.wait()
    c_route.wait()
    info[0, 0, 0:8, 0:16] = ids_buf[...].astype(F32)
    info[0, 0, 8:16, 0:16] = route_buf[...]
    pl.semaphore_wait(barrier, 33)
    ring_w = Columns(links, side, ap, am, w_own, lambda source: w_buf.at[lax.rem(ca - source + 4, 4)])
    tell = Gather(links, side, b_way, x_way, info)

    def cut(size):
        return lambda ref, h: ref.at[:, h * size:(h + 1) * size]

    split = HEADS0 * HD
    ra = Gather(links, side, b_way, x_way, g0, cut(split // 2))
    rb = Gather(links, side, x_way, b_way, g1, cut((4096 - split) // 2))
    ra.start()
    rb.start()
    tell.start()
    ring_w.start()
    c_res = fetch(res_ref, res_buf, 12)
    c_gain = fetch(gain_ref, gain_buf, 13)
    c_ffn = []
    for h in range(2):
        depth = at_side(side if h == 0 else other, 2048)
        c_ffn.append(fetch(up_ref.at[depth, at_side(side, 384)], w_gu.at[h, :, 0:384], 4 + h))
        c_ffn.append(fetch(up_ref.at[depth, at_side(side + 2, 384)], w_gu.at[h, :, 384:768], 6 + h))
        c_ffn.append(fetch(down_ref.at[at_side(side if h == 0 else other, 384), at_side(side, 2048)], wd.at[h], 8 + h))
    ra.step1()
    rb.step1()
    tell.step1()
    ra.step2()
    rb.step2()
    tell.step2()
    ring_w.forward()
    ra.step3()
    rb.step3()
    tell.step3()
    tell.finish()
    experts = [moved(g, ca, sa, i) for i in range(4)]
    pick, weigh = routing(info, experts)
    ra.finish()
    rb.finish()
    c_w.wait()
    ring_w.finish()
    p0 = lax.dot_general(g0[...].reshape(256, split), w_buf[:, :, 0:split].reshape(256, split), NT,
                         preferred_element_type=F32)
    p1 = lax.dot_general(g1[...].reshape(256, 4096 - split), w_buf[:, :, split:4096].reshape(256, 4096 - split), NT,
                         preferred_element_type=F32)
    mine = cb * 4 + cx
    sent = []
    for n in sorted(range(16), key=lambda n: -((0, 1, 2, 1)[n // 4] + (0, 1, 2, 1)[n % 4])):
        bi, xi = n // 4, n % 4
        u = (xi * 4 + bi) * S
        block = (p0[u:u + S, :] + p1[n * S:(n + 1) * S, :]).astype(BF)
        o_st[n] = block
        if n == 0:
            r_buf[side, mine] = block
        to = moved(moved(g, cb, sb, -bi), cx, 1, -xi)
        for e in range(2):
            if n == 0 and e == 0:
                continue
            copy = pltpu.make_async_remote_copy(
                src_ref=o_st.at[n], dst_ref=r_buf.at[side, mine], send_sem=os.at[n, e], recv_sem=orv.at[side, mine],
                device_id=(side if e == 0 else other, to), device_id_type=MESH)
            copy.start()
            sent.append(copy)

    def arrived(source_side, n):
        pltpu.make_async_remote_copy(
            src_ref=o_st.at[0], dst_ref=r_buf.at[source_side, n], send_sem=os.at[0, 0], recv_sem=orv.at[source_side, n],
            device_id=(side, ap), device_id_type=MESH).wait_recv()

    for i in range(4):
        for j in range(4):
            if i or j:
                arrived(side, lax.rem(cb + i, 4) * 4 + lax.rem(cx + j, 4))
            arrived(other, lax.rem(ca + i, 4) * 4 + lax.rem(cx + j, 4))
    c_res.wait()
    c_gain.wait()
    squares = jnp.zeros((S, 128), F32)
    for y in range(4):
        for z in range(4):
            for m in range(2):
                pieces = []
                for x in (2 * m, 2 * m + 1):
                    pieces.append(r_buf[0, z * 4 + x, :, y * 64:(y + 1) * 64].astype(F32)
                                  + r_buf[1, y * 4 + x, :, z * 64:(z + 1) * 64].astype(F32))
                at = (y * 8 + z * 2 + m) * 128
                tile = res_buf[:, at:at + 128].astype(F32) + jnp.concatenate(pieces, axis=1)
                hid[:, at:at + 128] = tile
                squares = squares + tile * tile
    scaling = lax.rsqrt(jnp.sum(squares, axis=1, keepdims=True) * (1.0 / D) + 1e-06)

    half_at = pl.ds(pl.multiple_of(side * 2048, 128), 2048)
    na = Gather(links, side, x_way, b_way, n_buf, cut(1024))
    n_buf[0, 0] = (hid[:, half_at] * scaling * gain_buf[:, half_at]).astype(BF)
    na.start()

    def part(r):
        return slice(r * 1024, (r + 1) * 1024)

    a_way = (ap, am)
    c_via, c_on, c_one, c_swap = {}, {}, {}, {}

    def dispatch(b):
        rows = jnp.dot(pick[b], n_buf[b].reshape(64, 2048), preferred_element_type=F32).astype(BF)
        rows = rows.reshape(4, S, 2048)
        at = SLOT[b]
        x_st[at] = rows[1:]
        x_own[at, 0] = rows[0]
        for r in range(2):
            c_via[b, r] = links.push(x_st.at[at, 1, :, part(r)], x_via.at[r, at], side, a_way[r])
        c_one[b] = [links.push(x_st.at[at, 0], x_own.at[at, SLOT[1]], side, ap),
                    links.push(x_st.at[at, 2], x_own.at[at, SLOT[3]], side, am)]

    def pass_on(b):
        at = SLOT[b]
        for r in range(2):
            c_via[b, r].wait_recv()
            c_on[b, r] = links.push(x_via.at[r, at], x_own.at[at, SLOT[2], :, part(r)], side, a_way[r])

    def swap_three(b):
        at = SLOT[b]
        for copy in c_one[b]:
            copy.wait_recv()
        c_swap[b, 0] = links.push(x_own.at[at, 0:3], x_far.at[at, 0:3], other, g)

    def swap_last(b):
        at = SLOT[b]
        for r in range(2):
            c_on[b, r].wait_recv()
        c_swap[b, 1] = links.push(x_own.at[at, 3], x_far.at[at, 3], other, g)

    def front(src, dst, h, low, high):
        rows = src[low:high].reshape((high - low) * 64, 2048)
        dst[low:high] = jnp.dot(rows, w_gu[h], preferred_element_type=F32).reshape(high - low, 4, S, 768)

    na.step1()
    na.step2()
    dispatch(0)
    na.step3()
    na.wait(1, 2)
    na.wait(1, 3)
    dispatch(1)
    na.wait(3, 0)
    na.wait(3, 1)
    dispatch(3)
    pass_on(0)
    na.finish()
    dispatch(2)
    pass_on(1)
    pass_on(3)
    for b in (0, 1, 3):
        swap_three(b)
    pass_on(2)
    for b in (0, 1, 3):
        swap_last(b)
    for copy in c_ffn:
        copy.wait()
    front(x_own, h_own, 0, 0, 3)
    swap_three(2)
    for b in (0, 1, 3):
        c_swap[b, 0].wait_recv()
        c_swap[b, 1].wait_recv()
    front(x_far, h_far, 1, 0, 3)
    swap_last(2)
    front(x_own, h_own, 0, 3, 4)
    c_swap[2, 0].wait_recv()
    c_swap[2, 1].wait_recv()
    front(x_far, h_far, 1, 3, 4)
    swaps = []
    for i in range(4):
        both = h_own[i] + h_far[:, i]
        gate, up = both[:, :, 0:384], both[:, :, 384:768]
        a_own[i] = (gate / (1.0 + jnp.exp(-gate)) * up).astype(BF)
        swaps.append(links.push(a_own.at[i], a_far.at[:, i], other, g))
    d_near[...] = jnp.dot(a_own[...].reshape(256, 384), wd[0], preferred_element_type=F32).reshape(4, 64, 2048)
    for copy in swaps:
        copy.wait_recv()
    c_via, c_on, c_back = {}, {}, {}
    for b in (2, 1, 3, 0):
        at = SLOT[b]
        rows = d_near[at] + jnp.dot(a_far[at].reshape(64, 384), wd[1], preferred_element_type=F32)
        rows = rows.astype(BF).reshape(4, S, 2048)
        for a in (2, 1, 3):
            y_st[b, a - 1] = rows[SLOT[a]]
        z_buf[b, 0] = rows[0]
        for r in range(2):
            c_via[b, r] = links.push(y_st.at[b, 1, :, part(r)], z_via.at[r, b], side, a_way[r])
        c_back[b] = [links.push(y_st.at[b, 0], z_buf.at[b, 1], side, am),
                     links.push(y_st.at[b, 2], z_buf.at[b, 3], side, ap)]

    def back_on(b):
        for r in range(2):
            c_via[b, r].wait_recv()
            c_back[b].append(links.push(z_via.at[r, b], z_buf.at[b, 2, :, part(r)], side, a_way[r]))

    def mix(b):
        for copy in c_back[b]:
            copy.wait_recv()
        both = lax.dot_general(weigh[b], z_buf[b].reshape(64, 2048), (((0,), (0,)), ((), ())),
                               preferred_element_type=F32)
        m_buf[b] = (both[0:64, :] + both[64:128, :]).reshape(4, S, 2048)

    ring = Scatter(links, side, x_way, b_way, m_buf, far, over, near)
    back_on(2)
    back_on(1)
    back_on(3)
    mix(2)
    ring.start_far()
    back_on(0)
    mix(1)
    mix(3)
    ring.start_over()
    ring.forward()
    mix(0)
    ring.turn()
    out_ref[...] = hid[:, half_at] + ring.result()
    links.drain()
    for copy in sent:
        copy.wait_send()


def body(q, k, v, lens, out_weight, residual, norm_gain, expert_ids, route_weights, gate_up, down_weight):
    vm = pl.BlockSpec(memory_space=pltpu.VMEM)
    hb = pl.BlockSpec(memory_space=pltpu.HBM)
    dma = pltpu.SemaphoreType.DMA

    def vb(*shape):
        return pltpu.VMEM(shape, BF)

    def vf(*shape):
        return pltpu.VMEM(shape, F32)

    return pl.pallas_call(
        kernel,
        out_shape=jax.ShapeDtypeStruct((S, D // 2), F32),
        in_specs=[hb] * 11,
        out_specs=vm,
        scratch_shapes=[
            vb(S, 4096), vb(S, CTX, 256), vb(S, CTX, 256), vb(4, 64, 4096),
            vb(4, 4, S, HEADS0 * HD), vb(4, 4, S, 4096 - HEADS0 * HD),
            vb(16, S, 256), vb(2, 16, S, 256), vf(S, D), vf(4, 4, 16, 128), vb(4, 4, S, 2048),
            vb(4, 3, S, 2048), vb(4, 4, S, 2048), vb(4, 4, S, 2048), vb(2, 4, S, 1024),
            vb(2, 2048, 768), vb(2, 384, 2048), vf(4, 4, S, 768), vf(4, 4, S, 768), vb(4, 4, S, 384), vb(4, 4, S, 384),
            vf(4, 64, 2048), vb(4, 3, S, 2048), vb(4, 4, S, 2048), vb(2, 4, S, 1024), vf(4, 4, S, 2048),
            vb(2, 4, S, 2048), vb(2, 2, 4, S, 2048), vb(2, 4, S, 2048),
            vb(S, D), vf(1, D), pltpu.VMEM((8, S), jnp.int32), vf(8, S), pltpu.SMEM((S,), jnp.int32),
            dma((15,)), dma((160,)), dma((160,)), dma((16, 2)), dma((2, 16)),
        ],
        compiler_params=pltpu.CompilerParams(collective_id=0, has_side_effects=True, vmem_limit_bytes=46 << 20),
        name="decode_layer",
    )(*[pltpu.with_memory_space_constraint(value, pltpu.HBM) for value in (
        q, k, v, lens, out_weight.T, residual, norm_gain.reshape(1, -1), expert_ids.T, route_weights.T,
        gate_up[0], down_weight[0])]).astype(BF)


def solution(mesh):
    return jax.shard_map(
        body,
        mesh=mesh,
        in_specs=(
            P("grp", None), P("grp", None, None), P("grp", None, None), P("grp"), P(None, "grp"), P("grp", None), P(),
            P("grp", None), P("grp", None), P("grp", None, None), P("grp", None, None),
        ),
        out_specs=P("grp", "side"),
        check_vma=False,
    )
```

```python
import jax
import jax.numpy as jnp
from jax import lax
from jax.experimental import pallas as pl
from jax.experimental.pallas import tpu as pltpu
from jax.sharding import PartitionSpec as P

HQ = 64
KVH = 4
HD = 128
HID = 768
TOPK = 8
CTX = 128
D = 4096
S = 16
MESH = pl.DeviceIdType.MESH
BF = jnp.bfloat16
F32 = jnp.float32
NT = (((1,), (1,)), ((), ()))


def place():
    side = lax.axis_index("side")
    g = lax.axis_index("grp")
    sa = 16 - 12 * side
    sb = 4 + 12 * side
    ca = lax.rem(g // sa, 4)
    cb = lax.rem(g // sb, 4)
    cx = lax.rem(g, 4)
    return side, g, sa, sb, ca, cb, cx


def moved(g, c, stride, by):
    return g + (lax.rem(c + by + 4, 4) - c) * stride


def attend(q_buf, k_buf, v_buf, lens_ref, kv):
    lane = lax.broadcasted_iota(jnp.int32, (S, CTX), 1)
    row = lax.broadcasted_iota(jnp.int32, (S, CTX), 0)
    live = jnp.zeros((S, CTX), jnp.int32)
    for s in range(S):
        live = jnp.where(row == s, lens_ref[s], live)
    group = HQ // KVH
    live = jnp.concatenate([live] * group, axis=0)
    lane = jnp.concatenate([lane] * group, axis=0)
    row = jnp.concatenate([row] * group, axis=0)
    queries = jnp.concatenate(
        [q_buf[:, (kv * group + j) * HD:(kv * group + j + 1) * HD] for j in range(group)], axis=0)
    scores = jnp.zeros((S * group, CTX), F32)
    for s in range(S):
        part = lax.dot_general(queries, k_buf[s, :, kv * HD:(kv + 1) * HD], NT, preferred_element_type=F32)
        scores = jnp.where(row == s, part, scores)
    scores = jnp.where(lane < live, scores * HD ** (-0.5), -1e30)
    lifted = jnp.exp(scores - jnp.max(scores, axis=1, keepdims=True))
    weights = (lifted / jnp.sum(lifted, axis=1, keepdims=True))
    spread = jnp.concatenate([jnp.where(row == s, weights, 0.0).astype(BF) for s in range(S)], axis=1)
    values = v_buf[:, :, kv * HD:(kv + 1) * HD].reshape(S * CTX, HD)
    return jnp.dot(spread, values, preferred_element_type=F32).astype(BF)


class Links:
    def __init__(self, sends, recvs):
        self.sends, self.recvs, self.used, self.open = sends, recvs, 0, []

    def make(self, src, dst, to_side, to):
        i = self.used
        self.used += 1
        copy = pltpu.make_async_remote_copy(
            src_ref=src, dst_ref=dst, send_sem=self.sends.at[i], recv_sem=self.recvs.at[i],
            device_id=(to_side, to), device_id_type=MESH)
        self.open.append(copy)
        return copy

    def push(self, src, dst, to_side, to):
        copy = self.make(src, dst, to_side, to)
        copy.start()
        return copy

    def drain(self):
        for copy in self.open:
            copy.wait_send()


class Columns:
    def __init__(self, links, side, plus, minus, own, slot):
        self.links, self.side, self.plus, self.minus, self.own, self.slot = links, side, plus, minus, own, slot

    def start(self):
        low, high = slice(0, 32), slice(32, 64)
        push, own, slot = self.links.push, self.own, self.slot(0)
        self.c0 = push(own.at[low], slot.at[low], self.side, self.plus)
        self.c1 = push(own.at[high], slot.at[high], self.side, self.minus)
        self.rest = [push(own.at[high], slot.at[high], self.side, self.plus),
                     push(own.at[low], slot.at[low], self.side, self.minus)]

    def forward(self):
        self.c0.wait_recv()
        at = self.slot(1).at[0:32]
        self.rest.append(self.links.push(at, at, self.side, self.plus))
        self.c1.wait_recv()
        at = self.slot(3).at[32:64]
        self.rest.append(self.links.push(at, at, self.side, self.minus))

    def finish(self):
        for copy in self.rest:
            copy.wait_recv()


class Gather:
    def __init__(self, links, side, p, q, buf, direct):
        self.links, self.side, self.p, self.q, self.buf, self.direct = links, side, p, q, buf, direct
        self.got = {}

    def send(self, i, j, to, di, dj):
        at = (i + di) % 4, (j + dj) % 4
        self.got[at] = self.links.push(self.buf.at[i, j], self.buf.at[at], self.side, to)

    def wait(self, i, j):
        self.got.pop((i, j)).wait_recv()

    def along_q(self, j):
        if self.direct:
            self.send(0, j, self.q[2], 2, 0)
        self.send(0, j, self.q[0], 1, 0)
        self.send(0, j, self.q[1], 3, 0)

    def start(self):
        self.send(0, 0, self.p[2], 0, 2)
        self.send(0, 0, self.p[0], 0, 1)
        self.send(0, 0, self.p[1], 0, 3)
        self.along_q(0)

    def step1(self):
        self.wait(0, 1)
        self.along_q(1)
        self.wait(0, 3)
        self.along_q(3)
        if not self.direct:
            self.wait(1, 0)
            self.send(1, 0, self.q[0], 1, 0)

    def step2(self):
        self.wait(0, 2)
        self.along_q(2)

    def step3(self):
        self.wait(1, 1)
        self.send(1, 1, self.q[0], 1, 0)
        self.wait(3, 3)
        self.send(3, 3, self.q[1], 3, 0)
        self.wait(3, 2)
        self.send(3, 2, self.q[1], 3, 0)

    def finish(self):
        for key in list(self.got):
            self.wait(*key)


class Scatter:
    def __init__(self, links, side, p, q, m, over, near):
        self.links, self.side, self.p, self.q, self.m, self.over, self.near = links, side, p, q, m, over, near
        self.c_over, self.c_near = {}, {}

    def along_q(self, i):
        for j in (2, 1, 3, 0):
            self.over[0, i - 1, j] = self.m[i, j].astype(BF)
            self.c_over[i, j] = self.links.push(
                self.over.at[0, i - 1, j], self.over.at[1, i - 1, j], self.side, self.q[(None, 1, 2, 0)[i]])

    def turn(self):
        for j in (2, 1, 3, 0):
            block = self.m[0, j]
            for i in (2, 1, 3):
                self.c_over[i, j].wait_recv()
                block = block + self.over[1, i - 1, j].astype(F32)
            if j == 0:
                self.own = block
            else:
                self.near[0, j] = block.astype(BF)
                self.c_near[j] = self.links.push(
                    self.near.at[0, j], self.near.at[1, j], self.side, self.p[(None, 1, 2, 0)[j]])

    def result(self):
        block = self.own
        for j in (1, 3, 2):
            self.c_near[j].wait_recv()
            block = block + self.near[1, j].astype(F32)
        return block


def routing(info, experts):
    lane = lax.broadcasted_iota(jnp.int32, (16, 128), 1)
    tiles = []
    for t in range(2):
        tile = jnp.zeros((16, 128), F32)
        for i in range(8):
            b, x = divmod(t * 8 + i, 4)
            block = info[x, b]
            moved_block = pltpu.roll(block, 16 * i, 1) if i else block
            tile = jnp.where(lane // 16 == i, moved_block, tile)
        tiles.append(tile)
    table = jnp.concatenate(tiles, axis=1)
    ids, route = table[0:8, :], table[8:16, :]
    first = lax.broadcasted_iota(jnp.int32, (256, 256), 0)
    later = lax.broadcasted_iota(jnp.int32, (256, 256), 1)
    before = jnp.where((first // 16 == later // 16) & (first < later), 1.0, 0.0).astype(BF)
    token = lax.broadcasted_iota(jnp.int32, (8, 256), 1) // 16
    named, weight = [], []
    for e in experts:
        hit = ids == e.astype(F32)
        named.append(jnp.sum(jnp.where(hit, 1.0, 0.0), axis=0, keepdims=True))
        weight.append(jnp.sum(jnp.where(hit, route, 0.0), axis=0, keepdims=True))
    named8 = jnp.concatenate(named + [jnp.zeros((4, 256), F32)], axis=0)
    rank = jnp.dot(named8.astype(BF), before, preferred_element_type=F32)
    spot = jnp.where(named8 > 0.5, (token % 4).astype(F32) * 4.0 + rank, -1.0)
    rows = lax.broadcasted_iota(jnp.int32, (16, 256), 0).astype(F32)
    picks, weighted = [], []
    for i in range(4):
        hit = rows == spot[i:i + 1, :]
        picks.append(jnp.where(hit, 1.0, 0.0))
        weighted.append(jnp.where(hit, weight[i], 0.0))
    picks, weighted = jnp.concatenate(picks, axis=0), jnp.concatenate(weighted, axis=0)
    pick, weigh = [], []
    for b in range(4):
        at = slice(64 * b, 64 * b + 64)
        pick.append(picks[:, at].astype(BF))
        high = weighted[:, at].astype(BF)
        weigh.append(jnp.concatenate([high, (weighted[:, at] - high.astype(F32)).astype(BF)], axis=1))
    return pick, weigh


SLOT = (0, 1, 3, 2)
HEADS0 = 20


def kernel(q_ref, k_ref, v_ref, lens_ref, wt_ref, res_ref, gain_ref, ids_ref, route_ref, up_ref, down_ref, out_ref,
           q_buf, k_buf, v_buf, w_buf, g0, g1, o_st, r_buf, hid, info, n_buf, x_st, x_own, x_far,
           w_gu, wd, h_own, h_far, a_own, a_far, d_near, y_st, z_buf, m_buf, over, near,
           res_buf, gain_buf, ids_buf, route_buf, lens_buf, loc, sends, recvs, os, orv):
    side, g, sa, sb, ca, cb, cx = place()
    other = 1 - side
    a_way = [moved(g, ca, sa, i) for i in (1, -1, 2)]
    ap, am = a_way[0], a_way[1]
    b_way = [moved(g, cb, sb, i) for i in (1, -1, 2)]
    x_way = [moved(g, cx, 1, i) for i in (1, -1, 2)]
    links = Links(sends, recvs)
    barrier = pltpu.get_barrier_semaphore()

    def hello(to_side, to):
        pl.semaphore_signal(barrier, inc=1, device_id=(to_side, to), device_id_type=MESH)

    for to in a_way:
        hello(side, to)
    for i in range(4):
        for j in range(4):
            if i or j:
                hello(side, moved(moved(g, cb, sb, i), cx, 1, j))
            hello(other, moved(moved(g, ca, sa, i), cx, 1, j))

    def fetch(src, dst, i):
        copy = pltpu.make_async_copy(src, dst, loc.at[i])
        copy.start()
        return copy

    def at_side(base, size):
        return pl.ds(pl.multiple_of(base * size, 128), size)

    c_lens = fetch(lens_ref, lens_buf, 14)
    c_q = fetch(q_ref.at[:, at_side(side, 4096)], q_buf, 0)
    c_k = fetch(k_ref.at[:, :, at_side(side, 256)], k_buf, 1)
    c_v = fetch(v_ref.at[:, :, at_side(side, 256)], v_buf, 2)
    w_own = wt_ref.at[:, at_side(side, 4096)]
    c_w = fetch(w_own, w_buf.at[ca], 3)
    c_ids = fetch(ids_ref, ids_buf, 10)
    c_route = fetch(route_ref, route_buf, 11)
    info[0, 0] = jnp.zeros((16, 128), F32)
    c_lens.wait()
    c_q.wait()
    c_k.wait()
    c_v.wait()
    group = HQ // KVH
    for kv in range(2):
        result = attend(q_buf, k_buf, v_buf, lens_buf, kv)
        for j in range(group):
            n = kv * group + j
            out, n = (g0, n) if n < HEADS0 else (g1, n - HEADS0)
            out[0, 0, :, n * HD:(n + 1) * HD] = result[j * S:(j + 1) * S, :]
    c_ids.wait()
    c_route.wait()
    info[0, 0, 0:8, 0:16] = ids_buf[...].astype(F32)
    info[0, 0, 8:16, 0:16] = route_buf[...]
    pl.semaphore_wait(barrier, 34)
    ring_w = Columns(links, side, ap, am, w_own, lambda source: w_buf.at[lax.rem(ca - source + 4, 4)])
    split = HEADS0 * HD
    ra = Gather(links, side, b_way, x_way, g0, False)
    rb = Gather(links, side, x_way, b_way, g1, False)
    ring_w.start()
    ra.start()
    rb.start()
    told = []
    for i in range(4):
        for j in range(4):
            if i or j:
                told.append(links.push(info.at[0, 0], info.at[j, i], side, moved(moved(g, cb, sb, i), cx, 1, j)))
    c_res = fetch(res_ref, res_buf, 12)
    c_gain = fetch(gain_ref, gain_buf, 13)
    c_ffn = []
    for h in range(2):
        depth = at_side(side if h == 0 else other, 2048)
        c_ffn.append(fetch(up_ref.at[depth, at_side(side, 384)], w_gu.at[h, :, 0:384], 4 + h))
        c_ffn.append(fetch(up_ref.at[depth, at_side(side + 2, 384)], w_gu.at[h, :, 384:768], 6 + h))
        c_ffn.append(fetch(down_ref.at[at_side(side if h == 0 else other, 384), at_side(side, 2048)], wd.at[h], 8 + h))
    ra.step1()
    rb.step1()
    ra.step2()
    rb.step2()
    ring_w.forward()
    ra.step3()
    rb.step3()
    ra.finish()
    rb.finish()
    c_w.wait()
    ring_w.finish()
    p0 = lax.dot_general(g0[...].reshape(256, split), w_buf[:, :, 0:split].reshape(256, split), NT,
                         preferred_element_type=F32)
    p1 = lax.dot_general(g1[...].reshape(256, 4096 - split), w_buf[:, :, split:4096].reshape(256, 4096 - split), NT,
                         preferred_element_type=F32)
    mine = cb * 4 + cx
    sent = []
    for n in sorted(range(16), key=lambda n: -((0, 1, 2, 1)[n // 4] + (0, 1, 2, 1)[n % 4])):
        bi, xi = n // 4, n % 4
        u = (xi * 4 + bi) * S
        block = (p0[u:u + S, :] + p1[n * S:(n + 1) * S, :]).astype(BF)
        o_st[n] = block
        if n == 0:
            r_buf[side, mine] = block
        to = moved(moved(g, cb, sb, -bi), cx, 1, -xi)
        for e in range(2):
            if n == 0 and e == 0:
                continue
            copy = pltpu.make_async_remote_copy(
                src_ref=o_st.at[n], dst_ref=r_buf.at[side, mine], send_sem=os.at[n, e], recv_sem=orv.at[side, mine],
                device_id=(side if e == 0 else other, to), device_id_type=MESH)
            copy.start()
            sent.append(copy)

    def arrived(source_side, n):
        pltpu.make_async_remote_copy(
            src_ref=o_st.at[0], dst_ref=r_buf.at[source_side, n], send_sem=os.at[0, 0], recv_sem=orv.at[source_side, n],
            device_id=(side, ap), device_id_type=MESH).wait_recv()

    for copy in told:
        copy.wait_recv()
    experts = [moved(g, ca, sa, i) for i in range(4)]
    pick, weigh = routing(info, experts)
    for i in range(4):
        for j in range(4):
            if i or j:
                arrived(side, lax.rem(cb + i, 4) * 4 + lax.rem(cx + j, 4))
            arrived(other, lax.rem(ca + i, 4) * 4 + lax.rem(cx + j, 4))
    c_res.wait()
    c_gain.wait()
    squares = jnp.zeros((S, 128), F32)
    for y in range(4):
        for z in range(4):
            for m in range(2):
                pieces = []
                for x in (2 * m, 2 * m + 1):
                    pieces.append(r_buf[0, z * 4 + x, :, y * 64:(y + 1) * 64].astype(F32)
                                  + r_buf[1, y * 4 + x, :, z * 64:(z + 1) * 64].astype(F32))
                at = (y * 8 + z * 2 + m) * 128
                tile = res_buf[:, at:at + 128].astype(F32) + jnp.concatenate(pieces, axis=1)
                hid[:, at:at + 128] = tile
                squares = squares + tile * tile
    scaling = lax.rsqrt(jnp.sum(squares, axis=1, keepdims=True) * (1.0 / D) + 1e-06)

    half_at = pl.ds(pl.multiple_of(side * 2048, 128), 2048)
    na = Gather(links, side, x_way, b_way, n_buf, True)
    n_buf[0, 0] = (hid[:, half_at] * scaling * gain_buf[:, half_at]).astype(BF)
    na.start()

    c_one, c_swap = {}, {}

    def dispatch(b):
        rows = jnp.dot(pick[b], n_buf[b].reshape(64, 2048), preferred_element_type=F32).astype(BF)
        rows = rows.reshape(4, S, 2048)
        x_st[b] = rows[1:]
        x_own[SLOT[b], 0] = rows[0]
        c_one[b] = [links.push(x_st.at[b, a - 1], x_own.at[SLOT[b], SLOT[a]], side, a_way[(None, 0, 2, 1)[a]])
                    for a in (2, 1, 3)]

    def swap(b):
        for copy in c_one[b]:
            copy.wait_recv()
        c_swap[b] = links.push(x_own.at[SLOT[b]], x_far.at[SLOT[b]], other, g)

    def front(src, dst, h, low, high):
        rows = src[low:high].reshape((high - low) * 64, 2048)
        dst[low:high] = jnp.dot(rows, w_gu[h], preferred_element_type=F32).reshape(high - low, 4, S, 768)

    na.step1()
    na.step2()
    dispatch(0)
    for j in range(4):
        na.wait(1, j)
    dispatch(1)
    for j in range(4):
        na.wait(3, j)
    dispatch(3)
    na.finish()
    dispatch(2)
    for copy in c_ffn:
        copy.wait()
    swap(0)
    swap(1)
    swap(3)
    front(x_own, h_own, 0, 0, 3)
    swap(2)
    for b in (0, 1, 3):
        c_swap[b].wait_recv()
    front(x_far, h_far, 1, 0, 3)
    front(x_own, h_own, 0, 3, 4)
    c_swap[2].wait_recv()
    front(x_far, h_far, 1, 3, 4)
    swaps = []
    for i in range(4):
        both = h_own[i] + h_far[:, i]
        gate, up = both[:, :, 0:384], both[:, :, 384:768]
        a_own[i] = (gate / (1.0 + jnp.exp(-gate)) * up).astype(BF)
        swaps.append(links.push(a_own.at[i], a_far.at[:, i], other, g))
    d_near[...] = jnp.dot(a_own[...].reshape(256, 384), wd[0], preferred_element_type=F32).reshape(4, 64, 2048)
    for copy in swaps:
        copy.wait_recv()
    c_back = {}
    for b in (2, 1, 3, 0):
        rows = d_near[SLOT[b]] + jnp.dot(a_far[SLOT[b]].reshape(64, 384), wd[1], preferred_element_type=F32)
        rows = rows.astype(BF).reshape(4, S, 2048)
        z_buf[b, 0] = rows[0]
        c_back[b] = []
        for a in (2, 1, 3):
            y_st[b, a - 1] = rows[SLOT[a]]
            c_back[b].append(links.push(y_st.at[b, a - 1], z_buf.at[b, a], side, a_way[(None, 1, 2, 0)[a]]))

    def mix(b):
        for copy in c_back[b]:
            copy.wait_recv()
        both = lax.dot_general(weigh[b], z_buf[b].reshape(64, 2048), (((0,), (0,)), ((), ())),
                               preferred_element_type=F32)
        m_buf[b] = (both[0:64, :] + both[64:128, :]).reshape(4, S, 2048)

    ring = Scatter(links, side, x_way, b_way, m_buf, over, near)
    mix(2)
    ring.along_q(2)
    mix(1)
    ring.along_q(1)
    mix(3)
    ring.along_q(3)
    mix(0)
    ring.turn()
    out_ref[...] = hid[:, half_at] + ring.result()
    links.drain()
    for copy in sent:
        copy.wait_send()


def body(q, k, v, lens, out_weight, residual, norm_gain, expert_ids, route_weights, gate_up, down_weight):
    vm = pl.BlockSpec(memory_space=pltpu.VMEM)
    hb = pl.BlockSpec(memory_space=pltpu.HBM)
    dma = pltpu.SemaphoreType.DMA

    def vb(*shape):
        return pltpu.VMEM(shape, BF)

    def vf(*shape):
        return pltpu.VMEM(shape, F32)

    return pl.pallas_call(
        kernel,
        out_shape=jax.ShapeDtypeStruct((S, D // 2), F32),
        in_specs=[hb] * 11,
        out_specs=vm,
        scratch_shapes=[
            vb(S, 4096), vb(S, CTX, 256), vb(S, CTX, 256), vb(4, 64, 4096),
            vb(4, 4, S, HEADS0 * HD), vb(4, 4, S, 4096 - HEADS0 * HD),
            vb(16, S, 256), vb(2, 16, S, 256), vf(S, D), vf(4, 4, 16, 128), vb(4, 4, S, 2048),
            vb(4, 3, S, 2048), vb(4, 4, S, 2048), vb(4, 4, S, 2048),
            vb(2, 2048, 768), vb(2, 384, 2048), vf(4, 4, S, 768), vf(4, 4, S, 768), vb(4, 4, S, 384), vb(4, 4, S, 384),
            vf(4, 64, 2048), vb(4, 3, S, 2048), vb(4, 4, S, 2048), vf(4, 4, S, 2048), vb(2, 3, 4, S, 2048), vb(2, 4, S, 2048),
            vb(S, D), vf(1, D), pltpu.VMEM((8, S), jnp.int32), vf(8, S), pltpu.SMEM((S,), jnp.int32),
            dma((15,)), dma((160,)), dma((160,)), dma((16, 2)), dma((2, 16)),
        ],
        compiler_params=pltpu.CompilerParams(collective_id=0, has_side_effects=True, vmem_limit_bytes=46 << 20),
        name="decode_layer",
    )(*[pltpu.with_memory_space_constraint(value, pltpu.HBM) for value in (
        q, k, v, lens, out_weight.T, residual, norm_gain.reshape(1, -1), expert_ids.T, route_weights.T,
        gate_up[0], down_weight[0])]).astype(BF)


def solution(mesh):
    return jax.shard_map(
        body,
        mesh=mesh,
        in_specs=(
            P("grp", None), P("grp", None, None), P("grp", None, None), P("grp"), P(None, "grp"), P("grp", None), P(),
            P("grp", None), P("grp", None), P("grp", None, None), P("grp", None, None),
        ),
        out_specs=P("grp", "side"),
        check_vma=False,
    )
```

```python
import jax
import jax.numpy as jnp
from jax import lax
from jax.experimental import pallas as pl
from jax.experimental.pallas import tpu as pltpu
from jax.sharding import PartitionSpec as P

HQ = 64
KVH = 4
HD = 128
HID = 768
TOPK = 8
CTX = 128
D = 4096
S = 16
MESH = pl.DeviceIdType.MESH
BF = jnp.bfloat16
F32 = jnp.float32
NT = (((1,), (1,)), ((), ()))


def place():
    side = lax.axis_index("side")
    g = lax.axis_index("grp")
    sa = 16 - 12 * side
    sb = 4 + 12 * side
    ca = lax.rem(g // sa, 4)
    cb = lax.rem(g // sb, 4)
    cx = lax.rem(g, 4)
    return side, g, sa, sb, ca, cb, cx


def moved(g, c, stride, by):
    return g + (lax.rem(c + by + 4, 4) - c) * stride


def attend(q_buf, k_buf, v_buf, lens_ref, kv):
    lane = lax.broadcasted_iota(jnp.int32, (S, CTX), 1)
    row = lax.broadcasted_iota(jnp.int32, (S, CTX), 0)
    live = jnp.zeros((S, CTX), jnp.int32)
    for s in range(S):
        live = jnp.where(row == s, lens_ref[s], live)
    group = HQ // KVH
    live = jnp.concatenate([live] * group, axis=0)
    lane = jnp.concatenate([lane] * group, axis=0)
    row = jnp.concatenate([row] * group, axis=0)
    queries = jnp.concatenate(
        [q_buf[:, (kv * group + j) * HD:(kv * group + j + 1) * HD] for j in range(group)], axis=0)
    scores = jnp.zeros((S * group, CTX), F32)
    for s in range(S):
        part = lax.dot_general(queries, k_buf[s, :, kv * HD:(kv + 1) * HD], NT, preferred_element_type=F32)
        scores = jnp.where(row == s, part, scores)
    scores = jnp.where(lane < live, scores * HD ** (-0.5), -1e30)
    lifted = jnp.exp(scores - jnp.max(scores, axis=1, keepdims=True))
    weights = (lifted / jnp.sum(lifted, axis=1, keepdims=True))
    spread = jnp.concatenate([jnp.where(row == s, weights, 0.0).astype(BF) for s in range(S)], axis=1)
    values = v_buf[:, :, kv * HD:(kv + 1) * HD].reshape(S * CTX, HD)
    return jnp.dot(spread, values, preferred_element_type=F32).astype(BF)


class Links:
    def __init__(self, sends, recvs):
        self.sends, self.recvs, self.used, self.open = sends, recvs, 0, []

    def make(self, src, dst, to_side, to):
        i = self.used
        self.used += 1
        copy = pltpu.make_async_remote_copy(
            src_ref=src, dst_ref=dst, send_sem=self.sends.at[i], recv_sem=self.recvs.at[i],
            device_id=(to_side, to), device_id_type=MESH)
        self.open.append(copy)
        return copy

    def push(self, src, dst, to_side, to):
        copy = self.make(src, dst, to_side, to)
        copy.start()
        return copy

    def drain(self):
        for copy in self.open:
            copy.wait_send()


class Columns:
    def __init__(self, links, side, plus, minus, own, slot):
        self.links, self.side, self.plus, self.minus, self.own, self.slot = links, side, plus, minus, own, slot

    def start(self):
        low, high = slice(0, 32), slice(32, 64)
        push, own, slot = self.links.push, self.own, self.slot(0)
        self.c0 = push(own.at[low], slot.at[low], self.side, self.plus)
        self.c1 = push(own.at[high], slot.at[high], self.side, self.minus)
        self.rest = [push(own.at[high], slot.at[high], self.side, self.plus),
                     push(own.at[low], slot.at[low], self.side, self.minus)]

    def forward(self):
        self.c0.wait_recv()
        at = self.slot(1).at[0:32]
        self.rest.append(self.links.push(at, at, self.side, self.plus))
        self.c1.wait_recv()
        at = self.slot(3).at[32:64]
        self.rest.append(self.links.push(at, at, self.side, self.minus))

    def finish(self):
        for copy in self.rest:
            copy.wait_recv()


class Gather:
    def __init__(self, links, side, p, q, buf, direct):
        self.links, self.side, self.p, self.q, self.buf, self.direct = links, side, p, q, buf, direct
        self.got = {}

    def send(self, i, j, to, di, dj):
        at = (i + di) % 4, (j + dj) % 4
        self.got[at] = self.links.push(self.buf.at[i, j], self.buf.at[at], self.side, to)

    def wait(self, i, j):
        self.got.pop((i, j)).wait_recv()

    def along_q(self, j):
        self.send(0, j, self.q[0], 1, 0)
        self.send(0, j, self.q[1], 3, 0)
        if self.direct:
            self.send(0, j, self.q[2], 2, 0)

    def start(self):
        self.send(0, 0, self.p[0], 0, 1)
        self.send(0, 0, self.p[1], 0, 3)
        self.send(0, 0, self.p[2], 0, 2)
        self.along_q(0)

    def step1(self):
        self.wait(0, 1)
        self.along_q(1)
        self.wait(0, 3)
        self.along_q(3)
        if not self.direct:
            self.wait(1, 0)
            self.send(1, 0, self.q[0], 1, 0)

    def step2(self):
        self.wait(0, 2)
        self.along_q(2)

    def step3(self):
        self.wait(1, 1)
        self.send(1, 1, self.q[0], 1, 0)
        self.wait(3, 3)
        self.send(3, 3, self.q[1], 3, 0)
        self.wait(3, 2)
        self.send(3, 2, self.q[1], 3, 0)

    def finish(self):
        for key in list(self.got):
            self.wait(*key)


class Scatter:
    def __init__(self, links, side, p, q, block, over, near):
        self.links, self.side, self.p, self.q, self.block = links, side, p, q, block
        self.over, self.near = over, near
        self.c_over, self.c_near = {}, {}

    def along_q(self, i, j):
        self.over[0, i - 1, j] = self.block(i, j).astype(BF)
        self.c_over[i, j] = self.links.push(
            self.over.at[0, i - 1, j], self.over.at[1, i - 1, j], self.side, self.q[(None, 1, 2, 0)[i]])

    def turn(self, j):
        block = self.block(0, j)
        for i in (2, 1, 3):
            self.c_over[i, j].wait_recv()
            block = block + self.over[1, i - 1, j].astype(F32)
        if j == 0:
            self.own = block
        else:
            self.near[0, j] = block.astype(BF)
            self.c_near[j] = self.links.push(
                self.near.at[0, j], self.near.at[1, j], self.side, self.p[(None, 1, 2, 0)[j]])

    def result(self):
        block = self.own
        for j in (1, 3, 2):
            self.c_near[j].wait_recv()
            block = block + self.near[1, j].astype(F32)
        return block


def routing(info, experts):
    lane = lax.broadcasted_iota(jnp.int32, (16, 128), 1)
    tiles = []
    for t in range(2):
        tile = jnp.zeros((16, 128), F32)
        for i in range(8):
            b, x = divmod(t * 8 + i, 4)
            block = info[x, b]
            moved_block = pltpu.roll(block, 16 * i, 1) if i else block
            tile = jnp.where(lane // 16 == i, moved_block, tile)
        tiles.append(tile)
    table = jnp.concatenate(tiles, axis=1)
    ids, route = table[0:8, :], table[8:16, :]
    first = lax.broadcasted_iota(jnp.int32, (256, 256), 0)
    later = lax.broadcasted_iota(jnp.int32, (256, 256), 1)
    before = jnp.where((first // 16 == later // 16) & (first < later), 1.0, 0.0).astype(BF)
    token = lax.broadcasted_iota(jnp.int32, (8, 256), 1) // 16
    named, weight = [], []
    for e in experts:
        hit = ids == e.astype(F32)
        named.append(jnp.sum(jnp.where(hit, 1.0, 0.0), axis=0, keepdims=True))
        weight.append(jnp.sum(jnp.where(hit, route, 0.0), axis=0, keepdims=True))
    named8 = jnp.concatenate(named + [jnp.zeros((4, 256), F32)], axis=0)
    rank = jnp.dot(named8.astype(BF), before, preferred_element_type=F32)
    spot = jnp.where(named8 > 0.5, (token % 4).astype(F32) * 4.0 + rank, -1.0)
    rows = lax.broadcasted_iota(jnp.int32, (16, 256), 0).astype(F32)
    picks, weighted = [], []
    for i in range(4):
        hit = rows == spot[i:i + 1, :]
        picks.append(jnp.where(hit, 1.0, 0.0))
        weighted.append(jnp.where(hit, weight[i], 0.0))
    picks, weighted = jnp.concatenate(picks, axis=0), jnp.concatenate(weighted, axis=0)
    pick, weigh = [], []
    for b in range(4):
        at = slice(64 * b, 64 * b + 64)
        pick.append(picks[:, at].astype(BF))
        high = weighted[:, at].astype(BF)
        weigh.append(jnp.concatenate([high, (weighted[:, at] - high.astype(F32)).astype(BF)], axis=1))
    return pick, weigh


SLOT = (0, 1, 3, 2)
HEADS0 = 20
CUT = 1280


def kernel(q_ref, k_ref, v_ref, lens_ref, wt_ref, res_ref, gain_ref, ids_ref, route_ref, up_ref, down_ref, out_ref,
           q_buf, k_buf, v_buf, w_buf, g0, g1, o_st, r_buf, hid, info, n0, n1, x_st, x_own, x_far,
           w_gu, wd, h_own, h_far, a_own, a_far, d_near, y_st, z_buf, m_buf, over0, near0, over1, near1,
           res_buf, gain_buf, ids_buf, route_buf, lens_buf, loc, sends, recvs, os, orv):
    side, g, sa, sb, ca, cb, cx = place()
    other = 1 - side
    a_way = [moved(g, ca, sa, i) for i in (1, -1, 2)]
    ap, am = a_way[0], a_way[1]
    b_way = [moved(g, cb, sb, i) for i in (1, -1, 2)]
    x_way = [moved(g, cx, 1, i) for i in (1, -1, 2)]
    links = Links(sends, recvs)
    barrier = pltpu.get_barrier_semaphore()

    def hello(to_side, to):
        pl.semaphore_signal(barrier, inc=1, device_id=(to_side, to), device_id_type=MESH)

    for to in a_way:
        hello(side, to)
    for i in range(4):
        for j in range(4):
            if i or j:
                hello(side, moved(moved(g, cb, sb, i), cx, 1, j))
            hello(other, moved(moved(g, ca, sa, i), cx, 1, j))

    def fetch(src, dst, i):
        copy = pltpu.make_async_copy(src, dst, loc.at[i])
        copy.start()
        return copy

    def at_side(base, size):
        return pl.ds(pl.multiple_of(base * size, 128), size)

    c_lens = fetch(lens_ref, lens_buf, 14)
    c_q = fetch(q_ref.at[:, at_side(side, 4096)], q_buf, 0)
    c_k = fetch(k_ref.at[:, :, at_side(side, 256)], k_buf, 1)
    c_v = fetch(v_ref.at[:, :, at_side(side, 256)], v_buf, 2)
    w_own = wt_ref.at[:, at_side(side, 4096)]
    c_w = fetch(w_own, w_buf.at[ca], 3)
    c_ids = fetch(ids_ref, ids_buf, 10)
    c_route = fetch(route_ref, route_buf, 11)
    info[0, 0] = jnp.zeros((16, 128), F32)
    c_lens.wait()
    c_q.wait()
    c_k.wait()
    c_v.wait()
    group = HQ // KVH
    for kv in range(2):
        result = attend(q_buf, k_buf, v_buf, lens_buf, kv)
        for j in range(group):
            n = kv * group + j
            out, n = (g0, n) if n < HEADS0 else (g1, n - HEADS0)
            out[0, 0, :, n * HD:(n + 1) * HD] = result[j * S:(j + 1) * S, :]
    c_ids.wait()
    c_route.wait()
    info[0, 0, 0:8, 0:16] = ids_buf[...].astype(F32)
    info[0, 0, 8:16, 0:16] = route_buf[...]
    pl.semaphore_wait(barrier, 34)
    ring_w = Columns(links, side, ap, am, w_own, lambda source: w_buf.at[lax.rem(ca - source + 4, 4)])
    split = HEADS0 * HD
    ra = Gather(links, side, b_way, x_way, g0, False)
    rb = Gather(links, side, x_way, b_way, g1, False)
    ring_w.start()
    ra.start()
    rb.start()
    told = []
    for i in range(4):
        for j in range(4):
            if i or j:
                told.append(links.push(info.at[0, 0], info.at[j, i], side, moved(moved(g, cb, sb, i), cx, 1, j)))
    c_res = fetch(res_ref, res_buf, 12)
    c_gain = fetch(gain_ref, gain_buf, 13)
    c_ffn = []
    for h in range(2):
        depth = at_side(side if h == 0 else other, 2048)
        c_ffn.append(fetch(up_ref.at[depth, at_side(side, 384)], w_gu.at[h, :, 0:384], 4 + h))
        c_ffn.append(fetch(up_ref.at[depth, at_side(side + 2, 384)], w_gu.at[h, :, 384:768], 6 + h))
        c_ffn.append(fetch(down_ref.at[at_side(side if h == 0 else other, 384), at_side(side, 2048)], wd.at[h], 8 + h))
    ra.step1()
    rb.step1()
    ra.step2()
    rb.step2()
    ring_w.forward()
    ra.step3()
    rb.step3()
    ra.finish()
    rb.finish()
    c_w.wait()
    ring_w.finish()
    p0 = lax.dot_general(g0[...].reshape(256, split), w_buf[:, :, 0:split].reshape(256, split), NT,
                         preferred_element_type=F32)
    p1 = lax.dot_general(g1[...].reshape(256, 4096 - split), w_buf[:, :, split:4096].reshape(256, 4096 - split), NT,
                         preferred_element_type=F32)
    mine = cb * 4 + cx
    sent = []
    for n in sorted(range(16), key=lambda n: -((0, 1, 2, 1)[n // 4] + (0, 1, 2, 1)[n % 4])):
        bi, xi = n // 4, n % 4
        u = (xi * 4 + bi) * S
        block = (p0[u:u + S, :] + p1[n * S:(n + 1) * S, :]).astype(BF)
        o_st[n] = block
        if n == 0:
            r_buf[side, mine] = block
        to = moved(moved(g, cb, sb, -bi), cx, 1, -xi)
        for e in range(2):
            if n == 0 and e == 0:
                continue
            copy = pltpu.make_async_remote_copy(
                src_ref=o_st.at[n], dst_ref=r_buf.at[side, mine], send_sem=os.at[n, e], recv_sem=orv.at[side, mine],
                device_id=(side if e == 0 else other, to), device_id_type=MESH)
            copy.start()
            sent.append(copy)

    def arrived(source_side, n):
        pltpu.make_async_remote_copy(
            src_ref=o_st.at[0], dst_ref=r_buf.at[source_side, n], send_sem=os.at[0, 0], recv_sem=orv.at[source_side, n],
            device_id=(side, ap), device_id_type=MESH).wait_recv()

    for copy in told:
        copy.wait_recv()
    experts = [moved(g, ca, sa, i) for i in range(4)]
    pick, weigh = routing(info, experts)
    for i in range(4):
        for j in range(4):
            if i or j:
                arrived(side, lax.rem(cb + i, 4) * 4 + lax.rem(cx + j, 4))
            arrived(other, lax.rem(ca + i, 4) * 4 + lax.rem(cx + j, 4))
    c_res.wait()
    c_gain.wait()
    squares = jnp.zeros((S, 128), F32)
    for y in range(4):
        for z in range(4):
            for m in range(2):
                pieces = []
                for x in (2 * m, 2 * m + 1):
                    pieces.append(r_buf[0, z * 4 + x, :, y * 64:(y + 1) * 64].astype(F32)
                                  + r_buf[1, y * 4 + x, :, z * 64:(z + 1) * 64].astype(F32))
                at = (y * 8 + z * 2 + m) * 128
                tile = res_buf[:, at:at + 128].astype(F32) + jnp.concatenate(pieces, axis=1)
                hid[:, at:at + 128] = tile
                squares = squares + tile * tile
    scaling = lax.rsqrt(jnp.sum(squares, axis=1, keepdims=True) * (1.0 / D) + 1e-06)

    half_at = pl.ds(pl.multiple_of(side * 2048, 128), 2048)
    na = Gather(links, side, b_way, x_way, n0, True)
    nb = Gather(links, side, x_way, b_way, n1, True)
    normed = (hid[:, half_at] * scaling * gain_buf[:, half_at]).astype(BF)
    n0[0, 0] = normed[:, 0:CUT]
    n1[0, 0] = normed[:, CUT:]
    nb.start()
    na.start()

    c_one, c_swap = {}, {}

    def dispatch(b):
        for at, tokens in ((slice(0, CUT), n0[:, b]), (slice(CUT, 2048), n1[b])):
            rows = jnp.dot(pick[b], tokens.reshape(64, -1), preferred_element_type=F32).astype(BF).reshape(4, S, -1)
            x_st[b, :, :, at] = rows[1:]
            x_own[SLOT[b], 0, :, at] = rows[0]
        c_one[b] = [links.push(x_st.at[b, a - 1], x_own.at[SLOT[b], SLOT[a]], side, a_way[(None, 0, 2, 1)[a]])
                    for a in (2, 1, 3)]

    def swap(b):
        for copy in c_one[b]:
            copy.wait_recv()
        c_swap[b] = links.push(x_own.at[SLOT[b]], x_far.at[SLOT[b]], other, g)

    def front(src, dst, h, low, high):
        rows = src[low:high].reshape((high - low) * 64, 2048)
        dst[low:high] = jnp.dot(rows, w_gu[h], preferred_element_type=F32).reshape(high - low, 4, S, 768)

    nb.step1()
    na.step1()
    nb.step2()
    na.step2()
    for b in (0, 1, 3, 2):
        for j in range(4):
            for ring, at in ((nb, (b, j)), (na, (j, b))):
                if at in ring.got:
                    ring.wait(*at)
        dispatch(b)
    for copy in c_ffn:
        copy.wait()
    swap(0)
    swap(1)
    front(x_own, h_own, 0, 0, 2)
    swap(3)
    swap(2)
    front(x_own, h_own, 0, 2, 4)
    for b in (0, 1, 3, 2):
        c_swap[b].wait_recv()
    front(x_far, h_far, 1, 0, 4)
    swaps = []
    for i in range(4):
        both = h_own[i] + h_far[:, i]
        gate, up = both[:, :, 0:384], both[:, :, 384:768]
        a_own[i] = (gate / (1.0 + jnp.exp(-gate)) * up).astype(BF)
        swaps.append(links.push(a_own.at[i], a_far.at[:, i], other, g))
    d_near[...] = jnp.dot(a_own[...].reshape(256, 384), wd[0], preferred_element_type=F32).reshape(4, 64, 2048)
    for copy in swaps:
        copy.wait_recv()
    c_back = {}
    for b in (2, 1, 3, 0):
        rows = d_near[SLOT[b]] + jnp.dot(a_far[SLOT[b]].reshape(64, 384), wd[1], preferred_element_type=F32)
        rows = rows.astype(BF).reshape(4, S, 2048)
        z_buf[b, 0] = rows[0]
        c_back[b] = []
        for a in (2, 1, 3):
            y_st[b, a - 1] = rows[SLOT[a]]
            c_back[b].append(links.push(y_st.at[b, a - 1], z_buf.at[b, a], side, a_way[(None, 1, 2, 0)[a]]))

    def mix(b):
        for copy in c_back[b]:
            copy.wait_recv()
        both = lax.dot_general(weigh[b], z_buf[b].reshape(64, 2048), (((0,), (0,)), ((), ())),
                               preferred_element_type=F32)
        m_buf[b] = (both[0:64, :] + both[64:128, :]).reshape(4, S, 2048)

    r0 = Scatter(links, side, b_way, x_way, lambda i, j: m_buf[j, i, :, 0:CUT], over0, near0)
    r1 = Scatter(links, side, x_way, b_way, lambda i, j: m_buf[i, j, :, CUT:2048], over1, near1)
    for b in (2, 1, 3, 0):
        mix(b)
        for i in (2, 1, 3):
            r0.along_q(i, b)
        if b:
            for j in (2, 1, 3, 0):
                r1.along_q(b, j)
    for j in (2, 1, 3, 0):
        r0.turn(j)
        r1.turn(j)
    at = pl.multiple_of(side * 2048, 128)
    out_ref[:, 0:CUT] = hid[:, pl.ds(at, CUT)] + r0.result()
    out_ref[:, CUT:2048] = hid[:, pl.ds(at + CUT, 2048 - CUT)] + r1.result()
    links.drain()
    for copy in sent:
        copy.wait_send()


def body(q, k, v, lens, out_weight, residual, norm_gain, expert_ids, route_weights, gate_up, down_weight):
    vm = pl.BlockSpec(memory_space=pltpu.VMEM)
    hb = pl.BlockSpec(memory_space=pltpu.HBM)
    dma = pltpu.SemaphoreType.DMA

    def vb(*shape):
        return pltpu.VMEM(shape, BF)

    def vf(*shape):
        return pltpu.VMEM(shape, F32)

    return pl.pallas_call(
        kernel,
        out_shape=jax.ShapeDtypeStruct((S, D // 2), F32),
        in_specs=[hb] * 11,
        out_specs=vm,
        scratch_shapes=[
            vb(S, 4096), vb(S, CTX, 256), vb(S, CTX, 256), vb(4, 64, 4096),
            vb(4, 4, S, HEADS0 * HD), vb(4, 4, S, 4096 - HEADS0 * HD),
            vb(16, S, 256), vb(2, 16, S, 256), vf(S, D), vf(4, 4, 16, 128), vb(4, 4, S, CUT), vb(4, 4, S, 2048 - CUT),
            vb(4, 3, S, 2048), vb(4, 4, S, 2048), vb(4, 4, S, 2048),
            vb(2, 2048, 768), vb(2, 384, 2048), vf(4, 4, S, 768), vf(4, 4, S, 768), vb(4, 4, S, 384), vb(4, 4, S, 384),
            vf(4, 64, 2048), vb(4, 3, S, 2048), vb(4, 4, S, 2048), vf(4, 4, S, 2048),
            vb(2, 3, 4, S, CUT), vb(2, 4, S, CUT), vb(2, 3, 4, S, 2048 - CUT), vb(2, 4, S, 2048 - CUT),
            vb(S, D), vf(1, D), pltpu.VMEM((8, S), jnp.int32), vf(8, S), pltpu.SMEM((S,), jnp.int32),
            dma((15,)), dma((180,)), dma((180,)), dma((16, 2)), dma((2, 16)),
        ],
        compiler_params=pltpu.CompilerParams(collective_id=0, has_side_effects=True, vmem_limit_bytes=46 << 20),
        name="decode_layer",
    )(*[pltpu.with_memory_space_constraint(value, pltpu.HBM) for value in (
        q, k, v, lens, out_weight.T, residual, norm_gain.reshape(1, -1), expert_ids.T, route_weights.T,
        gate_up[0], down_weight[0])]).astype(BF)


def solution(mesh):
    return jax.shard_map(
        body,
        mesh=mesh,
        in_specs=(
            P("grp", None), P("grp", None, None), P("grp", None, None), P("grp"), P(None, "grp"), P("grp", None), P(),
            P("grp", None), P("grp", None), P("grp", None, None), P("grp", None, None),
        ),
        out_specs=P("grp", "side"),
        check_vma=False,
    )
```

```python
import jax
import jax.numpy as jnp
from jax import lax
from jax.experimental import pallas as pl
from jax.experimental.pallas import tpu as pltpu
from jax.sharding import PartitionSpec as P

HQ = 64
KVH = 4
HD = 128
HID = 768
TOPK = 8
CTX = 128
D = 4096
S = 16
MESH = pl.DeviceIdType.MESH
BF = jnp.bfloat16
F32 = jnp.float32
NT = (((1,), (1,)), ((), ()))


def place():
    side = lax.axis_index("side")
    g = lax.axis_index("grp")
    sa = 16 - 12 * side
    sb = 4 + 12 * side
    ca = lax.rem(g // sa, 4)
    cb = lax.rem(g // sb, 4)
    cx = lax.rem(g, 4)
    return side, g, sa, sb, ca, cb, cx


def moved(g, c, stride, by):
    return g + (lax.rem(c + by + 4, 4) - c) * stride


def attend(q_buf, k_buf, v_buf, lens_ref, kv):
    lane = lax.broadcasted_iota(jnp.int32, (S, CTX), 1)
    row = lax.broadcasted_iota(jnp.int32, (S, CTX), 0)
    live = jnp.zeros((S, CTX), jnp.int32)
    for s in range(S):
        live = jnp.where(row == s, lens_ref[s], live)
    group = HQ // KVH
    live = jnp.concatenate([live] * group, axis=0)
    lane = jnp.concatenate([lane] * group, axis=0)
    row = jnp.concatenate([row] * group, axis=0)
    queries = jnp.concatenate(
        [q_buf[:, (kv * group + j) * HD:(kv * group + j + 1) * HD] for j in range(group)], axis=0)
    scores = jnp.zeros((S * group, CTX), F32)
    for s in range(S):
        part = lax.dot_general(queries, k_buf[s, :, kv * HD:(kv + 1) * HD], NT, preferred_element_type=F32)
        scores = jnp.where(row == s, part, scores)
    scores = jnp.where(lane < live, scores * HD ** (-0.5), -1e30)
    lifted = jnp.exp(scores - jnp.max(scores, axis=1, keepdims=True))
    weights = (lifted / jnp.sum(lifted, axis=1, keepdims=True))
    spread = jnp.concatenate([jnp.where(row == s, weights, 0.0).astype(BF) for s in range(S)], axis=1)
    values = v_buf[:, :, kv * HD:(kv + 1) * HD].reshape(S * CTX, HD)
    return jnp.dot(spread, values, preferred_element_type=F32).astype(BF)


class Links:
    def __init__(self, side, near, sends, recvs):
        self.side, self.near, self.sends, self.recvs = side, near, sends, recvs
        self.slots, self.count, self.live = 0, 0, [None] * POOL

    def slot(self):
        assert self.slots < self.recvs.shape[0]
        self.slots += 1
        return self.slots - 1

    def make(self, src, dst, send, recv, to_side, to):
        return pltpu.make_async_remote_copy(
            src_ref=src, dst_ref=dst, send_sem=self.sends.at[send], recv_sem=self.recvs.at[recv],
            device_id=(to_side, to), device_id_type=MESH)

    def push(self, src, dst, to_side, to, recv=None, send=None):
        if recv is None:
            recv = self.slot()
        pooled = send is None
        if pooled:
            send = self.count % POOL
            self.count += 1
            if self.live[send] is not None:
                self.live[send].wait_send()
        copy = self.make(src, dst, send, recv, to_side, to)
        if pooled:
            self.live[send] = copy
        copy.start()
        return copy

    def wait(self, view, recv):
        self.make(view, view, 0, recv, self.side, self.near).wait_recv()

    def sent(self, view, send):
        self.make(view, view, send, 0, self.side, self.near).wait_send()

    def drain(self):
        for copy in self.live:
            if copy is not None:
                copy.wait_send()


class Columns:
    def __init__(self, links, side, plus, minus, own, slot, whole):
        self.links, self.side, self.plus, self.minus, self.own, self.slot = links, side, plus, minus, own, slot
        self.whole, self.rest = whole, links.slot()

    def start(self):
        low, high = slice(0, 32), slice(32, 64)
        push, own, slot = self.links.push, self.own, self.slot(0)
        self.c0 = push(own.at[low], slot.at[low], self.side, self.plus)
        self.c1 = push(own.at[high], slot.at[high], self.side, self.minus)
        push(own.at[high], slot.at[high], self.side, self.plus, self.rest)
        push(own.at[low], slot.at[low], self.side, self.minus, self.rest)

    def forward(self):
        self.c0.wait_recv()
        at = self.slot(1).at[0:32]
        self.links.push(at, at, self.side, self.plus, self.rest)
        self.c1.wait_recv()
        at = self.slot(3).at[32:64]
        self.links.push(at, at, self.side, self.minus, self.rest)

    def finish(self):
        self.links.wait(self.whole.at[0:2], self.rest)


class Gather:
    def __init__(self, links, side, p, q, buf, direct, group):
        self.links, self.side, self.p, self.q, self.buf, self.direct, self.group = links, side, p, q, buf, direct, group
        self.got, self.sems = {}, {}

    def send(self, i, j, to, di, dj):
        at = (i + di) % 4, (j + dj) % 4
        key = self.group(*at)
        recv = None
        if key is not None:
            if key not in self.sems:
                self.sems[key] = self.links.slot()
            recv = self.sems[key]
        self.got[at] = self.links.push(self.buf.at[i, j], self.buf.at[at], self.side, to, recv)

    def wait(self, i, j):
        self.got[i, j].wait_recv()

    def wait_group(self, key, view):
        self.links.wait(view, self.sems[key])

    def along_q(self, j):
        self.send(0, j, self.q[0], 1, 0)
        self.send(0, j, self.q[1], 3, 0)
        if self.direct:
            self.send(0, j, self.q[2], 2, 0)

    def start(self):
        self.send(0, 0, self.p[0], 0, 1)
        self.send(0, 0, self.p[1], 0, 3)
        self.send(0, 0, self.p[2], 0, 2)
        self.along_q(0)

    def step1(self):
        self.wait(0, 1)
        self.along_q(1)
        self.wait(0, 3)
        self.along_q(3)
        if not self.direct:
            self.wait(1, 0)
            self.send(1, 0, self.q[0], 1, 0)

    def step2(self):
        self.wait(0, 2)
        self.along_q(2)

    def step3(self):
        self.wait(1, 1)
        self.send(1, 1, self.q[0], 1, 0)
        self.wait(3, 3)
        self.send(3, 3, self.q[1], 3, 0)
        self.wait(3, 2)
        self.send(3, 2, self.q[1], 3, 0)


def relayed(i, j):
    return None if i == 0 or (i, j) in ((1, 0), (1, 1), (3, 3), (3, 2)) else 0


class Scatter:
    def __init__(self, links, side, p, q, block, over, near):
        self.links, self.side, self.p, self.q, self.block = links, side, p, q, block
        self.over, self.near = over, near
        self.s_over, self.s_near = [links.slot() for _ in range(4)], links.slot()

    def along_q(self, i, j):
        self.over[0, i - 1, j] = self.block(i, j).astype(BF)
        self.links.push(self.over.at[0, i - 1, j], self.over.at[1, i - 1, j], self.side, self.q[(None, 1, 2, 0)[i]],
                        self.s_over[j])

    def turn(self, j):
        self.links.wait(self.over.at[1, :, j], self.s_over[j])
        block = self.block(0, j)
        for i in (2, 1, 3):
            block = block + self.over[1, i - 1, j].astype(F32)
        if j == 0:
            self.own = block
        else:
            self.near[0, j] = block.astype(BF)
            self.links.push(self.near.at[0, j], self.near.at[1, j], self.side, self.p[(None, 1, 2, 0)[j]], self.s_near)

    def result(self):
        self.links.wait(self.near.at[1, 1:4], self.s_near)
        block = self.own
        for j in (1, 3, 2):
            block = block + self.near[1, j].astype(F32)
        return block


def routing(info, experts):
    lane = lax.broadcasted_iota(jnp.int32, (16, 128), 1)
    tiles = []
    for t in range(2):
        tile = jnp.zeros((16, 128), F32)
        for i in range(8):
            b, x = divmod(t * 8 + i, 4)
            block = info[x * 4 + b]
            moved_block = pltpu.roll(block, 16 * i, 1) if i else block
            tile = jnp.where(lane // 16 == i, moved_block, tile)
        tiles.append(tile)
    table = jnp.concatenate(tiles, axis=1)
    ids, route = table[0:8, :], table[8:16, :]
    first = lax.broadcasted_iota(jnp.int32, (256, 256), 0)
    later = lax.broadcasted_iota(jnp.int32, (256, 256), 1)
    before = jnp.where((first // 16 == later // 16) & (first < later), 1.0, 0.0).astype(BF)
    token = lax.broadcasted_iota(jnp.int32, (8, 256), 1) // 16
    named, weight = [], []
    for e in experts:
        hit = ids == e.astype(F32)
        named.append(jnp.sum(jnp.where(hit, 1.0, 0.0), axis=0, keepdims=True))
        weight.append(jnp.sum(jnp.where(hit, route, 0.0), axis=0, keepdims=True))
    named8 = jnp.concatenate(named + [jnp.zeros((4, 256), F32)], axis=0)
    rank = jnp.dot(named8.astype(BF), before, preferred_element_type=F32)
    spot = jnp.where(named8 > 0.5, (token % 4).astype(F32) * 4.0 + rank, -1.0)
    rows = lax.broadcasted_iota(jnp.int32, (16, 256), 0).astype(F32)
    picks, weighted = [], []
    for i in range(4):
        hit = rows == spot[i:i + 1, :]
        picks.append(jnp.where(hit, 1.0, 0.0))
        weighted.append(jnp.where(hit, weight[i], 0.0))
    picks, weighted = jnp.concatenate(picks, axis=0), jnp.concatenate(weighted, axis=0)
    pick, weigh = [], []
    for b in range(4):
        at = slice(64 * b, 64 * b + 64)
        pick.append(picks[:, at].astype(BF))
        high = weighted[:, at].astype(BF)
        weigh.append(jnp.concatenate([high, (weighted[:, at] - high.astype(F32)).astype(BF)], axis=1))
    return pick, weigh


SLOT = (0, 1, 3, 2)
HEADS0 = 20
POOL = 40
CUT = 1280


def kernel(q_ref, k_ref, v_ref, lens_ref, wt_ref, res_ref, gain_ref, ids_ref, route_ref, up_ref, down_ref, out_ref,
           q_buf, k_buf, v_buf, w_buf, g0, g1, o_st, r_buf, hid, info, n0, n1, x_st, x_own, x_far,
           w_gu, wd, h_own, h_far, a_own, a_far, d_near, y_st, z_buf, m_buf, over0, near0, over1, near1,
           res_buf, gain_buf, ids_buf, route_buf, lens_buf, loc, sends, recvs):
    side, g, sa, sb, ca, cb, cx = place()
    other = 1 - side
    a_way = [moved(g, ca, sa, i) for i in (1, -1, 2)]
    ap, am = a_way[0], a_way[1]
    b_way = [moved(g, cb, sb, i) for i in (1, -1, 2)]
    x_way = [moved(g, cx, 1, i) for i in (1, -1, 2)]
    links = Links(side, ap, sends, recvs)
    barrier = pltpu.get_barrier_semaphore()

    def hello(to_side, to):
        pl.semaphore_signal(barrier, inc=1, device_id=(to_side, to), device_id_type=MESH)

    for to in a_way:
        hello(side, to)
    for i in range(4):
        for j in range(4):
            if i or j:
                hello(side, moved(moved(g, cb, sb, i), cx, 1, j))
            hello(other, moved(moved(g, ca, sa, i), cx, 1, j))

    def fetch(src, dst, i):
        copy = pltpu.make_async_copy(src, dst, loc.at[i])
        copy.start()
        return copy

    def at_side(base, size):
        return pl.ds(pl.multiple_of(base * size, 128), size)

    c_lens = fetch(lens_ref, lens_buf, 14)
    c_q = fetch(q_ref.at[:, at_side(side, 4096)], q_buf, 0)
    c_k = fetch(k_ref.at[:, :, at_side(side, 256)], k_buf, 1)
    c_v = fetch(v_ref.at[:, :, at_side(side, 256)], v_buf, 2)
    w_own = wt_ref.at[:, at_side(side, 4096)]
    c_w = fetch(w_own, w_buf.at[ca], 3)
    c_ids = fetch(ids_ref, ids_buf, 10)
    c_route = fetch(route_ref, route_buf, 11)
    info[0] = jnp.zeros((16, 128), F32)
    c_lens.wait()
    c_q.wait()
    c_k.wait()
    c_v.wait()
    group = HQ // KVH
    for kv in range(2):
        result = attend(q_buf, k_buf, v_buf, lens_buf, kv)
        for j in range(group):
            n = kv * group + j
            out, n = (g0, n) if n < HEADS0 else (g1, n - HEADS0)
            out[0, 0, :, n * HD:(n + 1) * HD] = result[j * S:(j + 1) * S, :]
    c_ids.wait()
    c_route.wait()
    info[0, 0:8, 0:16] = ids_buf[...].astype(F32)
    info[0, 8:16, 0:16] = route_buf[...]
    pl.semaphore_wait(barrier, 34)
    ring_w = Columns(links, side, ap, am, w_own, lambda source: w_buf.at[lax.rem(ca - source + 4, 4)], w_buf)
    split = HEADS0 * HD
    ra = Gather(links, side, b_way, x_way, g0, False, relayed)
    rb = Gather(links, side, x_way, b_way, g1, False, relayed)
    ring_w.start()
    ra.start()
    rb.start()
    told = links.slot()
    for i in range(4):
        for j in range(4):
            if i or j:
                links.push(info.at[0], info.at[j * 4 + i], side, moved(moved(g, cb, sb, i), cx, 1, j), told, POOL)
    c_res = fetch(res_ref, res_buf, 12)
    c_gain = fetch(gain_ref, gain_buf, 13)
    c_ffn = []
    for h in range(2):
        depth = at_side(side if h == 0 else other, 2048)
        c_ffn.append(fetch(up_ref.at[depth, at_side(side, 384)], w_gu.at[h, :, 0:384], 4 + h))
        c_ffn.append(fetch(up_ref.at[depth, at_side(side + 2, 384)], w_gu.at[h, :, 384:768], 6 + h))
        c_ffn.append(fetch(down_ref.at[at_side(side if h == 0 else other, 384), at_side(side, 2048)], wd.at[h], 8 + h))
    ra.step1()
    rb.step1()
    ra.step2()
    rb.step2()
    ring_w.forward()
    ra.step3()
    rb.step3()
    ra.wait_group(0, g0.at[2:4])
    rb.wait_group(0, g1.at[2:4])
    c_w.wait()
    ring_w.finish()
    p0 = lax.dot_general(g0[...].reshape(256, split), w_buf[:, :, 0:split].reshape(256, split), NT,
                         preferred_element_type=F32)
    p1 = lax.dot_general(g1[...].reshape(256, 4096 - split), w_buf[:, :, split:4096].reshape(256, 4096 - split), NT,
                         preferred_element_type=F32)
    mine = side * 16 + cb * 4 + cx
    columns_in = links.slot()
    for n in sorted(range(16), key=lambda n: -((0, 1, 2, 1)[n // 4] + (0, 1, 2, 1)[n % 4])):
        bi, xi = n // 4, n % 4
        u = (xi * 4 + bi) * S
        block = (p0[u:u + S, :] + p1[n * S:(n + 1) * S, :]).astype(BF)
        o_st[n] = block
        if n == 0:
            r_buf[mine] = block
        to = moved(moved(g, cb, sb, -bi), cx, 1, -xi)
        for e in range(2):
            if n == 0 and e == 0:
                continue
            links.push(o_st.at[n], r_buf.at[mine], side if e == 0 else other, to, columns_in, POOL + 1)

    links.wait(info.at[1:16], told)
    experts = [moved(g, ca, sa, i) for i in range(4)]
    pick, weigh = routing(info, experts)
    links.wait(r_buf.at[0:31], columns_in)
    c_res.wait()
    c_gain.wait()
    squares = jnp.zeros((S, 128), F32)
    for y in range(4):
        for z in range(4):
            for m in range(2):
                pieces = []
                for x in (2 * m, 2 * m + 1):
                    pieces.append(r_buf[z * 4 + x, :, y * 64:(y + 1) * 64].astype(F32)
                                  + r_buf[16 + y * 4 + x, :, z * 64:(z + 1) * 64].astype(F32))
                at = (y * 8 + z * 2 + m) * 128
                tile = res_buf[:, at:at + 128].astype(F32) + jnp.concatenate(pieces, axis=1)
                hid[:, at:at + 128] = tile
                squares = squares + tile * tile
    scaling = lax.rsqrt(jnp.sum(squares, axis=1, keepdims=True) * (1.0 / D) + 1e-06)

    half_at = pl.ds(pl.multiple_of(side * 2048, 128), 2048)
    na = Gather(links, side, b_way, x_way, n0, True, lambda i, j: j if i else None)
    nb = Gather(links, side, x_way, b_way, n1, True, lambda i, j: i if i else None)
    normed = (hid[:, half_at] * scaling * gain_buf[:, half_at]).astype(BF)
    n0[0, 0] = normed[:, 0:CUT]
    n1[0, 0] = normed[:, CUT:]
    nb.start()
    na.start()

    s_one, s_swap = [links.slot() for _ in range(4)], links.slot()

    def dispatch(b):
        for at, tokens in ((slice(0, CUT), n0[:, b]), (slice(CUT, 2048), n1[b])):
            rows = jnp.dot(pick[b], tokens.reshape(64, -1), preferred_element_type=F32).astype(BF).reshape(4, S, -1)
            x_st[b, :, :, at] = rows[1:]
            x_own[SLOT[b], 0, :, at] = rows[0]
        for a in (2, 1, 3):
            links.push(x_st.at[b, a - 1], x_own.at[SLOT[b], SLOT[a]], side, a_way[(None, 0, 2, 1)[a]], s_one[b])

    def swap(b):
        links.wait(x_own.at[SLOT[b], 1:4], s_one[b])
        links.push(x_own.at[SLOT[b]], x_far.at[SLOT[b]], other, g, s_swap)

    def front(src, dst, h, low, high):
        rows = src[low:high].reshape((high - low) * 64, 2048)
        dst[low:high] = jnp.dot(rows, w_gu[h], preferred_element_type=F32).reshape(high - low, 4, S, 768)

    nb.step1()
    na.step1()
    nb.step2()
    na.step2()
    for b in (0, 1, 3, 2):
        if b:
            nb.wait_group(b, n1.at[b])
        na.wait_group(b, n0.at[1:4, b])
        dispatch(b)
    for copy in c_ffn:
        copy.wait()
    swap(0)
    swap(1)
    front(x_own, h_own, 0, 0, 2)
    swap(3)
    swap(2)
    front(x_own, h_own, 0, 2, 4)
    links.wait(x_far, s_swap)
    front(x_far, h_far, 1, 0, 4)
    s_act = links.slot()
    for i in range(4):
        both = h_own[i] + h_far[:, i]
        gate, up = both[:, :, 0:384], both[:, :, 384:768]
        a_own[i] = (gate / (1.0 + jnp.exp(-gate)) * up).astype(BF)
        links.push(a_own.at[i], a_far.at[:, i], other, g, s_act)
    d_near[...] = jnp.dot(a_own[...].reshape(256, 384), wd[0], preferred_element_type=F32).reshape(4, 64, 2048)
    links.wait(a_far, s_act)
    s_back = [links.slot() for _ in range(4)]
    for b in (2, 1, 3, 0):
        rows = d_near[SLOT[b]] + jnp.dot(a_far[SLOT[b]].reshape(64, 384), wd[1], preferred_element_type=F32)
        rows = rows.astype(BF).reshape(4, S, 2048)
        z_buf[b, 0] = rows[0]
        for a in (2, 1, 3):
            y_st[b, a - 1] = rows[SLOT[a]]
            links.push(y_st.at[b, a - 1], z_buf.at[b, a], side, a_way[(None, 1, 2, 0)[a]], s_back[b])

    def mix(b):
        links.wait(z_buf.at[b, 1:4], s_back[b])
        both = lax.dot_general(weigh[b], z_buf[b].reshape(64, 2048), (((0,), (0,)), ((), ())),
                               preferred_element_type=F32)
        m_buf[b] = (both[0:64, :] + both[64:128, :]).reshape(4, S, 2048)

    r0 = Scatter(links, side, b_way, x_way, lambda i, j: m_buf[j, i, :, 0:CUT], over0, near0)
    r1 = Scatter(links, side, x_way, b_way, lambda i, j: m_buf[i, j, :, CUT:2048], over1, near1)
    for b in (2, 1, 3, 0):
        mix(b)
        for i in (2, 1, 3):
            r0.along_q(i, b)
        if b:
            for j in (2, 1, 3, 0):
                r1.along_q(b, j)
    for j in (2, 1, 3, 0):
        r0.turn(j)
        r1.turn(j)
    at = pl.multiple_of(side * 2048, 128)
    out_ref[:, 0:CUT] = hid[:, pl.ds(at, CUT)] + r0.result()
    out_ref[:, CUT:2048] = hid[:, pl.ds(at + CUT, 2048 - CUT)] + r1.result()
    links.sent(info.at[1:16], POOL)
    links.sent(r_buf.at[0:31], POOL + 1)
    links.drain()


def body(q, k, v, lens, out_weight, residual, norm_gain, expert_ids, route_weights, gate_up, down_weight):
    vm = pl.BlockSpec(memory_space=pltpu.VMEM)
    hb = pl.BlockSpec(memory_space=pltpu.HBM)
    dma = pltpu.SemaphoreType.DMA

    def vb(*shape):
        return pltpu.VMEM(shape, BF)

    def vf(*shape):
        return pltpu.VMEM(shape, F32)

    return pl.pallas_call(
        kernel,
        out_shape=jax.ShapeDtypeStruct((S, D // 2), F32),
        in_specs=[hb] * 11,
        out_specs=vm,
        scratch_shapes=[
            vb(S, 4096), vb(S, CTX, 256), vb(S, CTX, 256), vb(4, 64, 4096),
            vb(4, 4, S, HEADS0 * HD), vb(4, 4, S, 4096 - HEADS0 * HD),
            vb(16, S, 256), vb(32, S, 256), vf(S, D), vf(16, 16, 128), vb(4, 4, S, CUT), vb(4, 4, S, 2048 - CUT),
            vb(4, 3, S, 2048), vb(4, 4, S, 2048), vb(4, 4, S, 2048),
            vb(2, 2048, 768), vb(2, 384, 2048), vf(4, 4, S, 768), vf(4, 4, S, 768), vb(4, 4, S, 384), vb(4, 4, S, 384),
            vf(4, 64, 2048), vb(4, 3, S, 2048), vb(4, 4, S, 2048), vf(4, 4, S, 2048),
            vb(2, 3, 4, S, CUT), vb(2, 4, S, CUT), vb(2, 3, 4, S, 2048 - CUT), vb(2, 4, S, 2048 - CUT),
            vb(S, D), vf(1, D), pltpu.VMEM((8, S), jnp.int32), vf(8, S), pltpu.SMEM((S,), jnp.int32),
            dma((15,)), dma((POOL + 2,)), dma((54,)),
        ],
        compiler_params=pltpu.CompilerParams(collective_id=0, has_side_effects=True, vmem_limit_bytes=46 << 20),
        name="decode_layer",
    )(*[pltpu.with_memory_space_constraint(value, pltpu.HBM) for value in (
        q, k, v, lens, out_weight.T, residual, norm_gain.reshape(1, -1), expert_ids.T, route_weights.T,
        gate_up[0], down_weight[0])]).astype(BF)


def solution(mesh):
    return jax.shard_map(
        body,
        mesh=mesh,
        in_specs=(
            P("grp", None), P("grp", None, None), P("grp", None, None), P("grp"), P(None, "grp"), P("grp", None), P(),
            P("grp", None), P("grp", None), P("grp", None, None), P("grp", None, None),
        ),
        out_specs=P("grp", "side"),
        check_vma=False,
    )
```

```python
import jax
import jax.numpy as jnp
from jax import lax
from jax.experimental import pallas as pl
from jax.experimental.pallas import tpu as pltpu
from jax.sharding import PartitionSpec as P

HQ = 64
KVH = 4
HD = 128
HID = 768
TOPK = 8
CTX = 128
D = 4096
S = 16
MESH = pl.DeviceIdType.MESH
BF = jnp.bfloat16
F32 = jnp.float32
NT = (((1,), (1,)), ((), ()))


def place():
    side = lax.axis_index("side")
    g = lax.axis_index("grp")
    sa = 16 - 12 * side
    sb = 4 + 12 * side
    ca = lax.rem(g // sa, 4)
    cb = lax.rem(g // sb, 4)
    cx = lax.rem(g, 4)
    return side, g, sa, sb, ca, cb, cx


def moved(g, c, stride, by):
    return g + (lax.rem(c + by + 4, 4) - c) * stride


def attend(q_buf, k_buf, lens_ref, kv):
    lane = lax.broadcasted_iota(jnp.int32, (S, CTX), 1)
    row = lax.broadcasted_iota(jnp.int32, (S, CTX), 0)
    live = jnp.zeros((S, CTX), jnp.int32)
    for s in range(S):
        live = jnp.where(row == s, lens_ref[s], live)
    group = HQ // KVH
    live = jnp.concatenate([live] * group, axis=0)
    lane = jnp.concatenate([lane] * group, axis=0)
    row = jnp.concatenate([row] * group, axis=0)
    queries = jnp.concatenate(
        [q_buf[:, (kv * group + j) * HD:(kv * group + j + 1) * HD] for j in range(group)], axis=0)
    scores = jnp.zeros((S * group, CTX), F32)
    for s in range(S):
        part = lax.dot_general(queries, k_buf[s], NT, preferred_element_type=F32)
        scores = jnp.where(row == s, part, scores)
    scores = jnp.where(lane < live, scores * HD ** (-0.5), -1e30)
    lifted = jnp.exp(scores - jnp.max(scores, axis=1, keepdims=True))
    weights = (lifted / jnp.sum(lifted, axis=1, keepdims=True))
    return jnp.concatenate([jnp.where(row == s, weights, 0.0).astype(BF) for s in range(S)], axis=1)


class Links:
    def __init__(self, side, near, sends, recvs):
        self.side, self.near, self.sends, self.recvs = side, near, sends, recvs
        self.slots, self.count, self.live = 0, 0, [None] * POOL

    def slot(self):
        assert self.slots < self.recvs.shape[0]
        self.slots += 1
        return self.slots - 1

    def make(self, src, dst, send, recv, to_side, to):
        return pltpu.make_async_remote_copy(
            src_ref=src, dst_ref=dst, send_sem=self.sends.at[send], recv_sem=self.recvs.at[recv],
            device_id=(to_side, to), device_id_type=MESH)

    def push(self, src, dst, to_side, to, recv=None, send=None):
        if recv is None:
            recv = self.slot()
        pooled = send is None
        if pooled:
            send = self.count % POOL
            self.count += 1
            if self.live[send] is not None:
                self.live[send].wait_send()
        copy = self.make(src, dst, send, recv, to_side, to)
        if pooled:
            self.live[send] = copy
        copy.start()
        return copy

    def wait(self, view, recv):
        self.make(view, view, 0, recv, self.side, self.near).wait_recv()

    def sent(self, view, send):
        self.make(view, view, send, 0, self.side, self.near).wait_send()

    def drain(self):
        for copy in self.live:
            if copy is not None:
                copy.wait_send()


class Columns:
    def __init__(self, links, side, plus, minus, own, slot, whole):
        self.links, self.side, self.plus, self.minus, self.own, self.slot = links, side, plus, minus, own, slot
        self.whole, self.rest = whole, links.slot()

    def start(self):
        push, own, slot = self.links.push, self.own, self.slot(0)
        self.up, self.down = [], []
        for k in range(2):
            up, down = slice(16 * k, 16 * k + 16), slice(32 + 16 * k, 48 + 16 * k)
            self.up.append(push(own.at[up], slot.at[up], self.side, self.plus))
            self.down.append(push(own.at[down], slot.at[down], self.side, self.minus))
        low, high = slice(0, 32), slice(32, 64)
        push(own.at[high], slot.at[high], self.side, self.plus, self.rest)
        push(own.at[low], slot.at[low], self.side, self.minus, self.rest)

    def forward(self, k):
        self.up[k].wait_recv()
        at = self.slot(1).at[16 * k:16 * k + 16]
        self.links.push(at, at, self.side, self.plus, self.rest)
        self.down[k].wait_recv()
        at = self.slot(3).at[32 + 16 * k:48 + 16 * k]
        self.links.push(at, at, self.side, self.minus, self.rest)

    def finish(self):
        self.links.wait(self.whole.at[0:2], self.rest)


class Gather:
    def __init__(self, links, side, p, q, buf, direct, group):
        self.links, self.side, self.p, self.q, self.buf, self.direct, self.group = links, side, p, q, buf, direct, group
        self.got, self.sems = {}, {}

    def send(self, i, j, to, di, dj):
        at = (i + di) % 4, (j + dj) % 4
        key = self.group(*at)
        recv = None
        if key is not None:
            if key not in self.sems:
                self.sems[key] = self.links.slot()
            recv = self.sems[key]
        self.got[at] = self.links.push(self.buf.at[i, j], self.buf.at[at], self.side, to, recv)

    def wait(self, i, j):
        self.got[i, j].wait_recv()

    def wait_group(self, key, view):
        self.links.wait(view, self.sems[key])

    def along_q(self, j):
        self.send(0, j, self.q[0], 1, 0)
        self.send(0, j, self.q[1], 3, 0)
        if self.direct:
            self.send(0, j, self.q[2], 2, 0)

    def start(self):
        self.send(0, 0, self.p[0], 0, 1)
        self.send(0, 0, self.p[1], 0, 3)
        self.send(0, 0, self.p[2], 0, 2)
        self.along_q(0)

    def step1(self):
        self.wait(0, 1)
        self.along_q(1)
        self.wait(0, 3)
        self.along_q(3)
        if not self.direct:
            self.wait(1, 0)
            self.send(1, 0, self.q[0], 1, 0)

    def step2(self):
        self.wait(0, 2)
        self.along_q(2)

    def step3(self):
        self.wait(1, 1)
        self.send(1, 1, self.q[0], 1, 0)
        self.wait(3, 3)
        self.send(3, 3, self.q[1], 3, 0)
        self.wait(3, 2)
        self.send(3, 2, self.q[1], 3, 0)


def relayed(i, j):
    return None if i == 0 or (i, j) in ((1, 0), (1, 1), (3, 3), (3, 2)) else 0


class Scatter:
    def __init__(self, links, side, p, q, block, over, near):
        self.links, self.side, self.p, self.q, self.block = links, side, p, q, block
        self.over, self.near = over, near
        self.s_over, self.s_near = [links.slot() for _ in range(4)], links.slot()

    def along_q(self, i, j):
        self.over[0, i - 1, j] = self.block(i, j).astype(BF)
        self.links.push(self.over.at[0, i - 1, j], self.over.at[1, i - 1, j], self.side, self.q[(None, 1, 2, 0)[i]],
                        self.s_over[j])

    def turn(self, j):
        self.links.wait(self.over.at[1, :, j], self.s_over[j])
        block = self.block(0, j)
        for i in (2, 1, 3):
            block = block + self.over[1, i - 1, j].astype(F32)
        if j == 0:
            self.own = block
        else:
            self.near[0, j] = block.astype(BF)
            self.links.push(self.near.at[0, j], self.near.at[1, j], self.side, self.p[(None, 1, 2, 0)[j]], self.s_near)

    def result(self):
        self.links.wait(self.near.at[1, 1:4], self.s_near)
        block = self.own
        for j in (1, 3, 2):
            block = block + self.near[1, j].astype(F32)
        return block


def routing(info, experts):
    lane = lax.broadcasted_iota(jnp.int32, (16, 128), 1)
    tiles = []
    for t in range(2):
        tile = jnp.zeros((16, 128), F32)
        for i in range(8):
            b, x = divmod(t * 8 + i, 4)
            block = info[x * 4 + b]
            moved_block = pltpu.roll(block, 16 * i, 1) if i else block
            tile = jnp.where(lane // 16 == i, moved_block, tile)
        tiles.append(tile)
    table = jnp.concatenate(tiles, axis=1)
    ids, route = table[0:8, :], table[8:16, :]
    first = lax.broadcasted_iota(jnp.int32, (256, 256), 0)
    later = lax.broadcasted_iota(jnp.int32, (256, 256), 1)
    before = jnp.where((first // 16 == later // 16) & (first < later), 1.0, 0.0).astype(BF)
    token = lax.broadcasted_iota(jnp.int32, (8, 256), 1) // 16
    named, weight = [], []
    for e in experts:
        hit = ids == e.astype(F32)
        named.append(jnp.sum(jnp.where(hit, 1.0, 0.0), axis=0, keepdims=True))
        weight.append(jnp.sum(jnp.where(hit, route, 0.0), axis=0, keepdims=True))
    named8 = jnp.concatenate(named + [jnp.zeros((4, 256), F32)], axis=0)
    rank = jnp.dot(named8.astype(BF), before, preferred_element_type=F32)
    spot = jnp.where(named8 > 0.5, (token % 4).astype(F32) * 4.0 + rank, -1.0)
    rows = lax.broadcasted_iota(jnp.int32, (16, 256), 0).astype(F32)
    picks, weighted = [], []
    for i in range(4):
        hit = rows == spot[i:i + 1, :]
        picks.append(jnp.where(hit, 1.0, 0.0))
        weighted.append(jnp.where(hit, weight[i], 0.0))
    picks, weighted = jnp.concatenate(picks, axis=0), jnp.concatenate(weighted, axis=0)
    pick, weigh = [], []
    for b in range(4):
        at = slice(64 * b, 64 * b + 64)
        pick.append(picks[:, at].astype(BF))
        high = weighted[:, at].astype(BF)
        weigh.append(jnp.concatenate([high, (weighted[:, at] - high.astype(F32)).astype(BF)], axis=1))
    return pick, weigh


SLOT = (0, 1, 3, 2)
HEADS0 = 22
POOL = 40
CUT = 1280
CUTR = 1280


def kernel(q_ref, k_ref, v_ref, lens_ref, wt_ref, res_ref, gain_ref, ids_ref, route_ref, up_ref, down_ref, out_ref,
           q_buf, k_buf, v_buf, w_buf, g0, g1, o_st, r_buf, hid, info, n0, n1, x_st, x_own, x_far,
           w_gu, wd, h_own, h_far, a_own, a_far, d_near, y_st, z_buf, m_buf, over0, near0, over1, near1,
           res_buf, gain_buf, ids_buf, route_buf, lens_buf, loc, sends, recvs):
    side, g, sa, sb, ca, cb, cx = place()
    other = 1 - side
    a_way = [moved(g, ca, sa, i) for i in (1, -1, 2)]
    ap, am = a_way[0], a_way[1]
    b_way = [moved(g, cb, sb, i) for i in (1, -1, 2)]
    x_way = [moved(g, cx, 1, i) for i in (1, -1, 2)]
    links = Links(side, ap, sends, recvs)
    barrier = pltpu.get_barrier_semaphore()

    def hello(to_side, to):
        pl.semaphore_signal(barrier, inc=1, device_id=(to_side, to), device_id_type=MESH)

    for to in a_way:
        hello(side, to)
    for i in range(4):
        for j in range(4):
            if i or j:
                hello(side, moved(moved(g, cb, sb, i), cx, 1, j))
            hello(other, moved(moved(g, ca, sa, i), cx, 1, j))

    def fetch(src, dst, i):
        copy = pltpu.make_async_copy(src, dst, loc.at[i])
        copy.start()
        return copy

    def at_side(base, size):
        return pl.ds(pl.multiple_of(base * size, 128), size)

    c_lens = fetch(lens_ref, lens_buf, 14)
    c_q = fetch(q_ref.at[:, at_side(side, 4096)], q_buf, 0)
    c_k = [fetch(k_ref.at[:, :, at_side(2 * side + i, 128)], k_buf.at[i], (1, 15)[i]) for i in range(2)]
    c_v = [fetch(v_ref.at[:, :, at_side(2 * side + i, 128)], v_buf.at[i], (2, 16)[i]) for i in range(2)]
    w_own = wt_ref.at[:, at_side(side, 4096)]
    c_w = fetch(w_own, w_buf.at[ca], 3)
    c_ids = fetch(ids_ref, ids_buf, 10)
    c_route = fetch(route_ref, route_buf, 11)
    info[0] = jnp.zeros((16, 128), F32)
    c_lens.wait()
    c_q.wait()
    spread = []
    for kv in range(2):
        c_k[kv].wait()
        spread.append(attend(q_buf, k_buf.at[kv], lens_buf, kv))
    group = HQ // KVH
    for kv in range(2):
        c_v[kv].wait()
        result = jnp.dot(spread[kv], v_buf[kv].reshape(S * CTX, HD), preferred_element_type=F32).astype(BF)
        for j in range(group):
            n = kv * group + j
            out, n = (g0, n) if n < HEADS0 else (g1, n - HEADS0)
            out[0, 0, :, n * HD:(n + 1) * HD] = result[j * S:(j + 1) * S, :]
    c_ids.wait()
    c_route.wait()
    info[0, 0:8, 0:16] = ids_buf[...].astype(F32)
    info[0, 8:16, 0:16] = route_buf[...]
    pl.semaphore_wait(barrier, 34)
    ring_w = Columns(links, side, ap, am, w_own, lambda source: w_buf.at[lax.rem(ca - source + 4, 4)], w_buf)
    split = HEADS0 * HD
    ra = Gather(links, side, b_way, x_way, g0, False, relayed)
    rb = Gather(links, side, x_way, b_way, g1, False, relayed)
    ring_w.start()
    ra.start()
    rb.start()
    told = links.slot()
    for i in range(4):
        for j in range(4):
            if i or j:
                links.push(info.at[0], info.at[j * 4 + i], side, moved(moved(g, cb, sb, i), cx, 1, j), told, POOL)
    c_res = fetch(res_ref, res_buf, 12)
    c_gain = fetch(gain_ref, gain_buf, 13)
    c_ffn = []
    for h in range(2):
        depth = at_side(side if h == 0 else other, 2048)
        c_ffn.append(fetch(up_ref.at[depth, at_side(side, 384)], w_gu.at[h, :, 0:384], 4 + h))
        c_ffn.append(fetch(up_ref.at[depth, at_side(side + 2, 384)], w_gu.at[h, :, 384:768], 6 + h))
        c_ffn.append(fetch(down_ref.at[at_side(side if h == 0 else other, 384), at_side(side, 2048)], wd.at[h], 8 + h))
    ra.step1()
    rb.step1()
    ra.step2()
    rb.step2()
    ring_w.forward(0)
    ring_w.forward(1)
    ra.step3()
    rb.step3()
    ra.wait_group(0, g0.at[2:4])
    rb.wait_group(0, g1.at[2:4])
    c_w.wait()
    ring_w.finish()
    p0 = lax.dot_general(g0[...].reshape(256, split), w_buf[:, :, 0:split].reshape(256, split), NT,
                         preferred_element_type=F32)
    p1 = lax.dot_general(g1[...].reshape(256, 4096 - split), w_buf[:, :, split:4096].reshape(256, 4096 - split), NT,
                         preferred_element_type=F32)
    mine = side * 16 + cb * 4 + cx
    columns_in = links.slot()
    for n in sorted(range(16), key=lambda n: -((0, 1, 2, 1)[n // 4] + (0, 1, 2, 1)[n % 4])):
        bi, xi = n // 4, n % 4
        u = (xi * 4 + bi) * S
        block = (p0[u:u + S, :] + p1[n * S:(n + 1) * S, :]).astype(BF)
        o_st[n] = block
        if n == 0:
            r_buf[mine] = block
        to = moved(moved(g, cb, sb, -bi), cx, 1, -xi)
        for e in range(2):
            if n == 0 and e == 0:
                continue
            links.push(o_st.at[n], r_buf.at[mine], side if e == 0 else other, to, columns_in, POOL + 1)

    links.wait(info.at[1:16], told)
    experts = [moved(g, ca, sa, i) for i in range(4)]
    pick, weigh = routing(info, experts)
    links.wait(r_buf.at[0:31], columns_in)
    c_res.wait()
    c_gain.wait()
    squares = jnp.zeros((S, 128), F32)
    for y in range(4):
        for z in range(4):
            for m in range(2):
                pieces = []
                for x in (2 * m, 2 * m + 1):
                    pieces.append(r_buf[z * 4 + x, :, y * 64:(y + 1) * 64].astype(F32)
                                  + r_buf[16 + y * 4 + x, :, z * 64:(z + 1) * 64].astype(F32))
                at = (y * 8 + z * 2 + m) * 128
                tile = res_buf[:, at:at + 128].astype(F32) + jnp.concatenate(pieces, axis=1)
                hid[:, at:at + 128] = tile
                squares = squares + tile * tile
    scaling = lax.rsqrt(jnp.sum(squares, axis=1, keepdims=True) * (1.0 / D) + 1e-06)

    half_at = pl.ds(pl.multiple_of(side * 2048, 128), 2048)
    na = Gather(links, side, b_way, x_way, n0, True, lambda i, j: j if i else None)
    nb = Gather(links, side, x_way, b_way, n1, True, lambda i, j: i if i else None)
    normed = (hid[:, half_at] * scaling * gain_buf[:, half_at]).astype(BF)
    n0[0, 0] = normed[:, 0:CUT]
    n1[0, 0] = normed[:, CUT:]
    nb.start()
    na.start()

    s_one, s_swap = [links.slot() for _ in range(4)], [links.slot(), links.slot()]

    def dispatch(b):
        for at, tokens in ((slice(0, CUT), n0[:, b]), (slice(CUT, 2048), n1[b])):
            rows = jnp.dot(pick[b], tokens.reshape(64, -1), preferred_element_type=F32).astype(BF).reshape(4, S, -1)
            x_st[b, :, :, at] = rows[1:]
            x_own[SLOT[b], 0, :, at] = rows[0]
        for a in (2, 1, 3):
            links.push(x_st.at[b, a - 1], x_own.at[SLOT[b], SLOT[a]], side, a_way[(None, 0, 2, 1)[a]], s_one[b])

    def swap(b):
        links.wait(x_own.at[SLOT[b], 1:4], s_one[b])
        links.push(x_own.at[SLOT[b]], x_far.at[SLOT[b]], other, g, s_swap[SLOT[b] // 2])

    def front(src, dst, h, low, high):
        rows = src[low:high].reshape((high - low) * 64, 2048)
        dst[low:high] = jnp.dot(rows, w_gu[h], preferred_element_type=F32).reshape(high - low, 4, S, 768)

    nb.step1()
    na.step1()
    nb.step2()
    na.step2()
    for b in (0, 1, 3, 2):
        if b:
            nb.wait_group(b, n1.at[b])
        na.wait_group(b, n0.at[1:4, b])
        dispatch(b)
    for copy in c_ffn:
        copy.wait()
    swap(0)
    swap(1)
    front(x_own, h_own, 0, 0, 2)
    links.wait(x_far.at[0:2], s_swap[0])
    front(x_far, h_far, 1, 0, 2)
    swap(3)
    swap(2)
    front(x_own, h_own, 0, 2, 4)
    links.wait(x_far.at[2:4], s_swap[1])
    front(x_far, h_far, 1, 2, 4)
    s_act = links.slot()
    for i in range(4):
        both = h_own[i] + h_far[:, i]
        gate, up = both[:, :, 0:384], both[:, :, 384:768]
        a_own[i] = (gate / (1.0 + jnp.exp(-gate)) * up).astype(BF)
        links.push(a_own.at[i], a_far.at[:, i], other, g, s_act)
    d_near[...] = jnp.dot(a_own[...].reshape(256, 384), wd[0], preferred_element_type=F32).reshape(4, 64, 2048)
    links.wait(a_far, s_act)
    s_back = [links.slot() for _ in range(4)]
    for b in (2, 1, 3, 0):
        rows = d_near[SLOT[b]] + jnp.dot(a_far[SLOT[b]].reshape(64, 384), wd[1], preferred_element_type=F32)
        rows = rows.astype(BF).reshape(4, S, 2048)
        z_buf[b, 0] = rows[0]
        for a in (2, 1, 3):
            y_st[b, a - 1] = rows[SLOT[a]]
            links.push(y_st.at[b, a - 1], z_buf.at[b, a], side, a_way[(None, 1, 2, 0)[a]], s_back[b])

    def mix(b):
        links.wait(z_buf.at[b, 1:4], s_back[b])
        both = lax.dot_general(weigh[b], z_buf[b].reshape(64, 2048), (((0,), (0,)), ((), ())),
                               preferred_element_type=F32)
        m_buf[b] = (both[0:64, :] + both[64:128, :]).reshape(4, S, 2048)

    r0 = Scatter(links, side, b_way, x_way, lambda i, j: m_buf[j, i, :, 0:CUTR], over0, near0)
    r1 = Scatter(links, side, x_way, b_way, lambda i, j: m_buf[i, j, :, CUTR:2048], over1, near1)
    for b in (2, 1, 3, 0):
        mix(b)
        for i in (2, 1, 3):
            r0.along_q(i, b)
        if b:
            for j in (2, 1, 3, 0):
                r1.along_q(b, j)
    for j in (2, 1, 3, 0):
        r0.turn(j)
        r1.turn(j)
    at = pl.multiple_of(side * 2048, 128)
    out_ref[:, 0:CUTR] = hid[:, pl.ds(at, CUTR)] + r0.result()
    out_ref[:, CUTR:2048] = hid[:, pl.ds(at + CUTR, 2048 - CUTR)] + r1.result()
    links.sent(info.at[1:16], POOL)
    links.sent(r_buf.at[0:31], POOL + 1)
    links.drain()


def body(q, k, v, lens, out_weight, residual, norm_gain, expert_ids, route_weights, gate_up, down_weight):
    vm = pl.BlockSpec(memory_space=pltpu.VMEM)
    hb = pl.BlockSpec(memory_space=pltpu.HBM)
    dma = pltpu.SemaphoreType.DMA

    def vb(*shape):
        return pltpu.VMEM(shape, BF)

    def vf(*shape):
        return pltpu.VMEM(shape, F32)

    return pl.pallas_call(
        kernel,
        out_shape=jax.ShapeDtypeStruct((S, D // 2), F32),
        in_specs=[hb] * 11,
        out_specs=vm,
        scratch_shapes=[
            vb(S, 4096), vb(2, S, CTX, HD), vb(2, S, CTX, HD), vb(4, 64, 4096),
            vb(4, 4, S, HEADS0 * HD), vb(4, 4, S, 4096 - HEADS0 * HD),
            vb(16, S, 256), vb(32, S, 256), vf(S, D), vf(16, 16, 128), vb(4, 4, S, CUT), vb(4, 4, S, 2048 - CUT),
            vb(4, 3, S, 2048), vb(4, 4, S, 2048), vb(4, 4, S, 2048),
            vb(2, 2048, 768), vb(2, 384, 2048), vf(4, 4, S, 768), vf(4, 4, S, 768), vb(4, 4, S, 384), vb(4, 4, S, 384),
            vf(4, 64, 2048), vb(4, 3, S, 2048), vb(4, 4, S, 2048), vf(4, 4, S, 2048),
            vb(2, 3, 4, S, CUTR), vb(2, 4, S, CUTR), vb(2, 3, 4, S, 2048 - CUTR), vb(2, 4, S, 2048 - CUTR),
            vb(S, D), vf(1, D), pltpu.VMEM((8, S), jnp.int32), vf(8, S), pltpu.SMEM((S,), jnp.int32),
            dma((17,)), dma((POOL + 2,)), dma((57,)),
        ],
        compiler_params=pltpu.CompilerParams(collective_id=0, has_side_effects=True, vmem_limit_bytes=46 << 20),
        name="decode_layer",
    )(*[pltpu.with_memory_space_constraint(value, pltpu.HBM) for value in (
        q, k, v, lens, out_weight.T, residual, norm_gain.reshape(1, -1), expert_ids.T, route_weights.T,
        gate_up[0], down_weight[0])]).astype(BF)


def solution(mesh):
    return jax.shard_map(
        body,
        mesh=mesh,
        in_specs=(
            P("grp", None), P("grp", None, None), P("grp", None, None), P("grp"), P(None, "grp"), P("grp", None), P(),
            P("grp", None), P("grp", None), P("grp", None, None), P("grp", None, None),
        ),
        out_specs=P("grp", "side"),
        check_vma=False,
    )
```

```python
import jax
import jax.numpy as jnp
from jax import lax
from jax.experimental import pallas as pl
from jax.experimental.pallas import tpu as pltpu
from jax.sharding import PartitionSpec as P

HQ = 64
KVH = 4
HD = 128
HID = 768
TOPK = 8
CTX = 128
D = 4096
S = 16
MESH = pl.DeviceIdType.MESH
BF = jnp.bfloat16
F32 = jnp.float32
NT = (((1,), (1,)), ((), ()))


def place():
    side = lax.axis_index("side")
    g = lax.axis_index("grp")
    sa = 16 - 12 * side
    sb = 4 + 12 * side
    ca = lax.rem(g // sa, 4)
    cb = lax.rem(g // sb, 4)
    cx = lax.rem(g, 4)
    return side, g, sa, sb, ca, cb, cx


def moved(g, c, stride, by):
    return g + (lax.rem(c + by + 4, 4) - c) * stride


def attend(q_buf, k_buf, lens_ref, kv):
    lane = lax.broadcasted_iota(jnp.int32, (S, CTX), 1)
    row = lax.broadcasted_iota(jnp.int32, (S, CTX), 0)
    live = jnp.zeros((S, CTX), jnp.int32)
    for s in range(S):
        live = jnp.where(row == s, lens_ref[s], live)
    group = HQ // KVH
    live = jnp.concatenate([live] * group, axis=0)
    lane = jnp.concatenate([lane] * group, axis=0)
    row = jnp.concatenate([row] * group, axis=0)
    queries = jnp.concatenate(
        [q_buf[:, (kv * group + j) * HD:(kv * group + j + 1) * HD] for j in range(group)], axis=0)
    scores = jnp.zeros((S * group, CTX), F32)
    for s in range(S):
        part = lax.dot_general(queries, k_buf[s], NT, preferred_element_type=F32)
        scores = jnp.where(row == s, part, scores)
    scores = jnp.where(lane < live, scores * HD ** (-0.5), -1e30)
    lifted = jnp.exp(scores - jnp.max(scores, axis=1, keepdims=True))
    weights = (lifted / jnp.sum(lifted, axis=1, keepdims=True))
    return jnp.concatenate([jnp.where(row == s, weights, 0.0).astype(BF) for s in range(S)], axis=1)


class Links:
    def __init__(self, side, near, sends, recvs):
        self.side, self.near, self.sends, self.recvs = side, near, sends, recvs
        self.slots, self.count, self.live = 0, 0, [None] * POOL

    def slot(self):
        assert self.slots < self.recvs.shape[0]
        self.slots += 1
        return self.slots - 1

    def make(self, src, dst, send, recv, to_side, to):
        return pltpu.make_async_remote_copy(
            src_ref=src, dst_ref=dst, send_sem=self.sends.at[send], recv_sem=self.recvs.at[recv],
            device_id=(to_side, to), device_id_type=MESH)

    def push(self, src, dst, to_side, to, recv=None, send=None):
        if recv is None:
            recv = self.slot()
        pooled = send is None
        if pooled:
            send = self.count % POOL
            self.count += 1
            if self.live[send] is not None:
                self.live[send].wait_send()
        copy = self.make(src, dst, send, recv, to_side, to)
        if pooled:
            self.live[send] = copy
        copy.start()
        return copy

    def wait(self, view, recv):
        self.make(view, view, 0, recv, self.side, self.near).wait_recv()

    def sent(self, view, send):
        self.make(view, view, send, 0, self.side, self.near).wait_send()

    def drain(self):
        for copy in self.live:
            if copy is not None:
                copy.wait_send()


class Columns:
    def __init__(self, links, side, plus, minus, own, slot, whole):
        self.links, self.side, self.plus, self.minus, self.own, self.slot = links, side, plus, minus, own, slot
        self.whole, self.rest = whole, links.slot()

    def start(self):
        push, own, slot = self.links.push, self.own, self.slot(0)
        self.up, self.down = [], []
        for k in range(2):
            up, down = slice(16 * k, 16 * k + 16), slice(32 + 16 * k, 48 + 16 * k)
            self.up.append(push(own.at[up], slot.at[up], self.side, self.plus))
            self.down.append(push(own.at[down], slot.at[down], self.side, self.minus))
        low, high = slice(0, 32), slice(32, 64)
        push(own.at[high], slot.at[high], self.side, self.plus, self.rest)
        push(own.at[low], slot.at[low], self.side, self.minus, self.rest)

    def forward(self, k):
        self.up[k].wait_recv()
        at = self.slot(1).at[16 * k:16 * k + 16]
        self.links.push(at, at, self.side, self.plus, self.rest)
        self.down[k].wait_recv()
        at = self.slot(3).at[32 + 16 * k:48 + 16 * k]
        self.links.push(at, at, self.side, self.minus, self.rest)

    def finish(self):
        self.links.wait(self.whole.at[0:2], self.rest)


class Gather:
    def __init__(self, links, side, p, q, buf, direct, group):
        self.links, self.side, self.p, self.q, self.buf, self.direct, self.group = links, side, p, q, buf, direct, group
        self.got, self.sems = {}, {}

    def send(self, i, j, to, di, dj):
        at = (i + di) % 4, (j + dj) % 4
        key = self.group(*at)
        recv = None
        if key is not None:
            if key not in self.sems:
                self.sems[key] = self.links.slot()
            recv = self.sems[key]
        self.got[at] = self.links.push(self.buf.at[i, j], self.buf.at[at], self.side, to, recv)

    def wait(self, i, j):
        self.got[i, j].wait_recv()

    def wait_group(self, key, view):
        self.links.wait(view, self.sems[key])

    def along_q(self, j):
        self.send(0, j, self.q[0], 1, 0)
        self.send(0, j, self.q[1], 3, 0)
        if self.direct:
            self.send(0, j, self.q[2], 2, 0)

    def start(self):
        self.send(0, 0, self.p[0], 0, 1)
        self.send(0, 0, self.p[1], 0, 3)
        self.send(0, 0, self.p[2], 0, 2)
        self.along_q(0)

    def step1(self):
        self.wait(0, 1)
        self.along_q(1)
        self.wait(0, 3)
        self.along_q(3)
        if not self.direct:
            self.wait(1, 0)
            self.send(1, 0, self.q[0], 1, 0)

    def step2(self):
        self.wait(0, 2)
        self.along_q(2)

    def step3(self):
        self.wait(1, 1)
        self.send(1, 1, self.q[0], 1, 0)
        self.wait(3, 3)
        self.send(3, 3, self.q[1], 3, 0)
        self.wait(3, 2)
        self.send(3, 2, self.q[1], 3, 0)


def relayed(i, j):
    return None if i == 0 or (i, j) in ((1, 0), (1, 1), (3, 3), (3, 2)) else 0


class Scatter:
    def __init__(self, links, side, p, q, block, over, near):
        self.links, self.side, self.p, self.q, self.block = links, side, p, q, block
        self.over, self.near = over, near
        self.s_over, self.s_near = [links.slot() for _ in range(4)], links.slot()

    def along_q(self, i, j):
        self.over[0, i - 1, j] = self.block(i, j).astype(BF)
        self.links.push(self.over.at[0, i - 1, j], self.over.at[1, i - 1, j], self.side, self.q[(None, 1, 2, 0)[i]],
                        self.s_over[j])

    def turn(self, j):
        self.links.wait(self.over.at[1, :, j], self.s_over[j])
        block = self.block(0, j)
        for i in (2, 1, 3):
            block = block + self.over[1, i - 1, j].astype(F32)
        if j == 0:
            self.own = block
        else:
            self.near[0, j] = block.astype(BF)
            self.links.push(self.near.at[0, j], self.near.at[1, j], self.side, self.p[(None, 1, 2, 0)[j]], self.s_near)

    def result(self):
        self.links.wait(self.near.at[1, 1:4], self.s_near)
        block = self.own
        for j in (1, 3, 2):
            block = block + self.near[1, j].astype(F32)
        return block


def routing(info, experts):
    lane = lax.broadcasted_iota(jnp.int32, (16, 128), 1)
    tiles = []
    for t in range(2):
        tile = jnp.zeros((16, 128), F32)
        for i in range(8):
            b, x = divmod(t * 8 + i, 4)
            block = info[x * 4 + b]
            moved_block = pltpu.roll(block, 16 * i, 1) if i else block
            tile = jnp.where(lane // 16 == i, moved_block, tile)
        tiles.append(tile)
    table = jnp.concatenate(tiles, axis=1)
    ids, route = table[0:8, :], table[8:16, :]
    first = lax.broadcasted_iota(jnp.int32, (256, 256), 0)
    later = lax.broadcasted_iota(jnp.int32, (256, 256), 1)
    before = jnp.where((first // 16 == later // 16) & (first < later), 1.0, 0.0).astype(BF)
    token = lax.broadcasted_iota(jnp.int32, (8, 256), 1) // 16
    named, weight = [], []
    for e in experts:
        hit = ids == e.astype(F32)
        named.append(jnp.sum(jnp.where(hit, 1.0, 0.0), axis=0, keepdims=True))
        weight.append(jnp.sum(jnp.where(hit, route, 0.0), axis=0, keepdims=True))
    named8 = jnp.concatenate(named + [jnp.zeros((4, 256), F32)], axis=0)
    rank = jnp.dot(named8.astype(BF), before, preferred_element_type=F32)
    spot = jnp.where(named8 > 0.5, (token % 4).astype(F32) * 4.0 + rank, -1.0)
    rows = lax.broadcasted_iota(jnp.int32, (16, 256), 0).astype(F32)
    picks, weighted = [], []
    for i in range(4):
        hit = rows == spot[i:i + 1, :]
        picks.append(jnp.where(hit, 1.0, 0.0))
        weighted.append(jnp.where(hit, weight[i], 0.0))
    picks, weighted = jnp.concatenate(picks, axis=0), jnp.concatenate(weighted, axis=0)
    pick, weigh = [], []
    for b in range(4):
        at = slice(64 * b, 64 * b + 64)
        pick.append(picks[:, at].astype(BF))
        high = weighted[:, at].astype(BF)
        weigh.append(jnp.concatenate([high, (weighted[:, at] - high.astype(F32)).astype(BF)], axis=1))
    return pick, weigh


SLOT = (0, 1, 3, 2)
HEADS0 = 22
POOL = 40
CUT = 1280
CUTR = 1280


def kernel(q_ref, k_ref, v_ref, lens_ref, wt_ref, res_ref, gain_ref, ids_ref, route_ref, up_ref, down_ref, out_ref,
           q_buf, k_buf, v_buf, w_buf, g0, g1, o_st, r_buf, hid, info, n0, n1, x_st, x_own, x_far,
           w_gu, wd, h_own, h_far, a_own, a_far, d_near, y_st, z_buf, m_buf, over0, near0, over1, near1,
           res_buf, gain_buf, ids_buf, route_buf, lens_buf, loc, sends, recvs):
    side, g, sa, sb, ca, cb, cx = place()
    other = 1 - side
    a_way = [moved(g, ca, sa, i) for i in (1, -1, 2)]
    ap, am = a_way[0], a_way[1]
    b_way = [moved(g, cb, sb, i) for i in (1, -1, 2)]
    x_way = [moved(g, cx, 1, i) for i in (1, -1, 2)]
    links = Links(side, ap, sends, recvs)
    barrier = pltpu.get_barrier_semaphore()

    def hello(to_side, to):
        pl.semaphore_signal(barrier, inc=1, device_id=(to_side, to), device_id_type=MESH)

    for to in a_way:
        hello(side, to)
    for i in range(4):
        for j in range(4):
            if i or j:
                hello(side, moved(moved(g, cb, sb, i), cx, 1, j))
            hello(other, moved(moved(g, ca, sa, i), cx, 1, j))

    def fetch(src, dst, i):
        copy = pltpu.make_async_copy(src, dst, loc.at[i])
        copy.start()
        return copy

    def at_side(base, size):
        return pl.ds(pl.multiple_of(base * size, 128), size)

    c_lens = fetch(lens_ref, lens_buf, 14)
    c_q = fetch(q_ref.at[:, at_side(side, 4096)], q_buf, 0)
    c_k = [fetch(k_ref.at[:, :, at_side(2 * side + i, 128)], k_buf.at[i], (1, 15)[i]) for i in range(2)]
    c_v = [fetch(v_ref.at[:, :, at_side(2 * side + i, 128)], v_buf.at[i], (2, 16)[i]) for i in range(2)]
    w_own = wt_ref.at[:, at_side(side, 4096)]
    c_w = fetch(w_own, w_buf.at[ca], 3)
    c_ids = fetch(ids_ref, ids_buf, 10)
    c_route = fetch(route_ref, route_buf, 11)
    info[0] = jnp.zeros((16, 128), F32)
    c_lens.wait()
    c_q.wait()
    spread = []
    for kv in range(2):
        c_k[kv].wait()
        spread.append(attend(q_buf, k_buf.at[kv], lens_buf, kv))
    group = HQ // KVH
    for kv in range(2):
        c_v[kv].wait()
        result = jnp.dot(spread[kv], v_buf[kv].reshape(S * CTX, HD), preferred_element_type=F32).astype(BF)
        for j in range(group):
            n = kv * group + j
            out, n = (g0, n) if n < HEADS0 else (g1, n - HEADS0)
            out[0, 0, :, n * HD:(n + 1) * HD] = result[j * S:(j + 1) * S, :]
    c_ids.wait()
    c_route.wait()
    info[0, 0:8, 0:16] = ids_buf[...].astype(F32)
    info[0, 8:16, 0:16] = route_buf[...]
    pl.semaphore_wait(barrier, 34)
    ring_w = Columns(links, side, ap, am, w_own, lambda source: w_buf.at[lax.rem(ca - source + 4, 4)], w_buf)
    split = HEADS0 * HD
    ra = Gather(links, side, b_way, x_way, g0, False, relayed)
    rb = Gather(links, side, x_way, b_way, g1, False, relayed)
    ring_w.start()
    ra.start()
    rb.start()
    c_res = fetch(res_ref, res_buf, 12)
    c_gain = fetch(gain_ref, gain_buf, 13)
    c_ffn = []
    for h in range(2):
        depth = at_side(side if h == 0 else other, 2048)
        c_ffn.append(fetch(up_ref.at[depth, at_side(side, 384)], w_gu.at[h, :, 0:384], 4 + h))
        c_ffn.append(fetch(up_ref.at[depth, at_side(side + 2, 384)], w_gu.at[h, :, 384:768], 6 + h))
        c_ffn.append(fetch(down_ref.at[at_side(side if h == 0 else other, 384), at_side(side, 2048)], wd.at[h], 8 + h))
    ra.step1()
    rb.step1()
    ra.step2()
    rb.step2()
    ring_w.forward(0)
    ring_w.forward(1)
    ra.step3()
    rb.step3()
    ra.wait_group(0, g0.at[2:4])
    rb.wait_group(0, g1.at[2:4])
    c_w.wait()
    ring_w.finish()
    p0 = lax.dot_general(g0[...].reshape(256, split), w_buf[:, :, 0:split].reshape(256, split), NT,
                         preferred_element_type=F32)
    p1 = lax.dot_general(g1[...].reshape(256, 4096 - split), w_buf[:, :, split:4096].reshape(256, 4096 - split), NT,
                         preferred_element_type=F32)
    mine = side * 16 + cb * 4 + cx
    columns_in = links.slot()
    for n in sorted(range(16), key=lambda n: -((0, 1, 2, 1)[n // 4] + (0, 1, 2, 1)[n % 4])):
        bi, xi = n // 4, n % 4
        u = (xi * 4 + bi) * S
        block = (p0[u:u + S, :] + p1[n * S:(n + 1) * S, :]).astype(BF)
        o_st[n] = block
        if n == 0:
            r_buf[mine] = block
        to = moved(moved(g, cb, sb, -bi), cx, 1, -xi)
        for e in range(2):
            if n == 0 and e == 0:
                continue
            links.push(o_st.at[n], r_buf.at[mine], side if e == 0 else other, to, columns_in, POOL + 1)

    told = links.slot()
    for i in range(4):
        for j in range(4):
            if i or j:
                links.push(info.at[0], info.at[j * 4 + i], side, moved(moved(g, cb, sb, i), cx, 1, j), told, POOL)
    links.wait(r_buf.at[0:31], columns_in)
    c_res.wait()
    c_gain.wait()
    squares = jnp.zeros((S, 128), F32)
    for y in range(4):
        for z in range(4):
            for m in range(2):
                pieces = []
                for x in (2 * m, 2 * m + 1):
                    pieces.append(r_buf[z * 4 + x, :, y * 64:(y + 1) * 64].astype(F32)
                                  + r_buf[16 + y * 4 + x, :, z * 64:(z + 1) * 64].astype(F32))
                at = (y * 8 + z * 2 + m) * 128
                tile = res_buf[:, at:at + 128].astype(F32) + jnp.concatenate(pieces, axis=1)
                hid[:, at:at + 128] = tile
                squares = squares + tile * tile
    scaling = lax.rsqrt(jnp.sum(squares, axis=1, keepdims=True) * (1.0 / D) + 1e-06)

    half_at = pl.ds(pl.multiple_of(side * 2048, 128), 2048)
    na = Gather(links, side, b_way, x_way, n0, True, lambda i, j: j if i else None)
    nb = Gather(links, side, x_way, b_way, n1, True, lambda i, j: i if i else None)
    normed = (hid[:, half_at] * scaling * gain_buf[:, half_at]).astype(BF)
    n0[0, 0] = normed[:, 0:CUT]
    n1[0, 0] = normed[:, CUT:]
    nb.start()
    na.start()

    s_one, s_swap = [links.slot() for _ in range(4)], [links.slot(), links.slot()]

    def dispatch(b):
        for at, tokens in ((slice(0, CUT), n0[:, b]), (slice(CUT, 2048), n1[b])):
            rows = jnp.dot(pick[b], tokens.reshape(64, -1), preferred_element_type=F32).astype(BF).reshape(4, S, -1)
            x_st[b, :, :, at] = rows[1:]
            x_own[SLOT[b], 0, :, at] = rows[0]
        for a in (2, 1, 3):
            links.push(x_st.at[b, a - 1], x_own.at[SLOT[b], SLOT[a]], side, a_way[(None, 0, 2, 1)[a]], s_one[b])

    def swap(b):
        links.wait(x_own.at[SLOT[b], 1:4], s_one[b])
        links.push(x_own.at[SLOT[b]], x_far.at[SLOT[b]], other, g, s_swap[SLOT[b] // 2])

    def front(src, dst, h, low, high):
        rows = src[low:high].reshape((high - low) * 64, 2048)
        dst[low:high] = jnp.dot(rows, w_gu[h], preferred_element_type=F32).reshape(high - low, 4, S, 768)

    nb.step1()
    na.step1()
    links.wait(info.at[1:16], told)
    experts = [moved(g, ca, sa, i) for i in range(4)]
    pick, weigh = routing(info, experts)
    nb.step2()
    na.step2()
    for b in (0, 1, 3, 2):
        if b:
            nb.wait_group(b, n1.at[b])
        na.wait_group(b, n0.at[1:4, b])
        dispatch(b)
    for copy in c_ffn:
        copy.wait()
    swap(0)
    swap(1)
    front(x_own, h_own, 0, 0, 2)
    links.wait(x_far.at[0:2], s_swap[0])
    front(x_far, h_far, 1, 0, 2)
    swap(3)
    swap(2)
    front(x_own, h_own, 0, 2, 4)
    links.wait(x_far.at[2:4], s_swap[1])
    front(x_far, h_far, 1, 2, 4)
    s_act = links.slot()
    for i in range(4):
        both = h_own[i] + h_far[:, i]
        gate, up = both[:, :, 0:384], both[:, :, 384:768]
        a_own[i] = (gate / (1.0 + jnp.exp(-gate)) * up).astype(BF)
        links.push(a_own.at[i], a_far.at[:, i], other, g, s_act)
    d_near[...] = jnp.dot(a_own[...].reshape(256, 384), wd[0], preferred_element_type=F32).reshape(4, 64, 2048)
    links.wait(a_far, s_act)
    s_back = [links.slot() for _ in range(4)]
    for b in (2, 1, 3, 0):
        rows = d_near[SLOT[b]] + jnp.dot(a_far[SLOT[b]].reshape(64, 384), wd[1], preferred_element_type=F32)
        rows = rows.astype(BF).reshape(4, S, 2048)
        z_buf[b, 0] = rows[0]
        for a in (2, 1, 3):
            y_st[b, a - 1] = rows[SLOT[a]]
            links.push(y_st.at[b, a - 1], z_buf.at[b, a], side, a_way[(None, 1, 2, 0)[a]], s_back[b])

    def mix(b):
        links.wait(z_buf.at[b, 1:4], s_back[b])
        both = lax.dot_general(weigh[b], z_buf[b].reshape(64, 2048), (((0,), (0,)), ((), ())),
                               preferred_element_type=F32)
        m_buf[b] = (both[0:64, :] + both[64:128, :]).reshape(4, S, 2048)

    r0 = Scatter(links, side, b_way, x_way, lambda i, j: m_buf[j, i, :, 0:CUTR], over0, near0)
    r1 = Scatter(links, side, x_way, b_way, lambda i, j: m_buf[i, j, :, CUTR:2048], over1, near1)
    for b in (2, 1, 3, 0):
        mix(b)
        for i in (2, 1, 3):
            r0.along_q(i, b)
        if b:
            for j in (2, 1, 3, 0):
                r1.along_q(b, j)
    for j in (2, 1, 3, 0):
        r0.turn(j)
        r1.turn(j)
    at = pl.multiple_of(side * 2048, 128)
    out_ref[:, 0:CUTR] = hid[:, pl.ds(at, CUTR)] + r0.result()
    out_ref[:, CUTR:2048] = hid[:, pl.ds(at + CUTR, 2048 - CUTR)] + r1.result()
    links.sent(info.at[1:16], POOL)
    links.sent(r_buf.at[0:31], POOL + 1)
    links.drain()


def body(q, k, v, lens, out_weight, residual, norm_gain, expert_ids, route_weights, gate_up, down_weight):
    vm = pl.BlockSpec(memory_space=pltpu.VMEM)
    hb = pl.BlockSpec(memory_space=pltpu.HBM)
    dma = pltpu.SemaphoreType.DMA

    def vb(*shape):
        return pltpu.VMEM(shape, BF)

    def vf(*shape):
        return pltpu.VMEM(shape, F32)

    return pl.pallas_call(
        kernel,
        out_shape=jax.ShapeDtypeStruct((S, D // 2), F32),
        in_specs=[hb] * 11,
        out_specs=vm,
        scratch_shapes=[
            vb(S, 4096), vb(2, S, CTX, HD), vb(2, S, CTX, HD), vb(4, 64, 4096),
            vb(4, 4, S, HEADS0 * HD), vb(4, 4, S, 4096 - HEADS0 * HD),
            vb(16, S, 256), vb(32, S, 256), vf(S, D), vf(16, 16, 128), vb(4, 4, S, CUT), vb(4, 4, S, 2048 - CUT),
            vb(4, 3, S, 2048), vb(4, 4, S, 2048), vb(4, 4, S, 2048),
            vb(2, 2048, 768), vb(2, 384, 2048), vf(4, 4, S, 768), vf(4, 4, S, 768), vb(4, 4, S, 384), vb(4, 4, S, 384),
            vf(4, 64, 2048), vb(4, 3, S, 2048), vb(4, 4, S, 2048), vf(4, 4, S, 2048),
            vb(2, 3, 4, S, CUTR), vb(2, 4, S, CUTR), vb(2, 3, 4, S, 2048 - CUTR), vb(2, 4, S, 2048 - CUTR),
            vb(S, D), vf(1, D), pltpu.VMEM((8, S), jnp.int32), vf(8, S), pltpu.SMEM((S,), jnp.int32),
            dma((17,)), dma((POOL + 2,)), dma((57,)),
        ],
        compiler_params=pltpu.CompilerParams(collective_id=0, has_side_effects=True, vmem_limit_bytes=46 << 20),
        name="decode_layer",
    )(*[pltpu.with_memory_space_constraint(value, pltpu.HBM) for value in (
        q, k, v, lens, out_weight.T, residual, norm_gain.reshape(1, -1), expert_ids.T, route_weights.T,
        gate_up[0], down_weight[0])]).astype(BF)


def solution(mesh):
    return jax.shard_map(
        body,
        mesh=mesh,
        in_specs=(
            P("grp", None), P("grp", None, None), P("grp", None, None), P("grp"), P(None, "grp"), P("grp", None), P(),
            P("grp", None), P("grp", None), P("grp", None, None), P("grp", None, None),
        ),
        out_specs=P("grp", "side"),
        check_vma=False,
    )
```
